32 devices in a mesh: seq: 8 (over z, y), tensor: 4 (over x, core).
Axes of the slice: x: 2, y: 2, z: 4, core: 2. Of those that a mesh axis runs over, the one named last changes fastest.
Arguments:
- tokens: bfloat16 [4096, 2048], P('seq'), may hold values from -6 to 6
- norm_gain: float32 [2048], replicated, may hold values from 0.1 to 1.9
- w_qk: bfloat16 [2048, 2048], P(None, 'tensor'), may hold values from -0.125 to 0.125
- w_value: bfloat16 [2048, 2048], P(None, 'tensor'), may hold values from -0.125 to 0.125
- w_out: bfloat16 [2048, 2048], P('tensor'), may hold values from -0.125 to 0.125
- w_up: bfloat16 [2048, 8192], P(None, 'tensor'), may hold values from -0.125 to 0.125
- w_down: bfloat16 [8192, 2048], P('tensor'), may hold values from -0.0625 to 0.0625
- centroids: float32 [16, 256, 128], P('tensor', 'seq'), may hold values from -6 to 6
- clusters: int32 [16, 4096], P('tensor', 'seq'), may hold values from 0 to 255, as said below
- slots: int32 [16, 4096], P('tensor', 'seq'), may hold values from 0 to 3, as said below
Outputs:
- layer_out: bfloat16 [4096, 2048], P(('seq', 'tensor'))
- new_centroids: float32 [16, 256, 128], P('tensor', 'seq')
The draws below stay inside these ranges and needn't reach their ends.
Inputs may be any that keep to these rules, and one draw needn't show every extreme that they name: `clusters`: within each head and each aligned block of 512 tokens (the tokens of one index of seq) no two tokens have the same cluster and the same slot, so a cluster holds at most 4 tokens of a block; in every such block some cluster holds exactly 4 tokens. `slots`: slots pair with clusters as stated for clusters.
All inputs are finite; a program needn't handle non-finite values.
Results may differ from the reference program's by a relative error of at most 0.01.
Values may be sent and summed in bfloat16 or wider, within the bound.
No kernel may reach another device: no remote copies, remote signals or barrier semaphores. Data moves between devices by JAX's collectives and lax.ppermute only.
A program may use at most 128 MiB of HBM per device.

```python
import jax
import jax.numpy as jnp
from jax import lax

D = 2048
HEADS = 16
HEAD_DIM = 128
FF = 8192
CLUSTERS = 256
TOK_DEV = 512
CAP = 4
SPAN = 32
SPLITS = 4
TOKENS = 4096


def routing_table(key):
    base = jax.random.fold_in(key, 41)
    streams = jax.random.split(base, 4)
    blocks = TOKENS // TOK_DEV
    slot_total = CLUSTERS * CAP
    cluster_of = jnp.arange(slot_total, dtype=jnp.int32) // CAP
    favour = jax.random.randint(streams[0], (HEADS, 1, CLUSTERS), 0, 4)
    favour_slot = jnp.take(favour, cluster_of, axis=2)
    noise = jax.random.randint(streams[1], (HEADS, blocks, slot_total), 0, 4096)
    forced = jax.random.randint(streams[2], (HEADS, blocks, 1), 0, CLUSTERS)
    score = noise + favour_slot * 1024 + jnp.where(cluster_of[None, None, :] == forced, 16384, 0)
    distinct = score * slot_total + jnp.arange(slot_total, dtype=jnp.int32)
    chosen = lax.top_k(distinct, TOK_DEV)[1].astype(jnp.int32)
    order_keys = jax.random.randint(streams[3], (HEADS, blocks, TOK_DEV), 0, 65536) * TOK_DEV + jnp.arange(TOK_DEV, dtype=jnp.int32)
    shuffle = jnp.argsort(order_keys, axis=-1)
    picked = jnp.take_along_axis(chosen, shuffle, axis=-1)
    cluster_ids = (picked // CAP).reshape(HEADS, TOKENS).astype(jnp.int32)
    slot_ids = (picked % CAP).reshape(HEADS, TOKENS).astype(jnp.int32)
    return (cluster_ids, slot_ids)


def draw_clusters(key, part):
    return routing_table(key)[0]


def draw_slots(key, part):
    return routing_table(key)[1]


def block_levels(stream_key, shape, cuts, least, high):
    def one(axis_at, shards_of):
        steps = jax.random.uniform(jax.random.fold_in(jax.random.fold_in(stream_key, 6), axis_at), (shards_of,), jnp.float32, least / len(cuts), high / len(cuts))
        return jnp.repeat(jnp.exp(steps), shape[axis_at] // shards_of).reshape((-1,) + (1,) * (len(shape) - axis_at - 1))

    gain = one(*cuts[0])
    for cut in cuts[1:]:
        gain = gain * one(*cut)
    return gain


def normal_values(key, extent, scale, bound, cuts=(), kind=jnp.bfloat16):
    result = scale * jax.random.normal(key, extent, jnp.float32)
    if cuts:
        result = result * block_levels(key, extent, cuts, -0.22, 0.18)
    return jnp.clip(result, -bound, bound).astype(kind)


def setup_inputs(seed: int = 0) -> dict:
    key_list = jax.random.split(jax.random.key(seed), 11)
    tokens = normal_values(key_list[0], (TOKENS, D), 1.0, 6.0, ((0, 8),))
    norm_gain = jnp.clip(1.0 + 0.18 * jax.random.normal(key_list[1], (D,), jnp.float32), 0.1, 1.9)
    w_qk = normal_values(key_list[2], (D, HEADS * HEAD_DIM), D ** -0.5, 0.125, ((1, 4),))
    w_value = normal_values(key_list[3], (D, HEADS * HEAD_DIM), D ** -0.5, 0.125, ((1, 4),))
    w_out = normal_values(key_list[4], (HEADS * HEAD_DIM, D), (HEADS * HEAD_DIM) ** -0.5, 0.125, ((0, 4),))
    w_up = normal_values(key_list[5], (D, FF), D ** -0.5, 0.125, ((1, 4),))
    w_down = normal_values(key_list[6], (FF, D), FF ** -0.5, 0.0625, ((0, 4),))
    centroids = normal_values(key_list[7], (HEADS, CLUSTERS, HEAD_DIM), 1.0, 6.0, ((0, 4), (1, 8)), jnp.float32)
    clusters = draw_clusters(jax.random.fold_in(key_list[10], 71), 0)
    slots = draw_slots(jax.random.fold_in(key_list[10], 71), 0)
    return dict(tokens=tokens, norm_gain=norm_gain, w_qk=w_qk, w_value=w_value, w_out=w_out, w_up=w_up, w_down=w_down, centroids=centroids, clusters=clusters, slots=slots)


SCORE_SCALE = 2.0
EMA_DECAY = 0.9
NORM_EPS = 1e-06

def rounded(term_value):
    return lax.optimization_barrier(term_value.astype(jnp.bfloat16)).astype(jnp.float32)

def reference(tokens, norm_gain, w_qk, w_value, w_out, w_up, w_down, centroids, clusters, slots):
    tokens_wide = tokens.astype(jnp.float32)
    normed = (tokens_wide * lax.rsqrt(lax.optimization_barrier(jnp.mean(tokens_wide * tokens_wide, axis=-1, keepdims=True)) + NORM_EPS) * norm_gain).astype(jnp.bfloat16)
    key_proj = jnp.dot(normed, w_qk, preferred_element_type=jnp.float32).reshape(TOKENS, HEADS, HEAD_DIM)
    key_unit = (key_proj * lax.rsqrt(lax.optimization_barrier(jnp.sum(key_proj * key_proj, axis=-1, keepdims=True)) + NORM_EPS)).astype(jnp.bfloat16)
    key_unit = lax.optimization_barrier(key_unit)
    val_proj = jnp.dot(normed, w_value, preferred_element_type=jnp.float32).astype(jnp.bfloat16)
    val_proj = lax.optimization_barrier(val_proj).reshape(TOKENS, HEADS, HEAD_DIM)
    positions = jnp.arange(TOKENS, dtype=jnp.int32)
    source = positions // TOK_DEV
    attended_heads = []
    centroid_rows = []
    for head_index in range(HEADS):
        cluster_row = clusters[head_index].astype(jnp.int32)
        global_slot = (cluster_row * SPAN + source * CAP + slots[head_index]).astype(jnp.int32)
        key_buf = jnp.zeros((CLUSTERS * SPAN, HEAD_DIM), jnp.float32).at[global_slot].set(key_unit[:, head_index].astype(jnp.float32)).reshape(CLUSTERS, SPAN, HEAD_DIM)
        val_buf = jnp.zeros((CLUSTERS * SPAN, HEAD_DIM), jnp.float32).at[global_slot].set(val_proj[:, head_index].astype(jnp.float32)).reshape(CLUSTERS, SPAN, HEAD_DIM)
        pos_buf = jnp.full((CLUSTERS * SPAN,), TOKENS, jnp.int32).at[global_slot].set(positions).reshape(CLUSTERS, SPAN)
        scores = jnp.einsum('ksd,ktd->kst', key_buf, key_buf, precision=lax.Precision.HIGHEST) * SCORE_SCALE
        causal = pos_buf[:, None, :] <= pos_buf[:, :, None]
        exponent = jnp.where(causal, jnp.exp(scores), 0.0)
        weights = (exponent / lax.optimization_barrier(jnp.sum(exponent, axis=-1, keepdims=True))).astype(jnp.bfloat16)
        weights = lax.optimization_barrier(weights).astype(jnp.float32)
        mixed_out = jnp.einsum('kst,ktd->ksd', weights, val_buf, precision=lax.Precision.HIGHEST).astype(jnp.bfloat16)
        attended_heads.append(mixed_out.reshape(CLUSTERS * SPAN, HEAD_DIM)[global_slot])
        key_sums = jax.ops.segment_sum(key_unit[:, head_index].astype(jnp.float32), cluster_row, num_segments=CLUSTERS)
        centroid_rows.append(EMA_DECAY * centroids[head_index] + (1.0 - EMA_DECAY) * key_sums)
    attended = jnp.stack(attended_heads, axis=1).reshape(TOKENS, HEADS * HEAD_DIM)
    new_centroids = jnp.stack(centroid_rows, axis=0)
    head_span = HEADS * HEAD_DIM // SPLITS
    unit_span = FF // SPLITS
    summed = jnp.zeros((TOKENS, D), jnp.float32)
    for group_index in range(SPLITS):
        attn_part = jnp.dot(attended[:, group_index * head_span:(group_index + 1) * head_span], w_out[group_index * head_span:(group_index + 1) * head_span], preferred_element_type=jnp.float32)
        hidden = jax.nn.relu(jnp.dot(normed, w_up[:, group_index * unit_span:(group_index + 1) * unit_span], preferred_element_type=jnp.float32)).astype(jnp.bfloat16)
        ffn_part = jnp.dot(hidden, w_down[group_index * unit_span:(group_index + 1) * unit_span], preferred_element_type=jnp.float32)
        summed = summed + rounded(attn_part + ffn_part)
    layer_out = (tokens_wide + summed).astype(jnp.bfloat16)
    return (layer_out, new_centroids)
```

```python
import functools

import jax
import jax.numpy as jnp
from jax import lax
from jax.experimental import pallas as pl
from jax.experimental.pallas import tpu as pltpu
from jax.sharding import PartitionSpec as P

CLUSTERS = 256
CAP = 4

SCORE_SCALE = 2.0
EMA_DECAY = 0.9
NORM_EPS = 1e-06
BOTH = ("seq", "tensor")
EXTRA = 16
VMEM_LIMIT = 62 * 1024 * 1024


def rounded(term_value):
    return lax.optimization_barrier(term_value.astype(jnp.bfloat16)).astype(jnp.float32)


def owner_pairs(step, seq_count, tensor_count):
    pairs = []
    for s in range(seq_count):
        for t in range(tensor_count):
            z, y, c = s // 2, s % 2, t % 2
            dest_s = 2 * (z ^ step) + c
            dest_t = (t - c) + (y ^ (z & 1))
            pairs.append((s * tensor_count + t, dest_s * tensor_count + dest_t))
    return pairs


def turned(pairs):
    return [(b, a) for a, b in pairs]


def any_spec():
    return pl.BlockSpec(memory_space=pl.ANY)


def vmem_spec():
    return pl.BlockSpec(memory_space=pltpu.VMEM)


def smem_spec():
    return pl.BlockSpec(memory_space=pltpu.SMEM)


def project_body(place, tokens, gain, w_qk, w_value, ids, *rest, heads, width):
    outs, normed = rest[:heads], rest[heads]
    qk_buf, val_buf, sems = rest[heads + 1 :]
    z = place[0]
    pairs = heads // 2
    span = 2 * width

    def copies(p):
        block = p ^ (z >> 1)
        cols = pl.ds(pl.multiple_of(block * span, span), span)
        return (
            pltpu.make_async_copy(w_qk.at[:, cols], qk_buf.at[p], sems.at[2 * p]),
            pltpu.make_async_copy(w_value.at[:, cols], val_buf.at[p], sems.at[2 * p + 1]),
        )

    for p in range(pairs):
        for copy in copies(p):
            copy.start()
    wide = tokens[...].astype(jnp.float32)
    mean = jnp.mean(wide * wide, axis=-1, keepdims=True)
    normed[...] = (wide * lax.rsqrt(mean + NORM_EPS) * gain[...]).astype(jnp.bfloat16)
    rows = tokens.shape[0]
    odd = (z & 1) == 1
    for p in range(pairs):
        key_copy, val_copy = copies(p)
        key_copy.wait()
        key_proj = jnp.dot(normed[...], qk_buf[p], preferred_element_type=jnp.float32)
        units = []
        for q in range(2):
            k = key_proj[:, q * width : (q + 1) * width]
            total = jnp.sum(k * k, axis=-1, keepdims=True)
            units.append((k * lax.rsqrt(total + NORM_EPS)).astype(jnp.bfloat16))
        val_copy.wait()
        val_proj = jnp.dot(normed[...], val_buf[p], preferred_element_type=jnp.float32)
        values = [
            val_proj[:, q * width : (q + 1) * width].astype(jnp.bfloat16) for q in range(2)
        ]
        for q in range(2):
            out = outs[2 * p + q]
            out[:rows, :width] = jnp.where(odd, units[1 - q], units[q])
            out[:rows, width:] = jnp.where(odd, values[1 - q], values[q])
            out[rows:, :] = ids[(2 * p + q) ^ z]


def project(place, tokens, gain, w_qk, w_value, ids, heads, width):
    rows, depth = tokens.shape
    message = jax.ShapeDtypeStruct((rows + EXTRA, 2 * width), jnp.bfloat16)
    pairs = heads // 2
    return pl.pallas_call(
        functools.partial(project_body, heads=heads, width=width),
        out_shape=(message,) * heads + (jax.ShapeDtypeStruct((rows, depth), jnp.bfloat16),),
        in_specs=[smem_spec(), vmem_spec(), vmem_spec(), any_spec(), any_spec(), vmem_spec()],
        out_specs=(vmem_spec(),) * (heads + 1),
        scratch_shapes=[
            pltpu.VMEM((pairs, depth, 2 * width), jnp.bfloat16),
            pltpu.VMEM((pairs, depth, 2 * width), jnp.bfloat16),
            pltpu.SemaphoreType.DMA((2 * pairs,)),
        ],
        compiler_params=pltpu.CompilerParams(vmem_limit_bytes=VMEM_LIMIT),
        cost_estimate=pl.CostEstimate(
            flops=4 * rows * depth * heads * width,
            bytes_accessed=4 * (depth * heads * width + rows * depth + rows * heads * width),
            transcendentals=0,
        ),
        name="project",
    )(place, tokens, gain.reshape(1, depth), w_qk, w_value, ids)


def codes(id_row, width):
    grid = jnp.transpose(jnp.broadcast_to(id_row, (width, width)))
    high = jnp.floor(grid * (1.0 / 16.0))
    low = grid - 16.0 * high
    lane = lax.broadcasted_iota(jnp.int32, (width, width), 1).astype(jnp.float32)
    hit = jnp.logical_or(lane == high, lane == low + 16.0)
    return jnp.where(hit, 1.0, 0.0), lane == 32.0


def attend_body(block_ids, *refs, heads, width, owned):
    own, other = refs[:heads], refs[heads : 2 * heads]
    outs = refs[2 * heads : 3 * heads]
    keys, vals, queries, acc = refs[3 * heads :]
    rows = keys.shape[1]
    sources = list(own) + list(other)
    sums = jnp.zeros((heads * owned, width), jnp.float32)
    cluster_col = lax.broadcasted_iota(jnp.int32, (owned, rows), 0)
    ranges = [cluster_col + owned * block_ids[q] for q in range(heads)]
    wanted = jnp.concatenate(ranges, axis=0).astype(jnp.float32)
    for b, source in enumerate(sources):
        key = source[:rows, :width]
        keys[b, :, :width] = key
        vals[b, :, :width] = source[:rows, width:]
        vals[b, :, width:] = jnp.ones((rows, width), jnp.bfloat16)
        if b < heads:
            queries[b, :, :width] = key * jnp.bfloat16(SCORE_SCALE)
        id_tile = source[rows:, :].astype(jnp.float32)
        id_rows = []
        for part in range(rows // width):
            r, l = (part * width) // (2 * width), (part * width) % (2 * width)
            id_row = id_tile[r : r + 1, l : l + width]
            id_rows.append(id_row)
            code, one = codes(id_row, width)
            here = pl.ds(part * width, width)
            keys[b, here, width:] = jnp.where(one, 1.0, code).astype(jnp.bfloat16)
            if b < heads:
                queries[b, here, width:] = jnp.where(one, -256.0, 128.0 * code).astype(
                    jnp.bfloat16
                )
        ids = jnp.concatenate(id_rows, axis=1)
        one_hot = jnp.where(wanted == ids, 1.0, 0.0).astype(jnp.bfloat16)
        sums = sums + jnp.dot(one_hot, key, preferred_element_type=jnp.float32)

    tile = 2 * width

    def pair(q, b, masked):
        for r in range(rows // tile):
            here = pl.ds(r * tile, tile)
            cols = (r + 1) * tile if masked else rows
            score = lax.dot_general(
                queries[q, here, :],
                keys[b, :cols, :],
                (((1,), (1,)), ((), ())),
                preferred_element_type=jnp.float32,
            )
            weight = jnp.exp(score)
            if masked:
                row_at = lax.broadcasted_iota(jnp.int32, weight.shape, 0) + r * tile
                col_at = lax.broadcasted_iota(jnp.int32, weight.shape, 1)
                weight = jnp.where(col_at <= row_at, weight, 0.0)
            mixed = jnp.dot(
                weight.astype(jnp.bfloat16),
                vals[b, :cols, :],
                preferred_element_type=jnp.float32,
            )
            if masked:
                acc[q, here, :] = mixed
            else:
                acc[q, here, :] += mixed

    def per_query(q, carry):
        pair(q, q, True)

        def per_key(b, inner):
            @pl.when(block_ids[b] < block_ids[q])
            def _():
                pair(q, b, False)

            return inner

        return lax.fori_loop(0, 2 * heads, per_key, carry)

    lax.fori_loop(0, heads, per_query, 0)
    for q in range(heads):
        out = outs[q]
        out[:rows, :] = (acc[q, :, :width] / acc[q, :, width:]).astype(jnp.bfloat16)
        out[rows:, :] = sums[q * owned : (q + 1) * owned].astype(jnp.bfloat16)


def attend(block_ids, own, other, width, owned):
    heads = len(own)
    rows = own[0].shape[0] - EXTRA
    result = jax.ShapeDtypeStruct((rows + owned, width), jnp.bfloat16)
    units = heads * heads + heads // 2
    return pl.pallas_call(
        functools.partial(attend_body, heads=heads, width=width, owned=owned),
        out_shape=(result,) * heads,
        in_specs=[smem_spec()] + [vmem_spec()] * (2 * heads),
        out_specs=(vmem_spec(),) * heads,
        scratch_shapes=[
            pltpu.VMEM((2 * heads, rows, 2 * width), jnp.bfloat16),
            pltpu.VMEM((2 * heads, rows, 2 * width), jnp.bfloat16),
            pltpu.VMEM((heads, rows, 2 * width), jnp.bfloat16),
            pltpu.VMEM((heads, rows, 2 * width), jnp.float32),
        ],
        compiler_params=pltpu.CompilerParams(vmem_limit_bytes=VMEM_LIMIT),
        cost_estimate=pl.CostEstimate(
            flops=units * rows * rows * width * 8,
            bytes_accessed=2 * heads * rows * width * 10,
            transcendentals=units * rows * rows,
        ),
        name="attend",
    )(block_ids, *own, *other)


def mix_body(place, *refs, heads, width, share, with_centroids):
    own, swapped = refs[:heads], refs[heads : 2 * heads]
    w_own, w_other, ffn_own, ffn_other = refs[2 * heads : 2 * heads + 4]
    rest = refs[2 * heads + 4 :]
    z, own_row, half_row = place[0], place[1], place[2]
    here = pl.ds(pl.multiple_of(own_row, share), share)
    half = pl.ds(pl.multiple_of(half_row, share), share)
    left = jnp.concatenate([own[k][here, :] for k in range(heads)], axis=1)
    right = jnp.concatenate([swapped[k][half, :] for k in range(heads)], axis=1)

    def gathered(w):
        return jnp.concatenate(
            [w[pl.ds(pl.multiple_of((z ^ k) * width, width), width), :] for k in range(heads)],
            axis=0,
        )

    total = ffn_own[...].astype(jnp.float32) + ffn_other[...].astype(jnp.float32)
    total = total + jnp.dot(left, gathered(w_own), preferred_element_type=jnp.float32)
    total = total + jnp.dot(right, gathered(w_other), preferred_element_type=jnp.float32)
    if not with_centroids:
        (part,) = rest
        part[...] = total.astype(part.dtype)
        return
    centroids, part, updated = rest
    part[...] = total.astype(part.dtype)
    owned = centroids.shape[1]
    for k in range(heads):
        sums = own[k][own[k].shape[0] - owned :, :].astype(jnp.float32)
        head = z ^ k
        updated[head] = EMA_DECAY * centroids[head] + (1.0 - EMA_DECAY) * sums


def mix(place, own, swapped, w_own, w_other, ffn_own, ffn_other, kind, centroids=None):
    heads, width = len(own), own[0].shape[1]
    share, depth = ffn_own.shape
    out_shape = [jax.ShapeDtypeStruct((share, depth), kind)]
    extra = []
    if centroids is not None:
        out_shape.append(jax.ShapeDtypeStruct(centroids.shape, jnp.float32))
        extra.append(centroids)
    return pl.pallas_call(
        functools.partial(
            mix_body,
            heads=heads,
            width=width,
            share=share,
            with_centroids=centroids is not None,
        ),
        out_shape=tuple(out_shape),
        in_specs=[smem_spec()] + [vmem_spec()] * (2 * heads + 4 + len(extra)),
        out_specs=(vmem_spec(),) * len(out_shape),
        compiler_params=pltpu.CompilerParams(vmem_limit_bytes=VMEM_LIMIT),
        cost_estimate=pl.CostEstimate(
            flops=4 * share * heads * width * depth,
            bytes_accessed=4 * heads * width * depth + 8 * share * depth,
            transcendentals=0,
        ),
        name="mix",
    )(place, *own, *swapped, w_own, w_other, ffn_own, ffn_other, *extra)


def by_heads(
    tokens, norm_gain, w_qk, w_value, w_out, w_up, w_down, centroids, clusters, slots
):
    tok_rows, depth = tokens.shape
    seq_count = lax.axis_size("seq")
    tensor_count = lax.axis_size("tensor")
    heads = clusters.shape[0]
    owned = centroids.shape[1]
    width = w_qk.shape[1] // heads
    share = tok_rows // tensor_count
    seq_at = lax.axis_index("seq")
    tensor_at = lax.axis_index("tensor")
    z, core = seq_at // 2, tensor_at % 2
    place = jnp.stack([z]).astype(jnp.int32)
    swap_core = [(t, t ^ 1) for t in range(tensor_count)]
    swap_x = [(t, t ^ 2) for t in range(tensor_count)]

    ids = clusters.astype(jnp.float32).astype(jnp.bfloat16)
    ids = ids.reshape(heads, tok_rows // (2 * width), 2 * width)
    ids = jnp.pad(ids, ((0, 0), (0, EXTRA - ids.shape[1]), (0, 0)))
    w_other = lax.ppermute(w_out, "tensor", swap_core)

    *messages, normed = project(place, tokens, norm_gain, w_qk, w_value, ids, heads, width)
    steps = [owner_pairs(k, seq_count, tensor_count) for k in range(heads)]
    own = [lax.ppermute(messages[k], BOTH, steps[k]) for k in range(heads)]
    other = [lax.ppermute(own[k], "tensor", swap_core) for k in range(heads)]

    hidden = jax.nn.relu(jnp.dot(normed, w_up, preferred_element_type=jnp.float32)).astype(
        jnp.bfloat16
    )
    ffn_part = jnp.dot(hidden, w_down, preferred_element_type=jnp.float32)
    quarters = ffn_part.reshape(2, 2, share, depth)
    ffn_mine = lax.dynamic_index_in_dim(quarters, core, 1, keepdims=False)
    ffn_away = lax.dynamic_index_in_dim(quarters, 1 - core, 1, keepdims=False)
    ffn_got = lax.ppermute(ffn_away.astype(jnp.bfloat16), "tensor", swap_core)

    step_at = jnp.arange(heads, dtype=jnp.int32)
    from_pair = z ^ step_at
    own_ids = 2 * from_pair + (core ^ (from_pair & 1))
    block_ids = jnp.concatenate([own_ids, own_ids ^ 1]).astype(jnp.int32)
    results = attend(block_ids, own, other, width, owned)
    back = [lax.ppermute(results[k], BOTH, turned(steps[k])) for k in range(heads)]

    away = [
        lax.dynamic_index_in_dim(
            b[:tok_rows].reshape(2, 2, share, width), 1 - core, 1, keepdims=False
        )
        for b in back
    ]
    swapped = lax.ppermute(jnp.stack(away), "tensor", swap_core)
    swapped = [swapped[k].reshape(2 * share, width) for k in range(heads)]

    x_at = tensor_at // 2

    def part(x, kind, cent=None):
        at = jnp.stack([z, (2 * x + core) * share, x * share]).astype(jnp.int32)
        mine = lax.dynamic_index_in_dim(ffn_mine, x, 0, keepdims=False)
        got = lax.dynamic_index_in_dim(ffn_got, x, 0, keepdims=False)
        return mix(at, back, swapped, w_out, w_other, mine, got, kind, cent)

    (sent,) = part(1 - x_at, jnp.bfloat16)
    came = lax.ppermute(sent, "tensor", swap_x)
    kept, new_centroids = part(x_at, jnp.float32, centroids)
    own_rows = lax.dynamic_slice_in_dim(tokens, tensor_at * share, share, 0)
    mixed_rows = (own_rows.astype(jnp.float32) + (kept + came.astype(jnp.float32))).astype(
        jnp.bfloat16
    )
    return (mixed_rows, new_centroids)


def by_clusters(tokens, norm_gain, w_qk, w_value, w_out, w_up, w_down, centroids, clusters, slots):
    tok_rows = tokens.shape[0]
    seq_count = lax.axis_size("seq")
    tensor_count = lax.axis_size("tensor")
    heads_here = clusters.shape[0]
    owned_count = centroids.shape[1]
    head_width = w_qk.shape[1] // heads_here
    share_rows = tok_rows // tensor_count
    row_first = lax.axis_index("tensor") * share_rows
    tokens_wide = tokens.astype(jnp.float32)
    normed = (
        tokens_wide
        * lax.rsqrt(jnp.mean(tokens_wide * tokens_wide, axis=-1, keepdims=True) + NORM_EPS)
        * norm_gain
    ).astype(jnp.bfloat16)
    key_proj = jnp.dot(normed, w_qk, preferred_element_type=jnp.float32).reshape(
        tok_rows, heads_here, head_width
    )
    key_unit = (
        key_proj * lax.rsqrt(jnp.sum(key_proj * key_proj, axis=-1, keepdims=True) + NORM_EPS)
    ).astype(jnp.bfloat16)
    val_proj = (
        jnp.dot(normed, w_value, preferred_element_type=jnp.float32)
        .astype(jnp.bfloat16)
        .reshape(tok_rows, heads_here, head_width)
    )
    positions = lax.axis_index("seq") * tok_rows + jnp.arange(tok_rows, dtype=jnp.int32)
    pos_high = (positions // 256).astype(jnp.float32).astype(jnp.bfloat16)
    pos_low = (positions % 256).astype(jnp.float32).astype(jnp.bfloat16)
    flat_slot = clusters.T * CAP + slots.T
    head_grid = jnp.broadcast_to(jnp.arange(heads_here, dtype=jnp.int32)[None, :], flat_slot.shape)
    slot_total = CLUSTERS * CAP
    layout = (heads_here, seq_count, owned_count, CAP)
    key_buf = (
        jnp.zeros((heads_here, slot_total, head_width), jnp.bfloat16)
        .at[head_grid, flat_slot]
        .set(key_unit)
        .reshape(layout + (head_width,))
    )
    val_buf = (
        jnp.zeros((heads_here, slot_total, head_width), jnp.bfloat16)
        .at[head_grid, flat_slot]
        .set(val_proj)
        .reshape(layout + (head_width,))
    )
    high_buf = (
        jnp.full((heads_here, slot_total), 256.0, jnp.bfloat16)
        .at[head_grid, flat_slot]
        .set(jnp.broadcast_to(pos_high[:, None], flat_slot.shape))
        .reshape(layout)
    )
    low_buf = (
        jnp.zeros((heads_here, slot_total), jnp.bfloat16)
        .at[head_grid, flat_slot]
        .set(jnp.broadcast_to(pos_low[:, None], flat_slot.shape))
        .reshape(layout)
    )
    key_in = lax.all_to_all(key_buf, "seq", split_axis=1, concat_axis=1, tiled=True)
    val_in = lax.all_to_all(val_buf, "seq", split_axis=1, concat_axis=1, tiled=True)
    high_in = lax.all_to_all(high_buf, "seq", split_axis=1, concat_axis=1, tiled=True)
    low_in = lax.all_to_all(low_buf, "seq", split_axis=1, concat_axis=1, tiled=True)
    scores = (
        jnp.einsum("hskad,htkbd->hksatb", key_in, key_in, preferred_element_type=jnp.float32)
        * SCORE_SCALE
    )
    key_place = high_in.astype(jnp.float32) * 256.0 + low_in.astype(jnp.float32)
    ordered = jnp.transpose(key_place, (0, 2, 1, 3))
    causal = ordered[:, :, None, None, :, :] <= ordered[:, :, :, :, None, None]
    exponent = jnp.where(causal, jnp.exp(scores), 0.0)
    weights = (exponent / jnp.sum(exponent, axis=(4, 5), keepdims=True)).astype(jnp.bfloat16)
    mixed_out = jnp.einsum(
        "hksatb,htkbd->hskad", weights, val_in, preferred_element_type=jnp.float32
    ).astype(jnp.bfloat16)
    returned_back = lax.all_to_all(mixed_out, "seq", split_axis=1, concat_axis=1, tiled=True)
    one_hot = (clusters[:, :, None] == jnp.arange(CLUSTERS, dtype=jnp.int32)[None, None, :]).astype(
        jnp.bfloat16
    )
    local_sums = jnp.einsum("htk,thd->hkd", one_hot, key_unit, preferred_element_type=jnp.float32)
    totals = lax.psum_scatter(
        local_sums.astype(jnp.bfloat16), "seq", scatter_dimension=1, tiled=True
    ).astype(jnp.float32)
    new_centroids = EMA_DECAY * centroids + (1.0 - EMA_DECAY) * totals
    returned = returned_back.reshape(heads_here, slot_total, head_width)
    attended = returned[head_grid, flat_slot].reshape(tok_rows, heads_here * head_width)
    attn_part = jnp.dot(attended, w_out, preferred_element_type=jnp.float32)
    hidden = jax.nn.relu(jnp.dot(normed, w_up, preferred_element_type=jnp.float32)).astype(
        jnp.bfloat16
    )
    ffn_part = jnp.dot(hidden, w_down, preferred_element_type=jnp.float32)
    summed = lax.psum_scatter(
        rounded(attn_part + ffn_part).astype(jnp.bfloat16),
        "tensor",
        scatter_dimension=0,
        tiled=True,
    ).astype(jnp.float32)
    own_rows = lax.dynamic_slice_in_dim(tokens_wide, row_first, share_rows, 0)
    mixed_rows = (own_rows + summed).astype(jnp.bfloat16)
    return (mixed_rows, new_centroids)


def solution(mesh):
    in_specs = (
        P("seq", None),
        P(),
        P(None, "tensor"),
        P(None, "tensor"),
        P("tensor", None),
        P(None, "tensor"),
        P("tensor", None),
        P("tensor", "seq", None),
        P("tensor", "seq"),
        P("tensor", "seq"),
    )
    out_specs = (P(("seq", "tensor"), None), P("tensor", "seq", None))
    sizes = dict(mesh.shape)

    def local(*args):
        heads = args[8].shape[0]
        fits = (
            sizes["tensor"] == 4
            and sizes["seq"] == 2 * heads
            and heads & (heads - 1) == 0
            and heads > 1
        )
        return (by_heads if fits else by_clusters)(*args)

    return jax.shard_map(local, mesh=mesh, in_specs=in_specs, out_specs=out_specs, check_vma=False)
```

```python
import functools

import jax
import jax.numpy as jnp
from jax import lax
from jax.experimental import pallas as pl
from jax.experimental.pallas import tpu as pltpu
from jax.sharding import PartitionSpec as P


CLUSTERS = 256
CAP = 4

SCORE_SCALE = 2.0
EMA_DECAY = 0.9
NORM_EPS = 1e-06
BOTH = ("seq", "tensor")
EXTRA = 16
VMEM_LIMIT = 60 * 1024 * 1024


def rounded(term_value):
    return lax.optimization_barrier(term_value.astype(jnp.bfloat16)).astype(jnp.float32)


def owner_pairs(step, seq_count, tensor_count):
    pairs = []
    for s in range(seq_count):
        for t in range(tensor_count):
            z, y, c = s // 2, s % 2, t % 2
            dest_s = 2 * (z ^ step) + c
            dest_t = (t - c) + (y ^ (z & 1))
            pairs.append((s * tensor_count + t, dest_s * tensor_count + dest_t))
    return pairs


def turned(pairs):
    return [(b, a) for a, b in pairs]


def any_spec():
    return pl.BlockSpec(memory_space=pl.ANY)


def vmem_spec():
    return pl.BlockSpec(memory_space=pltpu.VMEM)


def params():
    return pltpu.CompilerParams(vmem_limit_bytes=VMEM_LIMIT)


def cost(flops, moved, transcendentals=0):
    return pl.CostEstimate(
        flops=flops, bytes_accessed=moved, transcendentals=transcendentals
    )


def shape(dims, kind=jnp.bfloat16):
    return jax.ShapeDtypeStruct(dims, kind)


def project_body(tokens, gain, w_qk, w_value, clusters, *rest, heads, width):
    outs, normed = rest[:heads], rest[heads]
    qk_buf, val_buf, sems = rest[heads + 1 :]
    z = lax.axis_index("seq") >> 1
    pairs = heads // 2
    span = 2 * width

    def copies(p):
        block = p ^ (z >> 1)
        cols = pl.ds(pl.multiple_of(block * span, span), span)
        return (
            pltpu.make_async_copy(w_qk.at[:, cols], qk_buf.at[p], sems.at[2 * p]),
            pltpu.make_async_copy(w_value.at[:, cols], val_buf.at[p], sems.at[2 * p + 1]),
        )

    for p in range(pairs):
        for copy in copies(p):
            copy.start()
    wide = tokens[...].astype(jnp.float32)
    mean = jnp.mean(wide * wide, axis=-1, keepdims=True)
    normed[...] = (wide * lax.rsqrt(mean + NORM_EPS) * gain[...]).astype(jnp.bfloat16)
    rows = tokens.shape[0]
    odd = (z & 1) == 1
    row_at = lax.broadcasted_iota(jnp.int32, (EXTRA, span), 0)
    for p in range(pairs):
        key_copy, val_copy = copies(p)
        key_copy.wait()
        key_proj = jnp.dot(normed[...], qk_buf[p], preferred_element_type=jnp.float32)
        units = []
        for q in range(2):
            k = key_proj[:, q * width : (q + 1) * width]
            total = jnp.sum(k * k, axis=-1, keepdims=True)
            units.append((k * lax.rsqrt(total + NORM_EPS)).astype(jnp.bfloat16))
        val_copy.wait()
        val_proj = jnp.dot(normed[...], val_buf[p], preferred_element_type=jnp.float32)
        values = [
            val_proj[:, q * width : (q + 1) * width].astype(jnp.bfloat16) for q in range(2)
        ]
        for q in range(2):
            out = outs[2 * p + q]
            out[:rows, :width] = jnp.where(odd, units[1 - q], units[q])
            out[:rows, width:] = jnp.where(odd, values[1 - q], values[q])
            id_row = clusters[pl.ds((2 * p + q) ^ z, 1), :].astype(jnp.float32)
            tail = jnp.zeros((EXTRA, span), jnp.float32)
            for part in range(rows // span):
                piece = id_row[:, part * span : (part + 1) * span]
                tail = jnp.where(row_at == part, piece, tail)
            out[rows:, :] = tail.astype(jnp.bfloat16)


def project(tokens, gain, w_qk, w_value, clusters, heads, width):
    rows, depth = tokens.shape
    pairs = heads // 2
    return pl.pallas_call(
        functools.partial(project_body, heads=heads, width=width),
        out_shape=(shape((rows + EXTRA, 2 * width)),) * heads + (shape((rows, depth)),),
        in_specs=[vmem_spec(), vmem_spec(), any_spec(), any_spec(), vmem_spec()],
        out_specs=(vmem_spec(),) * (heads + 1),
        scratch_shapes=[
            pltpu.VMEM((pairs, depth, 2 * width), jnp.bfloat16),
            pltpu.VMEM((pairs, depth, 2 * width), jnp.bfloat16),
            pltpu.SemaphoreType.DMA((2 * pairs,)),
        ],
        compiler_params=params(),
        cost_estimate=cost(
            4 * rows * depth * heads * width,
            4 * (depth * heads * width + rows * depth + rows * heads * width),
        ),
        name="project",
    )(tokens, gain.reshape(1, depth), w_qk, w_value, clusters)


def up_body(normed, w_up, hidden):
    grown = jnp.dot(normed[...], w_up[...], preferred_element_type=jnp.float32)
    hidden[...] = jnp.maximum(grown, 0.0).astype(jnp.bfloat16)


def up(normed, w_up, blocks=2):
    rows, depth = normed.shape
    units = w_up.shape[1]
    block = units // blocks
    return pl.pallas_call(
        up_body,
        grid=(blocks,),
        out_shape=shape((rows, units)),
        in_specs=[
            pl.BlockSpec((rows, depth), lambda i: (0, 0)),
            pl.BlockSpec((depth, block), lambda i: (0, i)),
        ],
        out_specs=pl.BlockSpec((rows, block), lambda i: (0, i)),
        compiler_params=params(),
        cost_estimate=cost(2 * rows * depth * units, 2 * depth * units + 4 * rows * depth),
        name="grow",
    )(normed, w_up)


def down_body(hidden, w_down, mine, away, *, share):
    core = lax.axis_index("tensor") % 2
    part = jnp.dot(hidden[...], w_down[...], preferred_element_type=jnp.float32)
    even = core == 0
    for x in range(2):
        low = part[(2 * x) * share : (2 * x + 1) * share]
        high = part[(2 * x + 1) * share : (2 * x + 2) * share]
        mine[x] = jnp.where(even, low, high)
        away[x] = jnp.where(even, high, low).astype(jnp.bfloat16)


def down(hidden, w_down, share, blocks=2):
    rows, units = hidden.shape
    depth = w_down.shape[1]
    block = depth // blocks
    out = pl.BlockSpec((2, share, block), lambda i: (0, 0, i))
    return pl.pallas_call(
        functools.partial(down_body, share=share),
        grid=(blocks,),
        out_shape=(shape((2, share, depth), jnp.float32), shape((2, share, depth))),
        in_specs=[
            pl.BlockSpec((rows, units), lambda i: (0, 0)),
            pl.BlockSpec((units, block), lambda i: (0, i)),
        ],
        out_specs=(out, out),
        compiler_params=params(),
        cost_estimate=cost(2 * rows * depth * units, 2 * depth * units + 6 * rows * depth),
        name="shrink",
    )(hidden, w_down)


def pick_body(mine, got, sent):
    away = 1 - lax.axis_index("tensor") // 2
    sent[...] = (mine[away] + got[away].astype(jnp.float32)).astype(jnp.bfloat16)


def pick(mine, got):
    return pl.pallas_call(
        pick_body,
        out_shape=shape(mine.shape[1:]),
        in_specs=[vmem_spec(), vmem_spec()],
        out_specs=vmem_spec(),
        compiler_params=params(),
        cost_estimate=cost(mine.size, mine.size * 4),
        name="pick",
    )(mine, got)


def block_of(b, heads):
    z = lax.axis_index("seq") >> 1
    core = lax.axis_index("tensor") % 2
    pair = z ^ (b % heads)
    return 2 * pair + (core ^ (pair & 1) ^ (b // heads))


def attend_body(*refs, heads, width, owned, steps, first):
    if first:
        own, other = refs[:heads], refs[heads : 2 * heads]
        outs = refs[2 * heads : 2 * heads + len(steps)]
        kv, id_rows = refs[2 * heads + len(steps) : 2 * heads + len(steps) + 2]
        query, id_cols, acc, den = refs[2 * heads + len(steps) + 2 :]
        rows = kv.shape[1]
        for b, source in enumerate(list(own) + list(other)):
            kv[b] = source[:rows, :]
            tile = source[rows:, :].astype(jnp.float32)
            id_row = jnp.concatenate(
                [tile[r : r + 1, :] for r in range(rows // (2 * width))], axis=1
            )
            id_rows[b] = jnp.broadcast_to(id_row, (8, rows))
    else:
        kv, id_rows = refs[:2]
        outs = refs[2 : 2 + len(steps)]
        query, id_cols, acc, den = refs[2 + len(steps) :]
        rows = kv.shape[1]

    count = 2 * heads
    cluster_col = lax.broadcasted_iota(jnp.int32, (owned, rows), 0)
    wanted = jnp.concatenate(
        [cluster_col + owned * block_of(k, heads) for k in steps], axis=0
    ).astype(jnp.float32)
    sums = jnp.zeros((len(steps) * owned, width), jnp.float32)
    for b in range(count):
        one_hot = jnp.where(wanted == id_rows[b, :1, :], 1.0, 0.0).astype(jnp.bfloat16)
        sums = sums + jnp.dot(one_hot, kv[b, :, :width], preferred_element_type=jnp.float32)

    def pair(b, masked):
        score = lax.dot_general(
            query[...],
            kv[b, :, :width],
            (((1,), (1,)), ((), ())),
            preferred_element_type=jnp.float32,
        )
        weight = jnp.exp(score)
        same = jnp.concatenate([id_cols[...]] * (rows // width), axis=1) == id_rows[b, :1, :]
        if masked:
            row_at = lax.broadcasted_iota(jnp.int32, weight.shape, 0)
            col_at = lax.broadcasted_iota(jnp.int32, weight.shape, 1)
            same = jnp.logical_and(same, col_at <= row_at)
        weight = jnp.where(same, weight, 0.0)
        share = weight[:, :width]
        for part in range(1, rows // width):
            share = share + weight[:, part * width : (part + 1) * width]
        mixed = jnp.dot(
            weight.astype(jnp.bfloat16), kv[b, :, width:], preferred_element_type=jnp.float32
        )
        if masked:
            den[...] = share
            acc[...] = mixed
        else:
            den[...] += share
            acc[...] += mixed

    for at, k in enumerate(steps):
        query[...] = kv[k, :, :width] * jnp.bfloat16(SCORE_SCALE)
        for part in range(rows // width):
            here = pl.ds(part * width, width)
            id_cols[here, :] = jnp.transpose(
                jnp.broadcast_to(id_rows[k, :1, part * width : (part + 1) * width], (width, width))
            )
        pair(k, True)
        block = block_of(k, heads)

        def per_key(b, carry):
            @pl.when(block_of(b, heads) < block)
            def _():
                pair(b, False)

            return carry

        lax.fori_loop(0, count, per_key, 0)
        out = outs[at]
        whole = jnp.sum(den[...], axis=-1, keepdims=True)
        out[:rows, :] = (acc[...] / whole).astype(jnp.bfloat16)
        out[rows:, :] = sums[at * owned : (at + 1) * owned].astype(jnp.bfloat16)


def attend(inputs, heads, rows, width, owned, steps, first):
    result = shape((rows + owned, width))
    out_shape = (result,) * len(steps)
    if first:
        out_shape += (
            shape((2 * heads, rows, 2 * width)),
            shape((2 * heads, 8, rows), jnp.float32),
        )
    units = (heads * heads + heads // 2) * len(steps) // heads
    return pl.pallas_call(
        functools.partial(
            attend_body, heads=heads, width=width, owned=owned, steps=steps, first=first
        ),
        out_shape=out_shape,
        in_specs=[vmem_spec()] * len(inputs),
        out_specs=(vmem_spec(),) * len(out_shape),
        scratch_shapes=[
            pltpu.VMEM((rows, width), jnp.bfloat16),
            pltpu.VMEM((rows, width), jnp.float32),
            pltpu.VMEM((rows, width), jnp.float32),
            pltpu.VMEM((rows, width), jnp.float32),
        ],
        compiler_params=params(),
        cost_estimate=cost(
            units * rows * rows * width * 8,
            2 * heads * rows * width * 4,
            units * rows * rows,
        ),
        name="attend",
    )(*inputs)


def cut_body(*refs, heads, share):
    back, centroids = refs[:heads], refs[heads]
    kept, away, updated = refs[heads + 1], refs[heads + 2 : -1], refs[-1]
    z = lax.axis_index("seq") >> 1
    at = lax.axis_index("tensor")
    owned = centroids.shape[1]
    for k in range(heads):
        for turn in range(len(away) + 1):
            here = pl.ds(pl.multiple_of((at ^ turn) * share, share), share)
            (kept if turn == 0 else away[turn - 1])[k] = back[k][here, :]
        rows = back[k].shape[0] - owned
        sums = back[k][rows:, :].astype(jnp.float32)
        head = z ^ k
        updated[head] = EMA_DECAY * centroids[head] + (1.0 - EMA_DECAY) * sums


def cut(back, centroids, share, tensor_count):
    heads, width = len(back), back[0].shape[1]
    piece = shape((heads, share, width))
    return pl.pallas_call(
        functools.partial(cut_body, heads=heads, share=share),
        out_shape=(piece,) * tensor_count + (shape(centroids.shape, jnp.float32),),
        in_specs=[vmem_spec()] * (heads + 1),
        out_specs=(vmem_spec(),) * (tensor_count + 1),
        compiler_params=params(),
        cost_estimate=cost(centroids.size, 2 * heads * tensor_count * share * width * 2),
        name="cut",
    )(*back, centroids)


def mix_body(*refs, heads, width, groups):
    pieces, weights = refs[:groups], refs[groups : 2 * groups]
    tokens, mine, got, came, out, left, buf, sems = refs[2 * groups :]
    copies = [
        pltpu.make_async_copy(weights[g], buf.at[g], sems.at[g]) for g in range(groups)
    ]
    for copy in copies:
        copy.start()
    z = lax.axis_index("seq") >> 1
    at = lax.axis_index("tensor")
    share = out.shape[0]
    for g in range(groups):
        for k in range(heads):
            cols = pl.ds(pl.multiple_of((z ^ k) * width, width), width)
            left[g, :, cols] = pieces[g][k]
    x = at // 2
    total = mine[x] + got[x].astype(jnp.float32) + came[...].astype(jnp.float32)
    for g in range(groups):
        copies[g].wait()
        total = total + jnp.dot(left[g], buf[g], preferred_element_type=jnp.float32)
    here = pl.ds(pl.multiple_of(at * share, share), share)
    out[...] = (tokens[here, :].astype(jnp.float32) + total).astype(jnp.bfloat16)


def mix(pieces, weights, tokens, mine, got, came):
    groups = len(pieces)
    heads, share, width = pieces[0].shape
    depth = tokens.shape[1]
    return pl.pallas_call(
        functools.partial(mix_body, heads=heads, width=width, groups=groups),
        out_shape=shape((share, depth)),
        in_specs=[vmem_spec()] * groups + [any_spec()] * groups + [vmem_spec()] * 4,
        out_specs=vmem_spec(),
        scratch_shapes=[
            pltpu.VMEM((groups, share, heads * width), jnp.bfloat16),
            pltpu.VMEM((groups, heads * width, depth), jnp.bfloat16),
            pltpu.SemaphoreType.DMA((groups,)),
        ],
        compiler_params=params(),
        cost_estimate=cost(
            2 * groups * share * heads * width * depth,
            2 * groups * heads * width * depth + 8 * share * depth,
        ),
        name="mix",
    )(*pieces, *weights, tokens, mine, got, came)


def by_heads(
    tokens, norm_gain, w_qk, w_value, w_out, w_up, w_down, centroids, clusters, slots
):
    tok_rows, _ = tokens.shape
    seq_count = lax.axis_size("seq")
    tensor_count = lax.axis_size("tensor")
    heads = clusters.shape[0]
    owned = centroids.shape[1]
    width = w_qk.shape[1] // heads
    share = tok_rows // tensor_count
    swaps = [None] + [[(t, t ^ d) for t in range(tensor_count)] for d in range(1, tensor_count)]

    w_x = lax.ppermute(w_out, "tensor", swaps[2])
    w_core = lax.ppermute(w_out, "tensor", swaps[1])

    *messages, normed = project(tokens, norm_gain, w_qk, w_value, clusters, heads, width)
    steps = [owner_pairs(k, seq_count, tensor_count) for k in range(heads)]
    own, other = [None] * heads, [None] * heads
    for k in reversed(range(heads)):
        own[k] = lax.ppermute(messages[k], BOTH, steps[k])
    hidden = up(normed, w_up)
    for k in range(heads):
        other[k] = lax.ppermute(own[k], "tensor", swaps[1])
    mine, sent = down(hidden, w_down, share)
    got = lax.ppermute(sent, "tensor", swaps[1])
    picked = pick(mine, got)
    came = lax.ppermute(picked, "tensor", swaps[2])
    w_both = lax.ppermute(w_x, "tensor", swaps[1])

    back = [None] * heads
    far = tuple(reversed(range(heads // 2, heads)))
    near = tuple(reversed(range(heads // 2)))
    *results, kv, id_rows = attend(
        own + other, heads, tok_rows, width, owned, far, True
    )
    for k, result in zip(far, results):
        back[k] = lax.ppermute(result, BOTH, turned(steps[k]))
    results = attend([kv, id_rows], heads, tok_rows, width, owned, near, False)
    for k, result in zip(near, results):
        back[k] = lax.ppermute(result, BOTH, turned(steps[k]))

    kept, *away, new_centroids = cut(back, centroids, share, tensor_count)
    arrived = [lax.ppermute(away[d - 1], "tensor", swaps[d]) for d in range(1, tensor_count)]
    mixed_rows = mix(
        [kept] + arrived, [w_out, w_core, w_x, w_both], tokens, mine, got, came
    )
    return (mixed_rows, new_centroids)


def by_clusters(tokens, norm_gain, w_qk, w_value, w_out, w_up, w_down, centroids, clusters, slots):
    tok_rows = tokens.shape[0]
    seq_count = lax.axis_size("seq")
    tensor_count = lax.axis_size("tensor")
    heads_here = clusters.shape[0]
    owned_count = centroids.shape[1]
    head_width = w_qk.shape[1] // heads_here
    share_rows = tok_rows // tensor_count
    row_first = lax.axis_index("tensor") * share_rows
    tokens_wide = tokens.astype(jnp.float32)
    normed = (
        tokens_wide
        * lax.rsqrt(jnp.mean(tokens_wide * tokens_wide, axis=-1, keepdims=True) + NORM_EPS)
        * norm_gain
    ).astype(jnp.bfloat16)
    key_proj = jnp.dot(normed, w_qk, preferred_element_type=jnp.float32).reshape(
        tok_rows, heads_here, head_width
    )
    key_unit = (
        key_proj * lax.rsqrt(jnp.sum(key_proj * key_proj, axis=-1, keepdims=True) + NORM_EPS)
    ).astype(jnp.bfloat16)
    val_proj = (
        jnp.dot(normed, w_value, preferred_element_type=jnp.float32)
        .astype(jnp.bfloat16)
        .reshape(tok_rows, heads_here, head_width)
    )
    positions = lax.axis_index("seq") * tok_rows + jnp.arange(tok_rows, dtype=jnp.int32)
    pos_high = (positions // 256).astype(jnp.float32).astype(jnp.bfloat16)
    pos_low = (positions % 256).astype(jnp.float32).astype(jnp.bfloat16)
    flat_slot = clusters.T * CAP + slots.T
    head_grid = jnp.broadcast_to(jnp.arange(heads_here, dtype=jnp.int32)[None, :], flat_slot.shape)
    slot_total = CLUSTERS * CAP
    layout = (heads_here, seq_count, owned_count, CAP)
    key_buf = (
        jnp.zeros((heads_here, slot_total, head_width), jnp.bfloat16)
        .at[head_grid, flat_slot]
        .set(key_unit)
        .reshape(layout + (head_width,))
    )
    val_buf = (
        jnp.zeros((heads_here, slot_total, head_width), jnp.bfloat16)
        .at[head_grid, flat_slot]
        .set(val_proj)
        .reshape(layout + (head_width,))
    )
    high_buf = (
        jnp.full((heads_here, slot_total), 256.0, jnp.bfloat16)
        .at[head_grid, flat_slot]
        .set(jnp.broadcast_to(pos_high[:, None], flat_slot.shape))
        .reshape(layout)
    )
    low_buf = (
        jnp.zeros((heads_here, slot_total), jnp.bfloat16)
        .at[head_grid, flat_slot]
        .set(jnp.broadcast_to(pos_low[:, None], flat_slot.shape))
        .reshape(layout)
    )
    key_in = lax.all_to_all(key_buf, "seq", split_axis=1, concat_axis=1, tiled=True)
    val_in = lax.all_to_all(val_buf, "seq", split_axis=1, concat_axis=1, tiled=True)
    high_in = lax.all_to_all(high_buf, "seq", split_axis=1, concat_axis=1, tiled=True)
    low_in = lax.all_to_all(low_buf, "seq", split_axis=1, concat_axis=1, tiled=True)
    scores = (
        jnp.einsum("hskad,htkbd->hksatb", key_in, key_in, preferred_element_type=jnp.float32)
        * SCORE_SCALE
    )
    key_place = high_in.astype(jnp.float32) * 256.0 + low_in.astype(jnp.float32)
    ordered = jnp.transpose(key_place, (0, 2, 1, 3))
    causal = ordered[:, :, None, None, :, :] <= ordered[:, :, :, :, None, None]
    exponent = jnp.where(causal, jnp.exp(scores), 0.0)
    weights = (exponent / jnp.sum(exponent, axis=(4, 5), keepdims=True)).astype(jnp.bfloat16)
    mixed_out = jnp.einsum(
        "hksatb,htkbd->hskad", weights, val_in, preferred_element_type=jnp.float32
    ).astype(jnp.bfloat16)
    returned_back = lax.all_to_all(mixed_out, "seq", split_axis=1, concat_axis=1, tiled=True)
    one_hot = (clusters[:, :, None] == jnp.arange(CLUSTERS, dtype=jnp.int32)[None, None, :]).astype(
        jnp.bfloat16
    )
    local_sums = jnp.einsum("htk,thd->hkd", one_hot, key_unit, preferred_element_type=jnp.float32)
    totals = lax.psum_scatter(
        local_sums.astype(jnp.bfloat16), "seq", scatter_dimension=1, tiled=True
    ).astype(jnp.float32)
    new_centroids = EMA_DECAY * centroids + (1.0 - EMA_DECAY) * totals
    returned = returned_back.reshape(heads_here, slot_total, head_width)
    attended = returned[head_grid, flat_slot].reshape(tok_rows, heads_here * head_width)
    attn_part = jnp.dot(attended, w_out, preferred_element_type=jnp.float32)
    hidden = jax.nn.relu(jnp.dot(normed, w_up, preferred_element_type=jnp.float32)).astype(
        jnp.bfloat16
    )
    ffn_part = jnp.dot(hidden, w_down, preferred_element_type=jnp.float32)
    summed = lax.psum_scatter(
        rounded(attn_part + ffn_part).astype(jnp.bfloat16),
        "tensor",
        scatter_dimension=0,
        tiled=True,
    ).astype(jnp.float32)
    own_rows = lax.dynamic_slice_in_dim(tokens_wide, row_first, share_rows, 0)
    mixed_rows = (own_rows + summed).astype(jnp.bfloat16)
    return (mixed_rows, new_centroids)


def solution(mesh):
    in_specs = (
        P("seq", None),
        P(),
        P(None, "tensor"),
        P(None, "tensor"),
        P("tensor", None),
        P(None, "tensor"),
        P("tensor", None),
        P("tensor", "seq", None),
        P("tensor", "seq"),
        P("tensor", "seq"),
    )
    out_specs = (P(("seq", "tensor"), None), P("tensor", "seq", None))
    sizes = dict(mesh.shape)

    def local(*args):
        heads = args[8].shape[0]
        fits = (
            sizes["tensor"] == 4
            and sizes["seq"] == 2 * heads
            and heads & (heads - 1) == 0
            and heads > 1
        )
        if not fits:
            return by_clusters(*args)
        return by_heads(*args)

    return jax.shard_map(
        local, mesh=mesh, in_specs=in_specs, out_specs=out_specs, check_vma=False
    )
```

```python
import functools

import jax
import jax.numpy as jnp
from jax import lax
from jax.experimental import pallas as pl
from jax.experimental.pallas import tpu as pltpu
from jax.sharding import PartitionSpec as P


CLUSTERS = 256
CAP = 4

SCORE_SCALE = 2.0
EMA_DECAY = 0.9
NORM_EPS = 1e-06
BOTH = ("seq", "tensor")
EXTRA = 16
MIB = 1024 * 1024


def rounded(term_value):
    return lax.optimization_barrier(term_value.astype(jnp.bfloat16)).astype(jnp.float32)


def owner_pairs(step, seq_count, tensor_count):
    pairs = []
    for s in range(seq_count):
        for t in range(tensor_count):
            z, y, c = s // 2, s % 2, t % 2
            dest_s = 2 * (z ^ step) + c
            dest_t = (t - c) + (y ^ (z & 1))
            pairs.append((s * tensor_count + t, dest_s * tensor_count + dest_t))
    return pairs


def turned(pairs):
    return [(b, a) for a, b in pairs]


def any_spec():
    return pl.BlockSpec(memory_space=pl.ANY)


def vmem_spec():
    return pl.BlockSpec(memory_space=pltpu.VMEM)


def held(value):
    return pltpu.with_memory_space_constraint(value, pltpu.HBM)


def params(mib):
    return pltpu.CompilerParams(vmem_limit_bytes=mib * MIB)


def cost(flops, moved, transcendentals=0):
    return pl.CostEstimate(
        flops=flops, bytes_accessed=moved, transcendentals=transcendentals
    )


def shape(dims, kind=jnp.bfloat16):
    return jax.ShapeDtypeStruct(dims, kind)


def project_body(
    tokens_at, gain_at, w_qk, w_value, clusters_at, *rest, heads, width, parts
):
    outs, normed = rest[:heads], rest[heads]
    tokens, gain, clusters, qk_buf, val_buf, sems, token_sems, small_sems = rest[heads + 1 :]
    step = tokens.shape[0] // parts
    small = (
        pltpu.make_async_copy(gain_at, gain, small_sems.at[0]),
        pltpu.make_async_copy(clusters_at, clusters, small_sems.at[1]),
    )
    slabs = [pl.ds(r * step, step) for r in range(parts)]
    slab_copies = [
        pltpu.make_async_copy(tokens_at.at[here, :], tokens.at[here, :], token_sems.at[r])
        for r, here in enumerate(slabs)
    ]
    for copy in (small[0], *slab_copies, small[1]):
        copy.start()
    z = lax.axis_index("seq") >> 1
    pairs = heads // 2
    span = 2 * width

    def copies(p):
        block = p ^ (z >> 1)
        cols = pl.ds(pl.multiple_of(block * span, span), span)
        return (
            pltpu.make_async_copy(w_qk.at[:, cols], qk_buf.at[p], sems.at[2 * p]),
            pltpu.make_async_copy(w_value.at[:, cols], val_buf.at[p], sems.at[2 * p + 1]),
        )

    for p in range(pairs):
        for copy in copies(p):
            copy.start()
    small[0].wait()
    for copy, here in zip(slab_copies, slabs):
        copy.wait()
        wide = tokens[here, :].astype(jnp.float32)
        mean = jnp.mean(wide * wide, axis=-1, keepdims=True)
        normed[here, :] = (wide * lax.rsqrt(mean + NORM_EPS) * gain[...]).astype(jnp.bfloat16)
    small[1].wait()
    rows = tokens.shape[0]
    odd = (z & 1) == 1
    row_at = lax.broadcasted_iota(jnp.int32, (EXTRA, span), 0)
    for p in range(pairs):
        key_copy, val_copy = copies(p)
        key_copy.wait()
        key_proj = jnp.dot(normed[...], qk_buf[p], preferred_element_type=jnp.float32)
        units = []
        for q in range(2):
            k = key_proj[:, q * width : (q + 1) * width]
            total = jnp.sum(k * k, axis=-1, keepdims=True)
            units.append((k * lax.rsqrt(total + NORM_EPS)).astype(jnp.bfloat16))
        val_copy.wait()
        val_proj = jnp.dot(normed[...], val_buf[p], preferred_element_type=jnp.float32)
        values = [
            val_proj[:, q * width : (q + 1) * width].astype(jnp.bfloat16) for q in range(2)
        ]
        for q in range(2):
            out = outs[2 * p + q]
            out[:rows, :width] = jnp.where(odd, units[1 - q], units[q])
            out[:rows, width:] = jnp.where(odd, values[1 - q], values[q])
            id_row = clusters[pl.ds((2 * p + q) ^ z, 1), :].astype(jnp.float32)
            tail = jnp.zeros((EXTRA, span), jnp.float32)
            for part in range(rows // span):
                piece = id_row[:, part * span : (part + 1) * span]
                tail = jnp.where(row_at == part, piece, tail)
            out[rows:, :] = tail.astype(jnp.bfloat16)


def project(tokens, gain, w_qk, w_value, clusters, heads, width, parts=4):
    rows, depth = tokens.shape
    pairs = heads // 2
    return pl.pallas_call(
        functools.partial(project_body, heads=heads, width=width, parts=parts),
        out_shape=(shape((rows + EXTRA, 2 * width)),) * heads + (shape((rows, depth)),),
        in_specs=[any_spec()] * 5,
        out_specs=(vmem_spec(),) * (heads + 1),
        scratch_shapes=[
            pltpu.VMEM((rows, depth), jnp.bfloat16),
            pltpu.VMEM((1, depth), jnp.float32),
            pltpu.VMEM(clusters.shape, jnp.int32),
            pltpu.VMEM((pairs, depth, 2 * width), jnp.bfloat16),
            pltpu.VMEM((pairs, depth, 2 * width), jnp.bfloat16),
            pltpu.SemaphoreType.DMA((2 * pairs,)),
            pltpu.SemaphoreType.DMA((parts,)),
            pltpu.SemaphoreType.DMA((2,)),
        ],
        compiler_params=params(20),
        cost_estimate=cost(
            4 * rows * depth * heads * width,
            4 * (depth * heads * width + rows * depth + rows * heads * width),
        ),
        name="project",
    )(*[held(a) for a in (tokens, gain.reshape(1, depth), w_qk, w_value, clusters)])


def up_body(normed, w_up, hidden):
    grown = jnp.dot(normed[...], w_up[...], preferred_element_type=jnp.float32)
    hidden[...] = jnp.maximum(grown, 0.0).astype(jnp.bfloat16)


def up(normed, w_up, blocks=2):
    rows, depth = normed.shape
    units = w_up.shape[1]
    block = units // blocks
    return pl.pallas_call(
        up_body,
        grid=(blocks,),
        out_shape=shape((rows, units)),
        in_specs=[
            pl.BlockSpec((rows, depth), lambda i: (0, 0)),
            pl.BlockSpec((depth, block), lambda i: (0, i)),
        ],
        out_specs=pl.BlockSpec((rows, block), lambda i: (0, i)),
        compiler_params=params(24),
        cost_estimate=cost(2 * rows * depth * units, 2 * depth * units + 4 * rows * depth),
        name="grow",
    )(normed, w_up)


def down_body(hidden, w_down, mine, far, away, held, *, share):
    at = lax.axis_index("tensor")
    held[...] = jnp.dot(hidden[...], w_down[...], preferred_element_type=jnp.float32)

    def quarter(turn):
        return held[pl.ds(pl.multiple_of((at ^ turn) * share, share), share), :]

    mine[...] = quarter(0)
    far[...] = quarter(2)
    away[0] = quarter(1).astype(jnp.bfloat16)
    away[1] = quarter(3).astype(jnp.bfloat16)


def down(hidden, w_down, share, blocks=2):
    rows, units = hidden.shape
    depth = w_down.shape[1]
    block = depth // blocks
    one = pl.BlockSpec((share, block), lambda i: (0, i))
    return pl.pallas_call(
        functools.partial(down_body, share=share),
        grid=(blocks,),
        out_shape=(
            shape((share, depth), jnp.float32),
            shape((share, depth), jnp.float32),
            shape((2, share, depth)),
        ),
        in_specs=[
            pl.BlockSpec((rows, units), lambda i: (0, 0)),
            pl.BlockSpec((units, block), lambda i: (0, i)),
        ],
        out_specs=(one, one, pl.BlockSpec((2, share, block), lambda i: (0, 0, i))),
        scratch_shapes=[pltpu.VMEM((rows, block), jnp.float32)],
        compiler_params=params(26),
        cost_estimate=cost(2 * rows * depth * units, 2 * depth * units + 6 * rows * depth),
        name="shrink",
    )(hidden, w_down)


def block_of(b, heads):
    z = lax.axis_index("seq") >> 1
    core = lax.axis_index("tensor") % 2
    pair = z ^ (b % heads)
    return 2 * pair + (core ^ (pair & 1) ^ (b // heads))


def attend_body(*refs, heads, width, owned, steps, first):
    if first:
        own, other = refs[:heads], refs[heads : 2 * heads]
        far, got = refs[2 * heads : 2 * heads + 2]
        refs = refs[2 * heads + 2 :]
        outs = refs[: len(steps)]
        kv, id_rows, picked = refs[len(steps) : len(steps) + 3]
        query, id_cols, acc, den = refs[len(steps) + 3 :]
        rows = kv.shape[1]
        picked[...] = (far[...] + got[1].astype(jnp.float32)).astype(jnp.bfloat16)
        for b, source in enumerate(list(own) + list(other)):
            kv[b] = source[:rows, :]
            tile = source[rows:, :].astype(jnp.float32)
            id_row = jnp.concatenate(
                [tile[r : r + 1, :] for r in range(rows // (2 * width))], axis=1
            )
            id_rows[b] = jnp.broadcast_to(id_row, (8, rows))
    else:
        kv, id_rows = refs[:2]
        outs = refs[2 : 2 + len(steps)]
        query, id_cols, acc, den = refs[2 + len(steps) :]
        rows = kv.shape[1]

    count = 2 * heads
    cluster_col = lax.broadcasted_iota(jnp.int32, (owned, rows), 0)
    wanted = jnp.concatenate(
        [cluster_col + owned * block_of(k, heads) for k in steps], axis=0
    ).astype(jnp.float32)
    sums = jnp.zeros((len(steps) * owned, width), jnp.float32)
    for b in range(count):
        one_hot = jnp.where(wanted == id_rows[b, :1, :], 1.0, 0.0).astype(jnp.bfloat16)
        sums = sums + jnp.dot(one_hot, kv[b, :, :width], preferred_element_type=jnp.float32)

    def pair(b, masked):
        score = lax.dot_general(
            query[...],
            kv[b, :, :width],
            (((1,), (1,)), ((), ())),
            preferred_element_type=jnp.float32,
        )
        weight = jnp.exp(score)
        same = jnp.concatenate([id_cols[...]] * (rows // width), axis=1) == id_rows[b, :1, :]
        if masked:
            row_at = lax.broadcasted_iota(jnp.int32, weight.shape, 0)
            col_at = lax.broadcasted_iota(jnp.int32, weight.shape, 1)
            same = jnp.logical_and(same, col_at <= row_at)
        weight = jnp.where(same, weight, 0.0)
        share = weight[:, :width]
        for part in range(1, rows // width):
            share = share + weight[:, part * width : (part + 1) * width]
        mixed = jnp.dot(
            weight.astype(jnp.bfloat16), kv[b, :, width:], preferred_element_type=jnp.float32
        )
        if masked:
            den[...] = share
            acc[...] = mixed
        else:
            den[...] += share
            acc[...] += mixed

    for at, k in enumerate(steps):
        query[...] = kv[k, :, :width] * jnp.bfloat16(SCORE_SCALE)
        for part in range(rows // width):
            here = pl.ds(part * width, width)
            id_cols[here, :] = jnp.transpose(
                jnp.broadcast_to(id_rows[k, :1, part * width : (part + 1) * width], (width, width))
            )
        pair(k, True)
        block = block_of(k, heads)

        def per_key(b, carry):
            @pl.when(block_of(b, heads) < block)
            def _():
                pair(b, False)

            return carry

        lax.fori_loop(0, count, per_key, 0)
        out = outs[at]
        whole = jnp.sum(den[...], axis=-1, keepdims=True)
        out[:rows, :] = (acc[...] / whole).astype(jnp.bfloat16)
        out[rows:, :] = sums[at * owned : (at + 1) * owned].astype(jnp.bfloat16)


def attend(inputs, heads, rows, width, owned, steps, first):
    result = shape((rows + owned, width))
    out_shape = (result,) * len(steps)
    if first:
        out_shape += (
            shape((2 * heads, rows, 2 * width)),
            shape((2 * heads, 8, rows), jnp.float32),
            shape(inputs[-2].shape),
        )
    units = (heads * heads + heads // 2) * len(steps) // heads
    return pl.pallas_call(
        functools.partial(
            attend_body, heads=heads, width=width, owned=owned, steps=steps, first=first
        ),
        out_shape=out_shape,
        in_specs=[vmem_spec()] * len(inputs),
        out_specs=(vmem_spec(),) * len(out_shape),
        scratch_shapes=[
            pltpu.VMEM((rows, width), jnp.bfloat16),
            pltpu.VMEM((rows, width), jnp.float32),
            pltpu.VMEM((rows, width), jnp.float32),
            pltpu.VMEM((rows, width), jnp.float32),
        ],
        compiler_params=params(20),
        cost_estimate=cost(
            units * rows * rows * width * 8,
            2 * heads * rows * width * 4,
            units * rows * rows,
        ),
        name="attend",
    )(*inputs)


def cut_body(*refs, count, share):
    back, kept, away, sums = refs[:count], refs[count], refs[count + 1 : -1], refs[-1]
    at = lax.axis_index("tensor")
    for k in range(count):
        for turn in range(len(away) + 1):
            here = pl.ds(pl.multiple_of((at ^ turn) * share, share), share)
            (kept if turn == 0 else away[turn - 1])[k] = back[k][here, :]
        rows = back[k].shape[0] - sums.shape[1]
        sums[k] = back[k][rows:, :].astype(jnp.float32)


def cut(back, owned, share, tensor_count):
    count, width = len(back), back[0].shape[1]
    piece = shape((count, share, width))
    return pl.pallas_call(
        functools.partial(cut_body, count=count, share=share),
        out_shape=(piece,) * tensor_count + (shape((count, owned, width), jnp.float32),),
        in_specs=[vmem_spec()] * count,
        out_specs=(vmem_spec(),) * (tensor_count + 1),
        compiler_params=params(8),
        cost_estimate=cost(0, 4 * count * tensor_count * share * width),
        name="cut",
    )(*back)


def head_rows(weights, buf, sems, steps, width):
    z = lax.axis_index("seq") >> 1
    copies = []
    for g, w in enumerate(weights):
        for i, k in enumerate(steps):
            here = pl.ds(pl.multiple_of((z ^ k) * width, width), width)
            to = pl.ds((g * len(steps) + i) * width, width)
            copies.append(
                pltpu.make_async_copy(
                    w.at[here, :], buf.at[to, :], sems.at[g * len(steps) + i]
                )
            )
    return copies


def side_by_side(pieces, count):
    return jnp.concatenate([p[k] for p in pieces for k in range(count)], axis=1)


def mix_first_body(*refs, groups, width, steps, later):
    pieces, weights = refs[:groups], refs[groups : 2 * groups]
    tokens, mine, got, total, kept, buf, sems, later_sems = refs[2 * groups :]
    now = head_rows(weights, buf, sems, steps, width)
    then = head_rows(weights, kept, later_sems, later, width)
    for copy in now + then:
        copy.start()
    share = total.shape[0]
    at = lax.axis_index("tensor")
    here = pl.ds(pl.multiple_of(at * share, share), share)
    left = side_by_side(pieces, len(steps))
    known = tokens[here, :].astype(jnp.float32) + mine[...] + got[0].astype(jnp.float32)
    for copy in now:
        copy.wait()
    total[...] = known + jnp.dot(left, buf[...], preferred_element_type=jnp.float32)
    for copy in then:
        copy.wait()


def mix_first(pieces, weights, tokens, mine, got, steps, later):
    groups = len(pieces)
    count, share, width = pieces[0].shape
    depth = tokens.shape[1]
    held = (groups * count * width, depth)
    return pl.pallas_call(
        functools.partial(
            mix_first_body, groups=groups, width=width, steps=steps, later=later
        ),
        out_shape=(shape((share, depth), jnp.float32), shape(held)),
        in_specs=[vmem_spec()] * groups + [any_spec()] * groups + [vmem_spec()] * 3,
        out_specs=(vmem_spec(), vmem_spec()),
        scratch_shapes=[
            pltpu.VMEM(held, jnp.bfloat16),
            pltpu.SemaphoreType.DMA((groups * count,)),
            pltpu.SemaphoreType.DMA((groups * count,)),
        ],
        compiler_params=params(24),
        cost_estimate=cost(
            2 * groups * share * count * width * depth,
            4 * groups * count * width * depth + 8 * share * depth,
        ),
        name="mix_first",
    )(*pieces, *weights, tokens, mine, got)


def mix_last_body(*refs, groups, steps, later):
    pieces = refs[:groups]
    total, held, came, first_sums, last_sums, centroids, out, updated = refs[groups:]
    z = lax.axis_index("seq") >> 1
    left = side_by_side(pieces, len(later))
    known = total[...] + came[...].astype(jnp.float32)
    summed = known + jnp.dot(left, held[...], preferred_element_type=jnp.float32)
    out[...] = summed.astype(jnp.bfloat16)
    for sums, turns in ((first_sums, steps), (last_sums, later)):
        for i, k in enumerate(turns):
            head = z ^ k
            updated[head] = EMA_DECAY * centroids[head] + (1.0 - EMA_DECAY) * sums[i]


def mix_last(pieces, total, held, came, first_sums, last_sums, centroids, steps, later):
    groups = len(pieces)
    share, depth = total.shape
    return pl.pallas_call(
        functools.partial(mix_last_body, groups=groups, steps=steps, later=later),
        out_shape=(shape((share, depth)), shape(centroids.shape, jnp.float32)),
        in_specs=[vmem_spec()] * (groups + 6),
        out_specs=(vmem_spec(), vmem_spec()),
        compiler_params=params(16),
        cost_estimate=cost(2 * held.size * share, 2 * held.size + 8 * share * depth),
        name="mix_last",
    )(*pieces, total, held, came, first_sums, last_sums, centroids)


def by_heads(
    tokens, norm_gain, w_qk, w_value, w_out, w_up, w_down, centroids, clusters, slots
):
    tok_rows, _ = tokens.shape
    seq_count = lax.axis_size("seq")
    tensor_count = lax.axis_size("tensor")
    heads = clusters.shape[0]
    owned = centroids.shape[1]
    width = w_qk.shape[1] // heads
    share = tok_rows // tensor_count
    swaps = [None] + [[(t, t ^ d) for t in range(tensor_count)] for d in range(1, tensor_count)]

    w_x = lax.ppermute(w_out, "tensor", swaps[2])
    w_core = lax.ppermute(w_out, "tensor", swaps[1])

    *messages, normed = project(tokens, norm_gain, w_qk, w_value, clusters, heads, width)
    steps = [owner_pairs(k, seq_count, tensor_count) for k in range(heads)]
    own, other = [None] * heads, [None] * heads
    for k in reversed(range(heads)):
        own[k] = lax.ppermute(messages[k], BOTH, steps[k])
    hidden = up(normed, held(w_up))
    for k in range(heads):
        other[k] = lax.ppermute(own[k], "tensor", swaps[1])
    mine, far, sent = down(hidden, held(w_down), share)
    got = lax.ppermute(sent, "tensor", swaps[1])

    early, late = (heads - 1, 0), (heads - 2, 1)
    back, pieces, sums = [None] * heads, {}, {}
    *results, kv, id_rows, picked = attend(
        own + other + [far, got], heads, tok_rows, width, owned, early, True
    )
    for k, result in zip(early, results):
        back[k] = lax.ppermute(result, BOTH, turned(steps[k]))
    results = attend([kv, id_rows], heads, tok_rows, width, owned, late, False)
    for k, result in zip(late, results):
        back[k] = lax.ppermute(result, BOTH, turned(steps[k]))
    w_both = lax.ppermute(w_x, "tensor", swaps[1])
    came = lax.ppermute(picked, "tensor", swaps[2])

    for name, turns in (("early", early), ("late", late)):
        kept, *away, sums[name] = cut([back[k] for k in turns], owned, share, tensor_count)
        pieces[name] = [kept] + [
            lax.ppermute(away[d - 1], "tensor", swaps[d])
            for d in range(1, tensor_count)
        ]
    total, late_rows = mix_first(
        pieces["early"], [held(w_out), w_core, w_x, w_both], tokens, mine, got, early, late
    )
    mixed_rows, new_centroids = mix_last(
        pieces["late"], total, late_rows, came, sums["early"], sums["late"], centroids, early, late
    )
    return (mixed_rows, new_centroids)


def by_clusters(tokens, norm_gain, w_qk, w_value, w_out, w_up, w_down, centroids, clusters, slots):
    tok_rows = tokens.shape[0]
    seq_count = lax.axis_size("seq")
    tensor_count = lax.axis_size("tensor")
    heads_here = clusters.shape[0]
    owned_count = centroids.shape[1]
    head_width = w_qk.shape[1] // heads_here
    share_rows = tok_rows // tensor_count
    row_first = lax.axis_index("tensor") * share_rows
    tokens_wide = tokens.astype(jnp.float32)
    normed = (
        tokens_wide
        * lax.rsqrt(jnp.mean(tokens_wide * tokens_wide, axis=-1, keepdims=True) + NORM_EPS)
        * norm_gain
    ).astype(jnp.bfloat16)
    key_proj = jnp.dot(normed, w_qk, preferred_element_type=jnp.float32).reshape(
        tok_rows, heads_here, head_width
    )
    key_unit = (
        key_proj * lax.rsqrt(jnp.sum(key_proj * key_proj, axis=-1, keepdims=True) + NORM_EPS)
    ).astype(jnp.bfloat16)
    val_proj = (
        jnp.dot(normed, w_value, preferred_element_type=jnp.float32)
        .astype(jnp.bfloat16)
        .reshape(tok_rows, heads_here, head_width)
    )
    positions = lax.axis_index("seq") * tok_rows + jnp.arange(tok_rows, dtype=jnp.int32)
    pos_high = (positions // 256).astype(jnp.float32).astype(jnp.bfloat16)
    pos_low = (positions % 256).astype(jnp.float32).astype(jnp.bfloat16)
    flat_slot = clusters.T * CAP + slots.T
    head_grid = jnp.broadcast_to(jnp.arange(heads_here, dtype=jnp.int32)[None, :], flat_slot.shape)
    slot_total = CLUSTERS * CAP
    layout = (heads_here, seq_count, owned_count, CAP)
    key_buf = (
        jnp.zeros((heads_here, slot_total, head_width), jnp.bfloat16)
        .at[head_grid, flat_slot]
        .set(key_unit)
        .reshape(layout + (head_width,))
    )
    val_buf = (
        jnp.zeros((heads_here, slot_total, head_width), jnp.bfloat16)
        .at[head_grid, flat_slot]
        .set(val_proj)
        .reshape(layout + (head_width,))
    )
    high_buf = (
        jnp.full((heads_here, slot_total), 256.0, jnp.bfloat16)
        .at[head_grid, flat_slot]
        .set(jnp.broadcast_to(pos_high[:, None], flat_slot.shape))
        .reshape(layout)
    )
    low_buf = (
        jnp.zeros((heads_here, slot_total), jnp.bfloat16)
        .at[head_grid, flat_slot]
        .set(jnp.broadcast_to(pos_low[:, None], flat_slot.shape))
        .reshape(layout)
    )
    key_in = lax.all_to_all(key_buf, "seq", split_axis=1, concat_axis=1, tiled=True)
    val_in = lax.all_to_all(val_buf, "seq", split_axis=1, concat_axis=1, tiled=True)
    high_in = lax.all_to_all(high_buf, "seq", split_axis=1, concat_axis=1, tiled=True)
    low_in = lax.all_to_all(low_buf, "seq", split_axis=1, concat_axis=1, tiled=True)
    scores = (
        jnp.einsum("hskad,htkbd->hksatb", key_in, key_in, preferred_element_type=jnp.float32)
        * SCORE_SCALE
    )
    key_place = high_in.astype(jnp.float32) * 256.0 + low_in.astype(jnp.float32)
    ordered = jnp.transpose(key_place, (0, 2, 1, 3))
    causal = ordered[:, :, None, None, :, :] <= ordered[:, :, :, :, None, None]
    exponent = jnp.where(causal, jnp.exp(scores), 0.0)
    weights = (exponent / jnp.sum(exponent, axis=(4, 5), keepdims=True)).astype(jnp.bfloat16)
    mixed_out = jnp.einsum(
        "hksatb,htkbd->hskad", weights, val_in, preferred_element_type=jnp.float32
    ).astype(jnp.bfloat16)
    returned_back = lax.all_to_all(mixed_out, "seq", split_axis=1, concat_axis=1, tiled=True)
    one_hot = (clusters[:, :, None] == jnp.arange(CLUSTERS, dtype=jnp.int32)[None, None, :]).astype(
        jnp.bfloat16
    )
    local_sums = jnp.einsum("htk,thd->hkd", one_hot, key_unit, preferred_element_type=jnp.float32)
    totals = lax.psum_scatter(
        local_sums.astype(jnp.bfloat16), "seq", scatter_dimension=1, tiled=True
    ).astype(jnp.float32)
    new_centroids = EMA_DECAY * centroids + (1.0 - EMA_DECAY) * totals
    returned = returned_back.reshape(heads_here, slot_total, head_width)
    attended = returned[head_grid, flat_slot].reshape(tok_rows, heads_here * head_width)
    attn_part = jnp.dot(attended, w_out, preferred_element_type=jnp.float32)
    hidden = jax.nn.relu(jnp.dot(normed, w_up, preferred_element_type=jnp.float32)).astype(
        jnp.bfloat16
    )
    ffn_part = jnp.dot(hidden, w_down, preferred_element_type=jnp.float32)
    summed = lax.psum_scatter(
        rounded(attn_part + ffn_part).astype(jnp.bfloat16),
        "tensor",
        scatter_dimension=0,
        tiled=True,
    ).astype(jnp.float32)
    own_rows = lax.dynamic_slice_in_dim(tokens_wide, row_first, share_rows, 0)
    mixed_rows = (own_rows + summed).astype(jnp.bfloat16)
    return (mixed_rows, new_centroids)


def solution(mesh):
    in_specs = (
        P("seq", None),
        P(),
        P(None, "tensor"),
        P(None, "tensor"),
        P("tensor", None),
        P(None, "tensor"),
        P("tensor", None),
        P("tensor", "seq", None),
        P("tensor", "seq"),
        P("tensor", "seq"),
    )
    out_specs = (P(("seq", "tensor"), None), P("tensor", "seq", None))
    sizes = dict(mesh.shape)

    def local(*args):
        heads = args[8].shape[0]
        fits = (
            sizes["tensor"] == 4
            and sizes["seq"] == 2 * heads
            and heads & (heads - 1) == 0
            and heads == 4
        )
        if not fits:
            return by_clusters(*args)
        return by_heads(*args)

    return jax.shard_map(
        local, mesh=mesh, in_specs=in_specs, out_specs=out_specs, check_vma=False
    )
```

```python
import functools

import jax
import jax.numpy as jnp
from jax import lax
from jax.experimental import pallas as pl
from jax.experimental.pallas import tpu as pltpu
from jax.sharding import PartitionSpec as P


CLUSTERS = 256
CAP = 4

SCORE_SCALE = 2.0
EMA_DECAY = 0.9
NORM_EPS = 1e-06
SEQ, TENSOR = "seq", "tensor"
BOTH = (SEQ, TENSOR)
EXTRA = 16
MIB = 1024 * 1024


def rounded(term_value):
    return lax.optimization_barrier(term_value.astype(jnp.bfloat16)).astype(jnp.float32)


def owner_pairs(step, seq_count, tensor_count):
    pairs = []
    for s in range(seq_count):
        for t in range(tensor_count):
            z, y, c = s // 2, s % 2, t % 2
            dest_s = 2 * (z ^ step) + c
            dest_t = (t - c) + (y ^ (z & 1))
            pairs.append((s * tensor_count + t, dest_s * tensor_count + dest_t))
    return pairs


def turned(pairs):
    return [(b, a) for a, b in pairs]


def any_spec():
    return pl.BlockSpec(memory_space=pl.ANY)


def vmem_spec():
    return pl.BlockSpec(memory_space=pltpu.VMEM)


def held(value):
    return pltpu.with_memory_space_constraint(value, pltpu.HBM)


def params(mib):
    return pltpu.CompilerParams(vmem_limit_bytes=mib * MIB)


def cost(flops, moved, transcendentals=0):
    return pl.CostEstimate(
        flops=flops, bytes_accessed=moved, transcendentals=transcendentals
    )


def shape(dims, kind=jnp.bfloat16):
    return jax.ShapeDtypeStruct(dims, kind)


def unit_heads(normed, w_qk, w_value, outs, clusters, steps, width):
    z = lax.axis_index(SEQ) >> 1
    rows = normed.shape[0]
    span = 2 * width
    odd = (z & 1) == 1
    row_at = lax.broadcasted_iota(jnp.int32, (EXTRA, span), 0)
    key_proj = jnp.dot(normed[...], w_qk[...], preferred_element_type=jnp.float32)
    units = []
    for q in range(2):
        k = key_proj[:, q * width : (q + 1) * width]
        total = jnp.sum(k * k, axis=-1, keepdims=True)
        units.append((k * lax.rsqrt(total + NORM_EPS)).astype(jnp.bfloat16))
    val_proj = jnp.dot(normed[...], w_value[...], preferred_element_type=jnp.float32)
    values = [val_proj[:, q * width : (q + 1) * width].astype(jnp.bfloat16) for q in range(2)]
    for q, out in enumerate(outs):
        out[:rows, :width] = jnp.where(odd, units[1 - q], units[q])
        out[:rows, width:] = jnp.where(odd, values[1 - q], values[q])
        id_row = clusters[pl.ds(steps[q] ^ z, 1), :].astype(jnp.float32)
        tail = jnp.zeros((EXTRA, span), jnp.float32)
        for part in range(rows // span):
            piece = id_row[:, part * span : (part + 1) * span]
            tail = jnp.where(row_at == part, piece, tail)
        out[rows:, :] = tail.astype(jnp.bfloat16)


def project_far_body(
    tokens_at, gain_at, w_qk, w_value, clusters_at, w_out, *rest, heads, width, parts
):
    out_low, out_high, normed, clusters, qk_next, val_next, out_part = rest[:7]
    tokens, gain, qk_buf, val_buf, sems, token_sems = rest[7:]
    z = lax.axis_index(SEQ) >> 1
    y = lax.axis_index(SEQ) & 1
    step = tokens.shape[0] // parts
    span = 2 * width
    slabs = [pl.ds(r * step, step) for r in range(parts)]
    slab_copies = [
        pltpu.make_async_copy(tokens_at.at[here, :], tokens.at[here, :], token_sems.at[r])
        for r, here in enumerate(slabs)
    ]

    def columns(block):
        return pl.ds(pl.multiple_of(block * span, span), span)

    first, second = columns(1 ^ (z >> 1)), columns(z >> 1)
    half = out_part.shape[1]
    out_cols = pl.ds(pl.multiple_of(y * half, half), half)
    copies = [
        pltpu.make_async_copy(gain_at, gain, sems.at[0]),
        pltpu.make_async_copy(w_qk.at[:, first], qk_buf, sems.at[1]),
        pltpu.make_async_copy(w_value.at[:, first], val_buf, sems.at[2]),
        pltpu.make_async_copy(clusters_at, clusters, sems.at[3]),
        pltpu.make_async_copy(w_out.at[:, out_cols], out_part, sems.at[4]),
        pltpu.make_async_copy(w_qk.at[:, second], qk_next, sems.at[5]),
        pltpu.make_async_copy(w_value.at[:, second], val_next, sems.at[6]),
    ]
    for copy in (copies[0], *slab_copies, *copies[1:]):
        copy.start()
    copies[0].wait()
    for copy, here in zip(slab_copies, slabs):
        copy.wait()
        wide = tokens[here, :].astype(jnp.float32)
        mean = jnp.mean(wide * wide, axis=-1, keepdims=True)
        normed[here, :] = (wide * lax.rsqrt(mean + NORM_EPS) * gain[...]).astype(jnp.bfloat16)
    for copy in copies[1:4]:
        copy.wait()
    unit_heads(normed, qk_buf, val_buf, (out_low, out_high), clusters, (2, 3), width)
    for copy in copies[4:]:
        copy.wait()


def project_far(tokens, gain, w_qk, w_value, clusters, w_out, heads, width, parts=4):
    rows, depth = tokens.shape
    message = shape((rows + EXTRA, 2 * width))
    pair = (depth, 2 * width)
    return pl.pallas_call(
        functools.partial(project_far_body, heads=heads, width=width, parts=parts),
        out_shape=(
            message,
            message,
            shape((rows, depth)),
            shape(clusters.shape, jnp.int32),
            shape(pair),
            shape(pair),
            shape((w_out.shape[0], w_out.shape[1] // 2)),
        ),
        in_specs=[any_spec()] * 6,
        out_specs=(vmem_spec(),) * 7,
        scratch_shapes=[
            pltpu.VMEM((rows, depth), jnp.bfloat16),
            pltpu.VMEM((1, depth), jnp.float32),
            pltpu.VMEM(pair, jnp.bfloat16),
            pltpu.VMEM(pair, jnp.bfloat16),
            pltpu.SemaphoreType.DMA((7,)),
            pltpu.SemaphoreType.DMA((parts,)),
        ],
        compiler_params=params(20),
        cost_estimate=cost(8 * rows * depth * width, 2 * rows * depth + 12 * depth * width),
    )(*[held(a) for a in (tokens, gain.reshape(1, depth), w_qk, w_value, clusters, w_out)])


def project_near_body(normed, w_qk, w_value, clusters, out_low, out_high, *, width):
    unit_heads(normed, w_qk, w_value, (out_low, out_high), clusters, (0, 1), width)


def project_near(normed, w_qk, w_value, clusters, width):
    rows, depth = normed.shape
    message = shape((rows + EXTRA, 2 * width))
    return pl.pallas_call(
        functools.partial(project_near_body, width=width),
        out_shape=(message, message),
        in_specs=[vmem_spec()] * 4,
        out_specs=(vmem_spec(),) * 2,
        compiler_params=params(14),
        cost_estimate=cost(8 * rows * depth * width, 2 * rows * depth + 8 * depth * width),
    )(normed, w_qk, w_value, clusters)


def up_body(normed, w_up, hidden):
    grown = jnp.dot(normed[...], w_up[...], preferred_element_type=jnp.float32)
    hidden[...] = jnp.maximum(grown, 0.0).astype(jnp.bfloat16)


def up(normed, w_up, blocks=2):
    rows, depth = normed.shape
    units = w_up.shape[1]
    block = units // blocks
    return pl.pallas_call(
        up_body,
        grid=(blocks,),
        out_shape=shape((rows, units)),
        in_specs=[
            pl.BlockSpec((rows, depth), lambda i: (0, 0)),
            pl.BlockSpec((depth, block), lambda i: (0, i)),
        ],
        out_specs=pl.BlockSpec((rows, block), lambda i: (0, i)),
        compiler_params=params(24),
        cost_estimate=cost(2 * rows * depth * units, 2 * depth * units + 4 * rows * depth),
    )(normed, w_up)


def down_body(hidden, w_down, mine, far, away, held, *, share):
    at = lax.axis_index(TENSOR)
    held[...] = jnp.dot(hidden[...], w_down[...], preferred_element_type=jnp.float32)

    def quarter(turn):
        return held[pl.ds(pl.multiple_of((at ^ turn) * share, share), share), :]

    mine[...] = quarter(0)
    far[...] = quarter(2)
    away[0] = quarter(1).astype(jnp.bfloat16)
    away[1] = quarter(3).astype(jnp.bfloat16)


def down(hidden, w_down, share, blocks=2):
    rows, units = hidden.shape
    depth = w_down.shape[1]
    block = depth // blocks
    one = pl.BlockSpec((share, block), lambda i: (0, i))
    return pl.pallas_call(
        functools.partial(down_body, share=share),
        grid=(blocks,),
        out_shape=(
            shape((share, depth), jnp.float32),
            shape((share, depth), jnp.float32),
            shape((2, share, depth)),
        ),
        in_specs=[
            pl.BlockSpec((rows, units), lambda i: (0, 0)),
            pl.BlockSpec((units, block), lambda i: (0, i)),
        ],
        out_specs=(one, one, pl.BlockSpec((2, share, block), lambda i: (0, 0, i))),
        scratch_shapes=[pltpu.VMEM((rows, block), jnp.float32)],
        compiler_params=params(26),
        cost_estimate=cost(2 * rows * depth * units, 2 * depth * units + 6 * rows * depth),
    )(hidden, w_down)


def pick_body(far, got, sent):
    sent[...] = (far[...] + got[1].astype(jnp.float32)).astype(jnp.bfloat16)


def pick(far, got):
    return pl.pallas_call(
        pick_body,
        out_shape=shape(far.shape),
        in_specs=[vmem_spec(), vmem_spec()],
        out_specs=vmem_spec(),
        compiler_params=params(6),
        cost_estimate=cost(far.size, far.size * 8),
    )(far, got)


def block_of(b, heads):
    z = lax.axis_index(SEQ) >> 1
    core = lax.axis_index(TENSOR) % 2
    pair = z ^ (b % heads)
    return 2 * pair + (core ^ (pair & 1) ^ (b // heads))


def attend_body(*refs, heads, width, owned, steps, first):
    if first:
        own, other = refs[:heads], refs[heads : 2 * heads]
        refs = refs[2 * heads :]
        outs = refs[: len(steps)]
        kv, id_rows = refs[len(steps) : len(steps) + 2]
        query, id_cols, acc, den = refs[len(steps) + 2 :]
        rows = kv.shape[1]
        for b, source in enumerate(list(own) + list(other)):
            kv[b] = source[:rows, :]
            tile = source[rows:, :].astype(jnp.float32)
            id_row = jnp.concatenate(
                [tile[r : r + 1, :] for r in range(rows // (2 * width))], axis=1
            )
            id_rows[b] = jnp.broadcast_to(id_row, (8, rows))
    else:
        kv, id_rows = refs[:2]
        outs = refs[2 : 2 + len(steps)]
        query, id_cols, acc, den = refs[2 + len(steps) :]
        rows = kv.shape[1]

    count = 2 * heads
    cluster_col = lax.broadcasted_iota(jnp.int32, (owned, rows), 0)
    wanted = jnp.concatenate(
        [cluster_col + owned * block_of(k, heads) for k in steps], axis=0
    ).astype(jnp.float32)
    sums = jnp.zeros((len(steps) * owned, width), jnp.float32)
    for b in range(count):
        one_hot = jnp.where(wanted == id_rows[b, :1, :], 1.0, 0.0).astype(jnp.bfloat16)
        sums = sums + jnp.dot(one_hot, kv[b, :, :width], preferred_element_type=jnp.float32)

    def pair(b, masked):
        score = lax.dot_general(
            query[...],
            kv[b, :, :width],
            (((1,), (1,)), ((), ())),
            preferred_element_type=jnp.float32,
        )
        weight = jnp.exp(score)
        same = jnp.concatenate([id_cols[...]] * (rows // width), axis=1) == id_rows[b, :1, :]
        if masked:
            row_at = lax.broadcasted_iota(jnp.int32, weight.shape, 0)
            col_at = lax.broadcasted_iota(jnp.int32, weight.shape, 1)
            same = jnp.logical_and(same, col_at <= row_at)
        weight = jnp.where(same, weight, 0.0)
        share = weight[:, :width]
        for part in range(1, rows // width):
            share = share + weight[:, part * width : (part + 1) * width]
        mixed = jnp.dot(
            weight.astype(jnp.bfloat16), kv[b, :, width:], preferred_element_type=jnp.float32
        )
        if masked:
            den[...] = share
            acc[...] = mixed
        else:
            den[...] += share
            acc[...] += mixed

    for at, k in enumerate(steps):
        query[...] = kv[k, :, :width] * jnp.bfloat16(SCORE_SCALE)
        for part in range(rows // width):
            here = pl.ds(part * width, width)
            id_cols[here, :] = jnp.transpose(
                jnp.broadcast_to(id_rows[k, :1, part * width : (part + 1) * width], (width, width))
            )
        pair(k, True)
        block = block_of(k, heads)

        def per_key(b, carry):
            @pl.when(block_of(b, heads) < block)
            def _():
                pair(b, False)

            return carry

        lax.fori_loop(0, count, per_key, 0)
        out = outs[at]
        whole = jnp.sum(den[...], axis=-1, keepdims=True)
        out[:rows, :] = (acc[...] / whole).astype(jnp.bfloat16)
        out[rows:, :] = sums[at * owned : (at + 1) * owned].astype(jnp.bfloat16)


def attend(inputs, heads, rows, width, owned, steps, first):
    result = shape((rows + owned, width))
    out_shape = (result,) * len(steps)
    if first:
        out_shape += (
            shape((2 * heads, rows, 2 * width)),
            shape((2 * heads, 8, rows), jnp.float32),
        )
    units = (heads * heads + heads // 2) * len(steps) // heads
    return pl.pallas_call(
        functools.partial(
            attend_body, heads=heads, width=width, owned=owned, steps=steps, first=first
        ),
        out_shape=out_shape,
        in_specs=[vmem_spec()] * len(inputs),
        out_specs=(vmem_spec(),) * len(out_shape),
        scratch_shapes=[
            pltpu.VMEM((rows, width), jnp.bfloat16),
            pltpu.VMEM((rows, width), jnp.float32),
            pltpu.VMEM((rows, width), jnp.float32),
            pltpu.VMEM((rows, width), jnp.float32),
        ],
        compiler_params=params(20),
        cost_estimate=cost(
            units * rows * rows * width * 8,
            2 * heads * rows * width * 4,
            units * rows * rows,
        ),
    )(*inputs)


def cut_body(*refs, count, share):
    back, kept, away, sums = refs[:count], refs[count], refs[count + 1 : -1], refs[-1]
    at = lax.axis_index(TENSOR)
    for k in range(count):
        for turn in range(len(away) + 1):
            here = pl.ds(pl.multiple_of((at ^ turn) * share, share), share)
            (kept if turn == 0 else away[turn - 1])[k] = back[k][here, :]
        rows = back[k].shape[0] - sums.shape[1]
        sums[k] = back[k][rows:, :].astype(jnp.float32)


def cut(back, owned, share, tensor_count):
    count, width = len(back), back[0].shape[1]
    piece = shape((count, share, width))
    return pl.pallas_call(
        functools.partial(cut_body, count=count, share=share),
        out_shape=(piece,) * tensor_count + (shape((count, owned, width), jnp.float32),),
        in_specs=[vmem_spec()] * count,
        out_specs=(vmem_spec(),) * (tensor_count + 1),
        compiler_params=params(8),
        cost_estimate=cost(0, 4 * count * tensor_count * share * width),
    )(*back)


def head_rows(weights, buf, sems, steps, width):
    z = lax.axis_index(SEQ) >> 1
    y = lax.axis_index(SEQ) & 1
    copies = []
    for g, source in enumerate(weights):
        for i, k in enumerate(steps):
            here = pl.ds(pl.multiple_of((z ^ k) * width, width), width)
            to = pl.ds((g * len(steps) + i) * width, width)
            for turn, w in enumerate(source):
                half = w.shape[1]
                cols = pl.ds(0, half)
                if len(source) == 2:
                    cols = pl.ds(pl.multiple_of((y ^ turn) * half, half), half)
                copies.append(
                    pltpu.make_async_copy(
                        w.at[here, :], buf.at[to, cols], sems.at[len(copies)]
                    )
                )
    return copies


def side_by_side(pieces, count):
    return jnp.concatenate([p[k] for p in pieces for k in range(count)], axis=1)


def mix_first_body(*refs, groups, width, steps, later):
    pieces, flat = refs[:groups], refs[groups : groups + 6]
    tokens, mine, got, total, kept, buf, sems, later_sems = refs[groups + 6 :]
    weights = [flat[0:1], flat[1:2], flat[2:4], flat[4:6]]
    now = head_rows(weights, buf, sems, steps, width)
    then = head_rows(weights, kept, later_sems, later, width)
    for copy in now + then:
        copy.start()
    share = total.shape[0]
    at = lax.axis_index(TENSOR)
    here = pl.ds(pl.multiple_of(at * share, share), share)
    left = side_by_side(pieces, len(steps))
    known = tokens[here, :].astype(jnp.float32) + mine[...] + got[0].astype(jnp.float32)
    for copy in now:
        copy.wait()
    total[...] = known + jnp.dot(left, buf[...], preferred_element_type=jnp.float32)
    for copy in then:
        copy.wait()


def mix_first(pieces, weights, tokens, mine, got, steps, later):
    groups = len(pieces)
    count, share, width = pieces[0].shape
    depth = tokens.shape[1]
    held = (groups * count * width, depth)
    return pl.pallas_call(
        functools.partial(
            mix_first_body, groups=groups, width=width, steps=steps, later=later
        ),
        out_shape=(shape((share, depth), jnp.float32), shape(held)),
        in_specs=[vmem_spec()] * groups + [any_spec()] * 6 + [vmem_spec()] * 3,
        out_specs=(vmem_spec(), vmem_spec()),
        scratch_shapes=[
            pltpu.VMEM(held, jnp.bfloat16),
            pltpu.SemaphoreType.DMA((6 * count,)),
            pltpu.SemaphoreType.DMA((6 * count,)),
        ],
        compiler_params=params(24),
        cost_estimate=cost(
            2 * groups * share * count * width * depth,
            4 * groups * count * width * depth + 8 * share * depth,
        ),
    )(*pieces, *weights, tokens, mine, got)


def mix_last_body(*refs, groups, steps, later):
    pieces = refs[:groups]
    total, held, came, first_sums, last_sums, centroids, out, updated = refs[groups:]
    z = lax.axis_index(SEQ) >> 1
    left = side_by_side(pieces, len(later))
    known = total[...] + came[...].astype(jnp.float32)
    summed = known + jnp.dot(left, held[...], preferred_element_type=jnp.float32)
    out[...] = summed.astype(jnp.bfloat16)
    for sums, turns in ((first_sums, steps), (last_sums, later)):
        for i, k in enumerate(turns):
            head = z ^ k
            updated[head] = EMA_DECAY * centroids[head] + (1.0 - EMA_DECAY) * sums[i]


def mix_last(pieces, total, held, came, first_sums, last_sums, centroids, steps, later):
    groups = len(pieces)
    share, depth = total.shape
    return pl.pallas_call(
        functools.partial(mix_last_body, groups=groups, steps=steps, later=later),
        out_shape=(shape((share, depth)), shape(centroids.shape, jnp.float32)),
        in_specs=[vmem_spec()] * (groups + 6),
        out_specs=(vmem_spec(), vmem_spec()),
        compiler_params=params(16),
        cost_estimate=cost(2 * held.size * share, 2 * held.size + 8 * share * depth),
    )(*pieces, total, held, came, first_sums, last_sums, centroids)


def by_heads(
    tokens, norm_gain, w_qk, w_value, w_out, w_up, w_down, centroids, clusters, slots
):
    tok_rows, _ = tokens.shape
    seq_count = lax.axis_size(SEQ)
    tensor_count = lax.axis_size(TENSOR)
    heads = clusters.shape[0]
    owned = centroids.shape[1]
    width = w_qk.shape[1] // heads
    share = tok_rows // tensor_count
    swaps = [None] + [[(t, t ^ d) for t in range(tensor_count)] for d in range(1, tensor_count)]

    w_core = lax.ppermute(w_out, TENSOR, swaps[1])
    steps = [owner_pairs(k, seq_count, tensor_count) for k in range(heads)]
    swap_y = [(s, s ^ 1) for s in range(seq_count)]
    messages, own, other = [None] * heads, [None] * heads, [None] * heads
    messages[2], messages[3], normed, ids, qk_next, val_next, out_part = project_far(
        tokens, norm_gain, w_qk, w_value, clusters, w_out, heads, width
    )
    for k in (3, 2):
        own[k] = lax.ppermute(messages[k], BOTH, steps[k])
    far_here = lax.ppermute(out_part, TENSOR, swaps[2])
    messages[0], messages[1] = project_near(normed, qk_next, val_next, ids, width)
    for k in (1, 0):
        own[k] = lax.ppermute(messages[k], BOTH, steps[k])
    hidden = up(normed, held(w_up))
    mine, far, sent = down(hidden, held(w_down), share)
    got = lax.ppermute(sent, TENSOR, swaps[1])
    for k in range(heads):
        other[k] = lax.ppermute(own[k], TENSOR, swaps[1])
    picked = pick(far, got)
    came = lax.ppermute(picked, TENSOR, swaps[2])
    far_there = lax.ppermute(far_here, SEQ, swap_y)
    both_here = lax.ppermute(far_here, TENSOR, swaps[1])
    both_there = lax.ppermute(far_there, TENSOR, swaps[1])

    early, late = (heads - 1, 0), (heads - 2, 1)
    back, pieces, sums = [None] * heads, {}, {}
    *results, kv, id_rows = attend(
        own + other, heads, tok_rows, width, owned, early, True
    )
    for k, result in zip(early, results):
        back[k] = lax.ppermute(result, BOTH, turned(steps[k]))
    results = attend([kv, id_rows], heads, tok_rows, width, owned, late, False)
    for k, result in zip(late, results):
        back[k] = lax.ppermute(result, BOTH, turned(steps[k]))

    for name, turns in (("e", early), ("l", late)):
        kept, *away, sums[name] = cut([back[k] for k in turns], owned, share, tensor_count)
        pieces[name] = [kept] + [
            lax.ppermute(away[d - 1], TENSOR, swaps[d])
            for d in range(1, tensor_count)
        ]
    weights = [held(w_out), w_core, far_here, far_there, both_here, both_there]
    total, late_rows = mix_first(pieces["e"], weights, tokens, mine, got, early, late)
    mixed_rows, new_centroids = mix_last(
        pieces["l"], total, late_rows, came, sums["e"], sums["l"], centroids, early, late
    )
    return (mixed_rows, new_centroids)


def by_clusters(tokens, norm_gain, w_qk, w_value, w_out, w_up, w_down, centroids, clusters, slots):
    tok_rows = tokens.shape[0]
    seq_count = lax.axis_size(SEQ)
    tensor_count = lax.axis_size(TENSOR)
    heads_here = clusters.shape[0]
    owned_count = centroids.shape[1]
    head_width = w_qk.shape[1] // heads_here
    share_rows = tok_rows // tensor_count
    row_first = lax.axis_index(TENSOR) * share_rows
    tokens_wide = tokens.astype(jnp.float32)
    normed = (
        tokens_wide
        * lax.rsqrt(jnp.mean(tokens_wide * tokens_wide, axis=-1, keepdims=True) + NORM_EPS)
        * norm_gain
    ).astype(jnp.bfloat16)
    key_proj = jnp.dot(normed, w_qk, preferred_element_type=jnp.float32).reshape(
        tok_rows, heads_here, head_width
    )
    key_unit = (
        key_proj * lax.rsqrt(jnp.sum(key_proj * key_proj, axis=-1, keepdims=True) + NORM_EPS)
    ).astype(jnp.bfloat16)
    val_proj = (
        jnp.dot(normed, w_value, preferred_element_type=jnp.float32)
        .astype(jnp.bfloat16)
        .reshape(tok_rows, heads_here, head_width)
    )
    positions = lax.axis_index(SEQ) * tok_rows + jnp.arange(tok_rows, dtype=jnp.int32)
    pos_high = (positions // 256).astype(jnp.float32).astype(jnp.bfloat16)
    pos_low = (positions % 256).astype(jnp.float32).astype(jnp.bfloat16)
    flat_slot = clusters.T * CAP + slots.T
    head_grid = jnp.broadcast_to(jnp.arange(heads_here, dtype=jnp.int32)[None, :], flat_slot.shape)
    slot_total = CLUSTERS * CAP
    layout = (heads_here, seq_count, owned_count, CAP)
    key_buf = (
        jnp.zeros((heads_here, slot_total, head_width), jnp.bfloat16)
        .at[head_grid, flat_slot]
        .set(key_unit)
        .reshape(layout + (head_width,))
    )
    val_buf = (
        jnp.zeros((heads_here, slot_total, head_width), jnp.bfloat16)
        .at[head_grid, flat_slot]
        .set(val_proj)
        .reshape(layout + (head_width,))
    )
    high_buf = (
        jnp.full((heads_here, slot_total), 256.0, jnp.bfloat16)
        .at[head_grid, flat_slot]
        .set(jnp.broadcast_to(pos_high[:, None], flat_slot.shape))
        .reshape(layout)
    )
    low_buf = (
        jnp.zeros((heads_here, slot_total), jnp.bfloat16)
        .at[head_grid, flat_slot]
        .set(jnp.broadcast_to(pos_low[:, None], flat_slot.shape))
        .reshape(layout)
    )
    key_in = lax.all_to_all(key_buf, SEQ, split_axis=1, concat_axis=1, tiled=True)
    val_in = lax.all_to_all(val_buf, SEQ, split_axis=1, concat_axis=1, tiled=True)
    high_in = lax.all_to_all(high_buf, SEQ, split_axis=1, concat_axis=1, tiled=True)
    low_in = lax.all_to_all(low_buf, SEQ, split_axis=1, concat_axis=1, tiled=True)
    scores = (
        jnp.einsum("hskad,htkbd->hksatb", key_in, key_in, preferred_element_type=jnp.float32)
        * SCORE_SCALE
    )
    key_place = high_in.astype(jnp.float32) * 256.0 + low_in.astype(jnp.float32)
    ordered = jnp.transpose(key_place, (0, 2, 1, 3))
    causal = ordered[:, :, None, None, :, :] <= ordered[:, :, :, :, None, None]
    exponent = jnp.where(causal, jnp.exp(scores), 0.0)
    weights = (exponent / jnp.sum(exponent, axis=(4, 5), keepdims=True)).astype(jnp.bfloat16)
    mixed_out = jnp.einsum(
        "hksatb,htkbd->hskad", weights, val_in, preferred_element_type=jnp.float32
    ).astype(jnp.bfloat16)
    returned_back = lax.all_to_all(mixed_out, SEQ, split_axis=1, concat_axis=1, tiled=True)
    one_hot = (clusters[:, :, None] == jnp.arange(CLUSTERS, dtype=jnp.int32)[None, None, :]).astype(
        jnp.bfloat16
    )
    local_sums = jnp.einsum("htk,thd->hkd", one_hot, key_unit, preferred_element_type=jnp.float32)
    totals = lax.psum_scatter(
        local_sums.astype(jnp.bfloat16), SEQ, scatter_dimension=1, tiled=True
    ).astype(jnp.float32)
    new_centroids = EMA_DECAY * centroids + (1.0 - EMA_DECAY) * totals
    returned = returned_back.reshape(heads_here, slot_total, head_width)
    attended = returned[head_grid, flat_slot].reshape(tok_rows, heads_here * head_width)
    attn_part = jnp.dot(attended, w_out, preferred_element_type=jnp.float32)
    hidden = jax.nn.relu(jnp.dot(normed, w_up, preferred_element_type=jnp.float32)).astype(
        jnp.bfloat16
    )
    ffn_part = jnp.dot(hidden, w_down, preferred_element_type=jnp.float32)
    summed = lax.psum_scatter(
        rounded(attn_part + ffn_part).astype(jnp.bfloat16),
        TENSOR,
        scatter_dimension=0,
        tiled=True,
    ).astype(jnp.float32)
    own_rows = lax.dynamic_slice_in_dim(tokens_wide, row_first, share_rows, 0)
    mixed_rows = (own_rows + summed).astype(jnp.bfloat16)
    return (mixed_rows, new_centroids)


def solution(mesh):
    in_specs = (
        P(SEQ, None),
        P(),
        P(None, TENSOR),
        P(None, TENSOR),
        P(TENSOR, None),
        P(None, TENSOR),
        P(TENSOR, None),
        P(TENSOR, SEQ, None),
        P(TENSOR, SEQ),
        P(TENSOR, SEQ),
    )
    out_specs = (P((SEQ, TENSOR), None), P(TENSOR, SEQ, None))
    sizes = dict(mesh.shape)

    def local(*args):
        heads = args[8].shape[0]
        fits = (
            sizes[TENSOR] == 4
            and sizes[SEQ] == 2 * heads
            and heads & (heads - 1) == 0
            and heads == 4
        )
        if not fits:
            return by_clusters(*args)
        return by_heads(*args)

    return jax.shard_map(
        local, mesh=mesh, in_specs=in_specs, out_specs=out_specs, check_vma=False
    )
```

```python
import functools

import jax
import jax.numpy as jnp
from jax import lax
from jax.experimental import pallas as pl
from jax.experimental.pallas import tpu as pltpu
from jax.sharding import PartitionSpec as P


CLUSTERS = 256
CAP = 4

SCORE_SCALE = 2.0
EMA_DECAY = 0.9
NORM_EPS = 1e-06
SEQ, TENSOR = "seq", "tensor"
BOTH = (SEQ, TENSOR)
EXTRA = 16
MIB = 1024 * 1024


def rounded(term_value):
    return lax.optimization_barrier(term_value.astype(jnp.bfloat16)).astype(jnp.float32)


def owner_pairs(step, seq_count, tensor_count):
    pairs = []
    for s in range(seq_count):
        for t in range(tensor_count):
            z, y, c = s // 2, s % 2, t % 2
            dest_s = 2 * (z ^ step) + c
            dest_t = (t - c) + (y ^ (z & 1))
            pairs.append((s * tensor_count + t, dest_s * tensor_count + dest_t))
    return pairs


def turned(pairs):
    return [(b, a) for a, b in pairs]


def any_spec():
    return pl.BlockSpec(memory_space=pl.ANY)


def vmem_spec():
    return pl.BlockSpec(memory_space=pltpu.VMEM)


def held(value):
    return pltpu.with_memory_space_constraint(value, pltpu.HBM)


def params(mib):
    return pltpu.CompilerParams(vmem_limit_bytes=mib * MIB)


def cost(flops, moved, transcendentals=0):
    return pl.CostEstimate(
        flops=flops, bytes_accessed=moved, transcendentals=transcendentals
    )


def shape(dims, kind=jnp.bfloat16):
    return jax.ShapeDtypeStruct(dims, kind)


def unit_heads(normed, w_qk, w_value, outs, clusters, steps, width):
    z = lax.axis_index(SEQ) >> 1
    rows = normed.shape[0]
    span = 2 * width
    odd = (z & 1) == 1
    row_at = lax.broadcasted_iota(jnp.int32, (EXTRA, span), 0)
    key_proj = jnp.dot(normed[...], w_qk[...], preferred_element_type=jnp.float32)
    units = []
    for q in range(2):
        k = key_proj[:, q * width : (q + 1) * width]
        total = jnp.sum(k * k, axis=-1, keepdims=True)
        units.append((k * lax.rsqrt(total + NORM_EPS)).astype(jnp.bfloat16))
    val_proj = jnp.dot(normed[...], w_value[...], preferred_element_type=jnp.float32)
    values = [val_proj[:, q * width : (q + 1) * width].astype(jnp.bfloat16) for q in range(2)]
    for q, out in enumerate(outs):
        out[:rows, :width] = jnp.where(odd, units[1 - q], units[q])
        out[:rows, width:] = jnp.where(odd, values[1 - q], values[q])
        id_row = clusters[pl.ds(steps[q] ^ z, 1), :].astype(jnp.float32)
        tail = jnp.zeros((EXTRA, span), jnp.float32)
        for part in range(rows // span):
            piece = id_row[:, part * span : (part + 1) * span]
            tail = jnp.where(row_at == part, piece, tail)
        out[rows:, :] = tail.astype(jnp.bfloat16)


def project_far_body(
    tokens_at, gain_at, w_qk, w_value, clusters_at, w_out, *rest, width, stages, parts
):
    out_low, out_high, normed, clusters, qk_next, val_next, out_early, out_late = rest[:8]
    tokens, gain, qk_buf, val_buf, sems, token_sems, out_sems = rest[8:]
    z = lax.axis_index(SEQ) >> 1
    y = lax.axis_index(SEQ) & 1
    step = tokens.shape[0] // parts
    span = 2 * width
    slabs = [pl.ds(r * step, step) for r in range(parts)]
    slab_copies = [
        pltpu.make_async_copy(tokens_at.at[here, :], tokens.at[here, :], token_sems.at[r])
        for r, here in enumerate(slabs)
    ]

    def columns(block):
        return pl.ds(pl.multiple_of(block * span, span), span)

    first, second = columns(1 ^ (z >> 1)), columns(z >> 1)
    half = out_early.shape[1]
    out_cols = pl.ds(pl.multiple_of(y * half, half), half)
    out_copies = []
    for part, turns in ((out_early, stages[0]), (out_late, stages[1])):
        for i, k in enumerate(turns):
            here = pl.ds(pl.multiple_of((z ^ k) * width, width), width)
            out_copies.append(
                pltpu.make_async_copy(
                    w_out.at[here, out_cols],
                    part.at[pl.ds(i * width, width), :],
                    out_sems.at[len(out_copies)],
                )
            )
    copies = [
        pltpu.make_async_copy(gain_at, gain, sems.at[0]),
        pltpu.make_async_copy(w_qk.at[:, first], qk_buf, sems.at[1]),
        pltpu.make_async_copy(w_value.at[:, first], val_buf, sems.at[2]),
        pltpu.make_async_copy(clusters_at, clusters, sems.at[3]),
        pltpu.make_async_copy(w_qk.at[:, second], qk_next, sems.at[4]),
        pltpu.make_async_copy(w_value.at[:, second], val_next, sems.at[5]),
    ]
    for copy in (copies[0], *slab_copies, *copies[1:4], *out_copies, *copies[4:]):
        copy.start()
    copies[0].wait()
    for copy, here in zip(slab_copies, slabs):
        copy.wait()
        wide = tokens[here, :].astype(jnp.float32)
        mean = jnp.mean(wide * wide, axis=-1, keepdims=True)
        normed[here, :] = (wide * lax.rsqrt(mean + NORM_EPS) * gain[...]).astype(jnp.bfloat16)
    for copy in copies[1:4]:
        copy.wait()
    unit_heads(normed, qk_buf, val_buf, (out_low, out_high), clusters, (2, 3), width)
    for copy in copies[4:] + out_copies:
        copy.wait()


def project_far(tokens, gain, w_qk, w_value, clusters, w_out, width, stages, parts=4):
    rows, depth = tokens.shape
    message = shape((rows + EXTRA, 2 * width))
    pair = (depth, 2 * width)
    return pl.pallas_call(
        functools.partial(project_far_body, width=width, stages=stages, parts=parts),
        out_shape=(
            message,
            message,
            shape((rows, depth)),
            shape(clusters.shape, jnp.int32),
            shape(pair),
            shape(pair),
            shape((2 * width, w_out.shape[1] // 2)),
            shape((2 * width, w_out.shape[1] // 2)),
        ),
        in_specs=[any_spec()] * 6,
        out_specs=(vmem_spec(),) * 8,
        scratch_shapes=[
            pltpu.VMEM((rows, depth), jnp.bfloat16),
            pltpu.VMEM((1, depth), jnp.float32),
            pltpu.VMEM(pair, jnp.bfloat16),
            pltpu.VMEM(pair, jnp.bfloat16),
            pltpu.SemaphoreType.DMA((6,)),
            pltpu.SemaphoreType.DMA((parts,)),
            pltpu.SemaphoreType.DMA((4,)),
        ],
        compiler_params=params(20),
        cost_estimate=cost(8 * rows * depth * width, 2 * rows * depth + 12 * depth * width),
    )(*[held(a) for a in (tokens, gain.reshape(1, depth), w_qk, w_value, clusters, w_out)])


def project_near_body(normed, w_qk, w_value, clusters, out_low, out_high, *, width):
    unit_heads(normed, w_qk, w_value, (out_low, out_high), clusters, (0, 1), width)


def project_near(normed, w_qk, w_value, clusters, width):
    rows, depth = normed.shape
    message = shape((rows + EXTRA, 2 * width))
    return pl.pallas_call(
        functools.partial(project_near_body, width=width),
        out_shape=(message, message),
        in_specs=[vmem_spec()] * 4,
        out_specs=(vmem_spec(),) * 2,
        compiler_params=params(14),
        cost_estimate=cost(8 * rows * depth * width, 2 * rows * depth + 8 * depth * width),
    )(normed, w_qk, w_value, clusters)


def up_body(normed, w_up, hidden):
    grown = jnp.dot(normed[...], w_up[...], preferred_element_type=jnp.float32)
    hidden[...] = jnp.maximum(grown, 0.0).astype(jnp.bfloat16)


def up(normed, w_up, blocks=2):
    rows, depth = normed.shape
    units = w_up.shape[1]
    block = units // blocks
    return pl.pallas_call(
        up_body,
        grid=(blocks,),
        out_shape=shape((rows, units)),
        in_specs=[
            pl.BlockSpec((rows, depth), lambda i: (0, 0)),
            pl.BlockSpec((depth, block), lambda i: (0, i)),
        ],
        out_specs=pl.BlockSpec((rows, block), lambda i: (0, i)),
        compiler_params=params(24),
        cost_estimate=cost(2 * rows * depth * units, 2 * depth * units + 4 * rows * depth),
    )(normed, w_up)


def down_body(hidden, w_down, mine, far, away, held, *, share):
    at = lax.axis_index(TENSOR)
    held[...] = jnp.dot(hidden[...], w_down[...], preferred_element_type=jnp.float32)

    def quarter(turn):
        return held[pl.ds(pl.multiple_of((at ^ turn) * share, share), share), :]

    mine[...] = quarter(0)
    far[...] = quarter(2)
    away[0] = quarter(1).astype(jnp.bfloat16)
    away[1] = quarter(3).astype(jnp.bfloat16)


def down(hidden, w_down, share, blocks=2):
    rows, units = hidden.shape
    depth = w_down.shape[1]
    block = depth // blocks
    one = pl.BlockSpec((share, block), lambda i: (0, i))
    return pl.pallas_call(
        functools.partial(down_body, share=share),
        grid=(blocks,),
        out_shape=(
            shape((share, depth), jnp.float32),
            shape((share, depth), jnp.float32),
            shape((2, share, depth)),
        ),
        in_specs=[
            pl.BlockSpec((rows, units), lambda i: (0, 0)),
            pl.BlockSpec((units, block), lambda i: (0, i)),
        ],
        out_specs=(one, one, pl.BlockSpec((2, share, block), lambda i: (0, 0, i))),
        scratch_shapes=[pltpu.VMEM((rows, block), jnp.float32)],
        compiler_params=params(26),
        cost_estimate=cost(2 * rows * depth * units, 2 * depth * units + 6 * rows * depth),
    )(hidden, w_down)


def pick_body(far, got, sent):
    sent[...] = (far[...] + got[1].astype(jnp.float32)).astype(jnp.bfloat16)


def pick(far, got):
    return pl.pallas_call(
        pick_body,
        out_shape=shape(far.shape),
        in_specs=[vmem_spec(), vmem_spec()],
        out_specs=vmem_spec(),
        compiler_params=params(6),
        cost_estimate=cost(far.size, far.size * 8),
    )(far, got)


def block_of(b, heads):
    z = lax.axis_index(SEQ) >> 1
    core = lax.axis_index(TENSOR) % 2
    pair = z ^ (b % heads)
    return 2 * pair + (core ^ (pair & 1) ^ (b // heads))


def attend_body(*refs, heads, width, owned, steps, first):
    if first:
        own, other = refs[:heads], refs[heads : 2 * heads]
        refs = refs[2 * heads :]
        outs = refs[: len(steps)]
        kv, id_rows = refs[len(steps) : len(steps) + 2]
        query, id_cols, acc, den = refs[len(steps) + 2 :]
        rows = kv.shape[1]
        for b, source in enumerate(list(own) + list(other)):
            kv[b] = source[:rows, :]
            tile = source[rows:, :].astype(jnp.float32)
            id_row = jnp.concatenate(
                [tile[r : r + 1, :] for r in range(rows // (2 * width))], axis=1
            )
            id_rows[b] = jnp.broadcast_to(id_row, (8, rows))
    else:
        kv, id_rows = refs[:2]
        outs = refs[2 : 2 + len(steps)]
        query, id_cols, acc, den = refs[2 + len(steps) :]
        rows = kv.shape[1]

    count = 2 * heads
    cluster_col = lax.broadcasted_iota(jnp.int32, (owned, rows), 0)
    wanted = jnp.concatenate(
        [cluster_col + owned * block_of(k, heads) for k in steps], axis=0
    ).astype(jnp.float32)
    sums = jnp.zeros((len(steps) * owned, width), jnp.float32)
    for b in range(count):
        one_hot = jnp.where(wanted == id_rows[b, :1, :], 1.0, 0.0).astype(jnp.bfloat16)
        sums = sums + jnp.dot(one_hot, kv[b, :, :width], preferred_element_type=jnp.float32)

    def pair(b, masked):
        score = lax.dot_general(
            query[...],
            kv[b, :, :width],
            (((1,), (1,)), ((), ())),
            preferred_element_type=jnp.float32,
        )
        weight = jnp.exp(score)
        same = jnp.concatenate([id_cols[...]] * (rows // width), axis=1) == id_rows[b, :1, :]
        if masked:
            row_at = lax.broadcasted_iota(jnp.int32, weight.shape, 0)
            col_at = lax.broadcasted_iota(jnp.int32, weight.shape, 1)
            same = jnp.logical_and(same, col_at <= row_at)
        weight = jnp.where(same, weight, 0.0)
        share = weight[:, :width]
        for part in range(1, rows // width):
            share = share + weight[:, part * width : (part + 1) * width]
        mixed = jnp.dot(
            weight.astype(jnp.bfloat16), kv[b, :, width:], preferred_element_type=jnp.float32
        )
        if masked:
            den[...] = share
            acc[...] = mixed
        else:
            den[...] += share
            acc[...] += mixed

    for at, k in enumerate(steps):
        query[...] = kv[k, :, :width] * jnp.bfloat16(SCORE_SCALE)
        for part in range(rows // width):
            here = pl.ds(part * width, width)
            id_cols[here, :] = jnp.transpose(
                jnp.broadcast_to(id_rows[k, :1, part * width : (part + 1) * width], (width, width))
            )
        pair(k, True)
        block = block_of(k, heads)

        def per_key(b, carry):
            @pl.when(block_of(b, heads) < block)
            def _():
                pair(b, False)

            return carry

        lax.fori_loop(0, count, per_key, 0)
        out = outs[at]
        whole = jnp.sum(den[...], axis=-1, keepdims=True)
        out[:rows, :] = (acc[...] / whole).astype(jnp.bfloat16)
        out[rows:, :] = sums[at * owned : (at + 1) * owned].astype(jnp.bfloat16)


def attend(inputs, heads, rows, width, owned, steps, first):
    result = shape((rows + owned, width))
    out_shape = (result,) * len(steps)
    if first:
        out_shape += (
            shape((2 * heads, rows, 2 * width)),
            shape((2 * heads, 8, rows), jnp.float32),
        )
    units = (heads * heads + heads // 2) * len(steps) // heads
    return pl.pallas_call(
        functools.partial(
            attend_body, heads=heads, width=width, owned=owned, steps=steps, first=first
        ),
        out_shape=out_shape,
        in_specs=[vmem_spec()] * len(inputs),
        out_specs=(vmem_spec(),) * len(out_shape),
        scratch_shapes=[
            pltpu.VMEM((rows, width), jnp.bfloat16),
            pltpu.VMEM((rows, width), jnp.float32),
            pltpu.VMEM((rows, width), jnp.float32),
            pltpu.VMEM((rows, width), jnp.float32),
        ],
        compiler_params=params(20),
        cost_estimate=cost(
            units * rows * rows * width * 8,
            2 * heads * rows * width * 4,
            units * rows * rows,
        ),
    )(*inputs)


def cut_body(*refs, count, share):
    back, kept, away, sums = refs[:count], refs[count], refs[count + 1 : -1], refs[-1]
    at = lax.axis_index(TENSOR)
    for k in range(count):
        for turn in range(len(away) + 1):
            here = pl.ds(pl.multiple_of((at ^ turn) * share, share), share)
            (kept if turn == 0 else away[turn - 1])[k] = back[k][here, :]
        rows = back[k].shape[0] - sums.shape[1]
        sums[k] = back[k][rows:, :].astype(jnp.float32)


def cut(back, owned, share, tensor_count):
    count, width = len(back), back[0].shape[1]
    piece = shape((count, share, width))
    return pl.pallas_call(
        functools.partial(cut_body, count=count, share=share),
        out_shape=(piece,) * tensor_count + (shape((count, owned, width), jnp.float32),),
        in_specs=[vmem_spec()] * count,
        out_specs=(vmem_spec(),) * (tensor_count + 1),
        compiler_params=params(8),
        cost_estimate=cost(0, 4 * count * tensor_count * share * width),
    )(*back)


def head_rows(weights, buf, sems, steps, width):
    z = lax.axis_index(SEQ) >> 1
    copies = []
    for g, w in enumerate(weights):
        for i, k in enumerate(steps):
            here = pl.ds(pl.multiple_of((z ^ k) * width, width), width)
            to = pl.ds((g * len(steps) + i) * width, width)
            copies.append(
                pltpu.make_async_copy(w.at[here, :], buf.at[to, :], sems.at[len(copies)])
            )
    return copies


def side_by_side(pieces, count):
    return jnp.concatenate([p[k] for p in pieces for k in range(count)], axis=1)


def products(pieces, count, near_rows, far_halves, known, put):
    y = lax.axis_index(SEQ) & 1
    half = far_halves[0].shape[1]
    near = side_by_side(pieces[:2], count)
    same, cross = side_by_side(pieces[2:3], count), side_by_side(pieces[3:4], count)
    for turn in range(2):
        cols = pl.ds(pl.multiple_of((y ^ turn) * half, half), half)
        total = known(cols)
        for left, rows in (
            (near, near_rows[:, cols]),
            (same, far_halves[turn][...]),
            (cross, far_halves[2 + turn][...]),
        ):
            total = total + jnp.dot(left, rows, preferred_element_type=jnp.float32)
        put(cols, total)


def mix_first_body(*refs, groups, width, steps, later):
    pieces, weights = refs[:groups], refs[groups : groups + 2]
    far_halves = refs[groups + 2 : groups + 6]
    tokens, mine, got, total, kept, buf, sems, later_sems = refs[groups + 6 :]
    now = head_rows(weights, buf, sems, steps, width)
    then = head_rows(weights, kept, later_sems, later, width)
    for copy in now + then:
        copy.start()
    share = total.shape[0]
    at = lax.axis_index(TENSOR)
    here = pl.ds(pl.multiple_of(at * share, share), share)
    for copy in now:
        copy.wait()

    def known(cols):
        base = tokens[here, cols].astype(jnp.float32) + mine[:, cols]
        return base + got[0, :, cols].astype(jnp.float32)

    def put(cols, value):
        total[:, cols] = value

    products(pieces, len(steps), buf, far_halves, known, put)
    for copy in then:
        copy.wait()


def mix_first(pieces, weights, far_halves, tokens, mine, got, steps, later):
    groups = len(pieces)
    count, share, width = pieces[0].shape
    depth = tokens.shape[1]
    rows = (2 * count * width, depth)
    return pl.pallas_call(
        functools.partial(
            mix_first_body, groups=groups, width=width, steps=steps, later=later
        ),
        out_shape=(shape((share, depth), jnp.float32), shape(rows)),
        in_specs=[vmem_spec()] * groups + [any_spec()] * 2 + [vmem_spec()] * 7,
        out_specs=(vmem_spec(), vmem_spec()),
        scratch_shapes=[
            pltpu.VMEM(rows, jnp.bfloat16),
            pltpu.SemaphoreType.DMA((2 * count,)),
            pltpu.SemaphoreType.DMA((2 * count,)),
        ],
        compiler_params=params(20),
        cost_estimate=cost(
            2 * groups * share * count * width * depth,
            4 * groups * count * width * depth + 8 * share * depth,
        ),
    )(*pieces, *weights, *far_halves, tokens, mine, got)


def mix_last_body(*refs, groups, steps, later):
    pieces, far_halves = refs[:groups], refs[groups : groups + 4]
    total, kept, came, first_sums, last_sums, centroids, out, updated = refs[groups + 4 :]
    z = lax.axis_index(SEQ) >> 1

    def known(cols):
        return total[:, cols] + came[:, cols].astype(jnp.float32)

    def put(cols, value):
        out[:, cols] = value.astype(jnp.bfloat16)

    products(pieces, len(later), kept, far_halves, known, put)
    for sums, turns in ((first_sums, steps), (last_sums, later)):
        for i, k in enumerate(turns):
            head = z ^ k
            updated[head] = EMA_DECAY * centroids[head] + (1.0 - EMA_DECAY) * sums[i]


def mix_last(
    pieces, far_halves, total, kept, came, first_sums, last_sums, centroids, steps, later
):
    groups = len(pieces)
    share, depth = total.shape
    return pl.pallas_call(
        functools.partial(mix_last_body, groups=groups, steps=steps, later=later),
        out_shape=(shape((share, depth)), shape(centroids.shape, jnp.float32)),
        in_specs=[vmem_spec()] * (groups + 10),
        out_specs=(vmem_spec(), vmem_spec()),
        compiler_params=params(16),
        cost_estimate=cost(4 * kept.size * share, 4 * kept.size + 8 * share * depth),
    )(*pieces, *far_halves, total, kept, came, first_sums, last_sums, centroids)


def by_heads(
    tokens, norm_gain, w_qk, w_value, w_out, w_up, w_down, centroids, clusters, slots
):
    tok_rows, _ = tokens.shape
    seq_count = lax.axis_size(SEQ)
    tensor_count = lax.axis_size(TENSOR)
    heads = clusters.shape[0]
    owned = centroids.shape[1]
    width = w_qk.shape[1] // heads
    share = tok_rows // tensor_count
    swaps = [None] + [[(t, t ^ d) for t in range(tensor_count)] for d in range(1, tensor_count)]

    w_core = lax.ppermute(w_out, TENSOR, swaps[1])
    steps = [owner_pairs(k, seq_count, tensor_count) for k in range(heads)]
    swap_y = [(s, s ^ 1) for s in range(seq_count)]
    messages, own, other = [None] * heads, [None] * heads, [None] * heads
    early, late = (heads - 1, 0), (heads - 2, 1)
    messages[2], messages[3], normed, ids, qk_next, val_next, *out_parts = project_far(
        tokens, norm_gain, w_qk, w_value, clusters, w_out, width, (early, late)
    )
    for k in (3, 2):
        own[k] = lax.ppermute(messages[k], BOTH, steps[k])
    halves = {}
    for name, part in zip("el", out_parts):
        here = lax.ppermute(part, TENSOR, swaps[2])
        there = lax.ppermute(here, SEQ, swap_y)
        halves[name] = [here, there] + [lax.ppermute(w, TENSOR, swaps[1]) for w in (here, there)]
    messages[0], messages[1] = project_near(normed, qk_next, val_next, ids, width)
    for k in (1, 0):
        own[k] = lax.ppermute(messages[k], BOTH, steps[k])
    hidden = up(normed, held(w_up))
    mine, far, sent = down(hidden, held(w_down), share)
    got = lax.ppermute(sent, TENSOR, swaps[1])
    for k in range(heads):
        other[k] = lax.ppermute(own[k], TENSOR, swaps[1])
    picked = pick(far, got)
    came = lax.ppermute(picked, TENSOR, swaps[2])
    back, pieces, sums = [None] * heads, {}, {}
    *results, kv, id_rows = attend(
        own + other, heads, tok_rows, width, owned, early, True
    )
    for k, result in zip(early, results):
        back[k] = lax.ppermute(result, BOTH, turned(steps[k]))
    results = attend([kv, id_rows], heads, tok_rows, width, owned, late, False)
    for k, result in zip(late, results):
        back[k] = lax.ppermute(result, BOTH, turned(steps[k]))

    for name, turns in (("e", early), ("l", late)):
        kept, *away, sums[name] = cut([back[k] for k in turns], owned, share, tensor_count)
        pieces[name] = [kept] + [
            lax.ppermute(away[d - 1], TENSOR, swaps[d])
            for d in range(1, tensor_count)
        ]
    total, late_rows = mix_first(
        pieces["e"], [held(w_out), w_core], halves["e"], tokens, mine, got, early, late
    )
    mixed_rows, new_centroids = mix_last(
        pieces["l"], halves["l"], total, late_rows, came, sums["e"], sums["l"],
        centroids, early, late,
    )
    return (mixed_rows, new_centroids)


def by_clusters(tokens, norm_gain, w_qk, w_value, w_out, w_up, w_down, centroids, clusters, slots):
    tok_rows = tokens.shape[0]
    seq_count = lax.axis_size(SEQ)
    tensor_count = lax.axis_size(TENSOR)
    heads_here = clusters.shape[0]
    owned_count = centroids.shape[1]
    head_width = w_qk.shape[1] // heads_here
    share_rows = tok_rows // tensor_count
    row_first = lax.axis_index(TENSOR) * share_rows
    tokens_wide = tokens.astype(jnp.float32)
    normed = (
        tokens_wide
        * lax.rsqrt(jnp.mean(tokens_wide * tokens_wide, axis=-1, keepdims=True) + NORM_EPS)
        * norm_gain
    ).astype(jnp.bfloat16)
    key_proj = jnp.dot(normed, w_qk, preferred_element_type=jnp.float32).reshape(
        tok_rows, heads_here, head_width
    )
    key_unit = (
        key_proj * lax.rsqrt(jnp.sum(key_proj * key_proj, axis=-1, keepdims=True) + NORM_EPS)
    ).astype(jnp.bfloat16)
    val_proj = (
        jnp.dot(normed, w_value, preferred_element_type=jnp.float32)
        .astype(jnp.bfloat16)
        .reshape(tok_rows, heads_here, head_width)
    )
    positions = lax.axis_index(SEQ) * tok_rows + jnp.arange(tok_rows, dtype=jnp.int32)
    pos_high = (positions // 256).astype(jnp.float32).astype(jnp.bfloat16)
    pos_low = (positions % 256).astype(jnp.float32).astype(jnp.bfloat16)
    flat_slot = clusters.T * CAP + slots.T
    head_grid = jnp.broadcast_to(jnp.arange(heads_here, dtype=jnp.int32)[None, :], flat_slot.shape)
    slot_total = CLUSTERS * CAP
    layout = (heads_here, seq_count, owned_count, CAP)
    key_buf = (
        jnp.zeros((heads_here, slot_total, head_width), jnp.bfloat16)
        .at[head_grid, flat_slot]
        .set(key_unit)
        .reshape(layout + (head_width,))
    )
    val_buf = (
        jnp.zeros((heads_here, slot_total, head_width), jnp.bfloat16)
        .at[head_grid, flat_slot]
        .set(val_proj)
        .reshape(layout + (head_width,))
    )
    high_buf = (
        jnp.full((heads_here, slot_total), 256.0, jnp.bfloat16)
        .at[head_grid, flat_slot]
        .set(jnp.broadcast_to(pos_high[:, None], flat_slot.shape))
        .reshape(layout)
    )
    low_buf = (
        jnp.zeros((heads_here, slot_total), jnp.bfloat16)
        .at[head_grid, flat_slot]
        .set(jnp.broadcast_to(pos_low[:, None], flat_slot.shape))
        .reshape(layout)
    )
    key_in = lax.all_to_all(key_buf, SEQ, split_axis=1, concat_axis=1, tiled=True)
    val_in = lax.all_to_all(val_buf, SEQ, split_axis=1, concat_axis=1, tiled=True)
    high_in = lax.all_to_all(high_buf, SEQ, split_axis=1, concat_axis=1, tiled=True)
    low_in = lax.all_to_all(low_buf, SEQ, split_axis=1, concat_axis=1, tiled=True)
    scores = (
        jnp.einsum("hskad,htkbd->hksatb", key_in, key_in, preferred_element_type=jnp.float32)
        * SCORE_SCALE
    )
    key_place = high_in.astype(jnp.float32) * 256.0 + low_in.astype(jnp.float32)
    ordered = jnp.transpose(key_place, (0, 2, 1, 3))
    causal = ordered[:, :, None, None, :, :] <= ordered[:, :, :, :, None, None]
    exponent = jnp.where(causal, jnp.exp(scores), 0.0)
    weights = (exponent / jnp.sum(exponent, axis=(4, 5), keepdims=True)).astype(jnp.bfloat16)
    mixed_out = jnp.einsum(
        "hksatb,htkbd->hskad", weights, val_in, preferred_element_type=jnp.float32
    ).astype(jnp.bfloat16)
    returned_back = lax.all_to_all(mixed_out, SEQ, split_axis=1, concat_axis=1, tiled=True)
    one_hot = (clusters[:, :, None] == jnp.arange(CLUSTERS, dtype=jnp.int32)[None, None, :]).astype(
        jnp.bfloat16
    )
    local_sums = jnp.einsum("htk,thd->hkd", one_hot, key_unit, preferred_element_type=jnp.float32)
    totals = lax.psum_scatter(
        local_sums.astype(jnp.bfloat16), SEQ, scatter_dimension=1, tiled=True
    ).astype(jnp.float32)
    new_centroids = EMA_DECAY * centroids + (1.0 - EMA_DECAY) * totals
    returned = returned_back.reshape(heads_here, slot_total, head_width)
    attended = returned[head_grid, flat_slot].reshape(tok_rows, heads_here * head_width)
    attn_part = jnp.dot(attended, w_out, preferred_element_type=jnp.float32)
    hidden = jax.nn.relu(jnp.dot(normed, w_up, preferred_element_type=jnp.float32)).astype(
        jnp.bfloat16
    )
    ffn_part = jnp.dot(hidden, w_down, preferred_element_type=jnp.float32)
    summed = lax.psum_scatter(
        rounded(attn_part + ffn_part).astype(jnp.bfloat16),
        TENSOR,
        scatter_dimension=0,
        tiled=True,
    ).astype(jnp.float32)
    own_rows = lax.dynamic_slice_in_dim(tokens_wide, row_first, share_rows, 0)
    mixed_rows = (own_rows + summed).astype(jnp.bfloat16)
    return (mixed_rows, new_centroids)


def solution(mesh):
    in_specs = (
        P(SEQ, None),
        P(),
        P(None, TENSOR),
        P(None, TENSOR),
        P(TENSOR, None),
        P(None, TENSOR),
        P(TENSOR, None),
        P(TENSOR, SEQ, None),
        P(TENSOR, SEQ),
        P(TENSOR, SEQ),
    )
    out_specs = (P((SEQ, TENSOR), None), P(TENSOR, SEQ, None))
    sizes = dict(mesh.shape)

    def local(*args):
        heads = args[8].shape[0]
        fits = (
            sizes[TENSOR] == 4
            and sizes[SEQ] == 2 * heads
            and heads & (heads - 1) == 0
            and heads == 4
        )
        if not fits:
            return by_clusters(*args)
        return by_heads(*args)

    return jax.shard_map(
        local, mesh=mesh, in_specs=in_specs, out_specs=out_specs, check_vma=False
    )
```

```python
import functools

import jax
import jax.numpy as jnp
from jax import lax
from jax.experimental import pallas as pl
from jax.experimental.pallas import tpu as pltpu
from jax.sharding import PartitionSpec as P


CLUSTERS = 256
CAP = 4

SCORE_SCALE = 2.0
EMA_DECAY = 0.9
NORM_EPS = 1e-06
SEQ, TENSOR = "seq", "tensor"
BOTH = (SEQ, TENSOR)
EXTRA = 16
MIB = 1024 * 1024


def rounded(term_value):
    return lax.optimization_barrier(term_value.astype(jnp.bfloat16)).astype(jnp.float32)


def owner_pairs(step, seq_count, tensor_count):
    pairs = []
    for s in range(seq_count):
        for t in range(tensor_count):
            z, y, c = s // 2, s % 2, t % 2
            dest_s = 2 * (z ^ step) + c
            dest_t = (t - c) + (y ^ (z & 1))
            pairs.append((s * tensor_count + t, dest_s * tensor_count + dest_t))
    return pairs


def turned(pairs):
    return [(b, a) for a, b in pairs]


def any_spec():
    return pl.BlockSpec(memory_space=pl.ANY)


def vmem_spec():
    return pl.BlockSpec(memory_space=pltpu.VMEM)


def held(value):
    return pltpu.with_memory_space_constraint(value, pltpu.HBM)


def params(mib):
    return pltpu.CompilerParams(vmem_limit_bytes=mib * MIB)


def cost(flops, moved, transcendentals=0):
    return pl.CostEstimate(
        flops=flops, bytes_accessed=moved, transcendentals=transcendentals
    )


def shape(dims, kind=jnp.bfloat16):
    return jax.ShapeDtypeStruct(dims, kind)


def unit_heads(normed, w_qk, w_value, outs, clusters, steps, width):
    z = lax.axis_index(SEQ) >> 1
    rows = normed.shape[0]
    span = 2 * width
    odd = (z & 1) == 1
    row_at = lax.broadcasted_iota(jnp.int32, (EXTRA, span), 0)
    key_proj = jnp.dot(normed[...], w_qk[...], preferred_element_type=jnp.float32)
    units = []
    for q in range(2):
        k = key_proj[:, q * width : (q + 1) * width]
        total = jnp.sum(k * k, axis=-1, keepdims=True)
        units.append((k * lax.rsqrt(total + NORM_EPS)).astype(jnp.bfloat16))
    val_proj = jnp.dot(normed[...], w_value[...], preferred_element_type=jnp.float32)
    values = [val_proj[:, q * width : (q + 1) * width].astype(jnp.bfloat16) for q in range(2)]
    for q, out in enumerate(outs):
        out[:rows, :width] = jnp.where(odd, units[1 - q], units[q])
        out[:rows, width:] = jnp.where(odd, values[1 - q], values[q])
        id_row = clusters[pl.ds(steps[q] ^ z, 1), :].astype(jnp.float32)
        tail = jnp.zeros((EXTRA, span), jnp.float32)
        for part in range(rows // span):
            piece = id_row[:, part * span : (part + 1) * span]
            tail = jnp.where(row_at == part, piece, tail)
        out[rows:, :] = tail.astype(jnp.bfloat16)


def project_far_body(
    tokens_at, gain_at, w_qk, w_value, clusters_at, w_out, *rest, width, stages, parts
):
    out_low, out_high, normed, clusters, qk_next, val_next, out_early, out_late = rest[:8]
    tokens, gain, qk_buf, val_buf, sems, token_sems, out_sems = rest[8:]
    z = lax.axis_index(SEQ) >> 1
    y = lax.axis_index(SEQ) & 1
    step = tokens.shape[0] // parts
    span = 2 * width
    slabs = [pl.ds(r * step, step) for r in range(parts)]
    slab_copies = [
        pltpu.make_async_copy(tokens_at.at[here, :], tokens.at[here, :], token_sems.at[r])
        for r, here in enumerate(slabs)
    ]

    def columns(block):
        return pl.ds(pl.multiple_of(block * span, span), span)

    first, second = columns(1 ^ (z >> 1)), columns(z >> 1)
    half = out_early.shape[1]
    out_cols = pl.ds(pl.multiple_of(y * half, half), half)
    out_copies = []
    for part, turns in ((out_early, stages[0]), (out_late, stages[1])):
        for i, k in enumerate(turns):
            here = pl.ds(pl.multiple_of((z ^ k) * width, width), width)
            out_copies.append(
                pltpu.make_async_copy(
                    w_out.at[here, out_cols],
                    part.at[pl.ds(i * width, width), :],
                    out_sems.at[len(out_copies)],
                )
            )
    copies = [
        pltpu.make_async_copy(gain_at, gain, sems.at[0]),
        pltpu.make_async_copy(w_qk.at[:, first], qk_buf, sems.at[1]),
        pltpu.make_async_copy(w_value.at[:, first], val_buf, sems.at[2]),
        pltpu.make_async_copy(clusters_at, clusters, sems.at[3]),
        pltpu.make_async_copy(w_qk.at[:, second], qk_next, sems.at[4]),
        pltpu.make_async_copy(w_value.at[:, second], val_next, sems.at[5]),
    ]
    for copy in (copies[0], *slab_copies, *copies[1:4], *out_copies, *copies[4:]):
        copy.start()
    copies[0].wait()
    for copy, here in zip(slab_copies, slabs):
        copy.wait()
        wide = tokens[here, :].astype(jnp.float32)
        mean = jnp.mean(wide * wide, axis=-1, keepdims=True)
        normed[here, :] = (wide * lax.rsqrt(mean + NORM_EPS) * gain[...]).astype(jnp.bfloat16)
    for copy in copies[1:4]:
        copy.wait()
    unit_heads(normed, qk_buf, val_buf, (out_low, out_high), clusters, (2, 3), width)
    for copy in copies[4:] + out_copies:
        copy.wait()


def project_far(tokens, gain, w_qk, w_value, clusters, w_out, width, stages, parts=4):
    rows, depth = tokens.shape
    message = shape((rows + EXTRA, 2 * width))
    pair = (depth, 2 * width)
    return pl.pallas_call(
        functools.partial(project_far_body, width=width, stages=stages, parts=parts),
        out_shape=(
            message,
            message,
            shape((rows, depth)),
            shape(clusters.shape, jnp.int32),
            shape(pair),
            shape(pair),
            shape((2 * width, w_out.shape[1] // 2)),
            shape((2 * width, w_out.shape[1] // 2)),
        ),
        in_specs=[any_spec()] * 6,
        out_specs=(vmem_spec(),) * 8,
        scratch_shapes=[
            pltpu.VMEM((rows, depth), jnp.bfloat16),
            pltpu.VMEM((1, depth), jnp.float32),
            pltpu.VMEM(pair, jnp.bfloat16),
            pltpu.VMEM(pair, jnp.bfloat16),
            pltpu.SemaphoreType.DMA((6,)),
            pltpu.SemaphoreType.DMA((parts,)),
            pltpu.SemaphoreType.DMA((4,)),
        ],
        compiler_params=params(20),
        cost_estimate=cost(8 * rows * depth * width, 2 * rows * depth + 12 * depth * width),
    )(*[held(a) for a in (tokens, gain.reshape(1, depth), w_qk, w_value, clusters, w_out)])


def project_near_body(normed, w_qk, w_value, clusters, out_low, out_high, *, width):
    unit_heads(normed, w_qk, w_value, (out_low, out_high), clusters, (0, 1), width)


def project_near(normed, w_qk, w_value, clusters, width):
    rows, depth = normed.shape
    message = shape((rows + EXTRA, 2 * width))
    return pl.pallas_call(
        functools.partial(project_near_body, width=width),
        out_shape=(message, message),
        in_specs=[vmem_spec()] * 4,
        out_specs=(vmem_spec(),) * 2,
        compiler_params=params(14),
        cost_estimate=cost(8 * rows * depth * width, 2 * rows * depth + 8 * depth * width),
    )(normed, w_qk, w_value, clusters)


def up_body(normed, w_up, hidden):
    grown = jnp.dot(normed[...], w_up[...], preferred_element_type=jnp.float32)
    hidden[...] = jnp.maximum(grown, 0.0).astype(jnp.bfloat16)


def up(normed, w_up, blocks=2):
    rows, depth = normed.shape
    units = w_up.shape[1]
    block = units // blocks
    return pl.pallas_call(
        up_body,
        grid=(blocks,),
        out_shape=shape((rows, units)),
        in_specs=[
            pl.BlockSpec((rows, depth), lambda i: (0, 0)),
            pl.BlockSpec((depth, block), lambda i: (0, i)),
        ],
        out_specs=pl.BlockSpec((rows, block), lambda i: (0, i)),
        compiler_params=params(24),
        cost_estimate=cost(2 * rows * depth * units, 2 * depth * units + 4 * rows * depth),
    )(normed, w_up)


def down_body(hidden, w_down, *rest, share):
    mine, far, away, held_rows = rest[-4:]
    at = lax.axis_index(TENSOR)
    held_rows[...] = jnp.dot(hidden[...], w_down[...], preferred_element_type=jnp.float32)

    def quarter(turn):
        return held_rows[pl.ds(pl.multiple_of((at ^ turn) * share, share), share), :]

    mine[...] = quarter(0)
    far[...] = quarter(2)
    away[0] = quarter(1).astype(jnp.bfloat16)
    away[1] = quarter(3).astype(jnp.bfloat16)


def down(hidden, w_down, share, part, earlier=(), parts=2, blocks=2):
    rows, units = hidden.shape
    depth = w_down.shape[1]
    block = depth // (parts * blocks)
    one = pl.BlockSpec((share, block), lambda i: (0, part * blocks + i))
    return pl.pallas_call(
        functools.partial(down_body, share=share),
        grid=(blocks,),
        out_shape=(
            shape((share, depth), jnp.float32),
            shape((share, depth), jnp.float32),
            shape((2, share, depth)),
        ),
        in_specs=[
            pl.BlockSpec((rows, units), lambda i: (0, 0)),
            pl.BlockSpec((units, block), lambda i: (0, part * blocks + i)),
        ]
        + [any_spec()] * len(earlier),
        out_specs=(
            one,
            one,
            pl.BlockSpec((2, share, block), lambda i: (0, 0, part * blocks + i)),
        ),
        scratch_shapes=[pltpu.VMEM((rows, block), jnp.float32)],
        input_output_aliases={2 + i: i for i in range(len(earlier))},
        compiler_params=params(20),
        cost_estimate=cost(
            2 * rows * depth * units // parts, (2 * depth * units + 6 * rows * depth) // parts
        ),
    )(hidden, w_down, *earlier)


def pick_body(far, got, sent):
    sent[...] = (far[...] + got[1].astype(jnp.float32)).astype(jnp.bfloat16)


def pick(far, got):
    return pl.pallas_call(
        pick_body,
        out_shape=shape(far.shape),
        in_specs=[vmem_spec(), vmem_spec()],
        out_specs=vmem_spec(),
        compiler_params=params(6),
        cost_estimate=cost(far.size, far.size * 8),
    )(far, got)


def block_of(b, heads):
    z = lax.axis_index(SEQ) >> 1
    core = lax.axis_index(TENSOR) % 2
    pair = z ^ (b % heads)
    return 2 * pair + (core ^ (pair & 1) ^ (b // heads))


def attend_body(*refs, heads, width, owned, steps, first):
    if first:
        own, other = refs[:heads], refs[heads : 2 * heads]
        refs = refs[2 * heads :]
        outs = refs[: len(steps)]
        kv, id_rows = refs[len(steps) : len(steps) + 2]
        query, id_cols, acc, den = refs[len(steps) + 2 :]
        rows = kv.shape[1]
        for b, source in enumerate(list(own) + list(other)):
            kv[b] = source[:rows, :]
            tile = source[rows:, :].astype(jnp.float32)
            id_row = jnp.concatenate(
                [tile[r : r + 1, :] for r in range(rows // (2 * width))], axis=1
            )
            id_rows[b] = jnp.broadcast_to(id_row, (8, rows))
    else:
        kv, id_rows = refs[:2]
        outs = refs[2 : 2 + len(steps)]
        query, id_cols, acc, den = refs[2 + len(steps) :]
        rows = kv.shape[1]

    count = 2 * heads
    cluster_col = lax.broadcasted_iota(jnp.int32, (owned, rows), 0)
    wanted = jnp.concatenate(
        [cluster_col + owned * block_of(k, heads) for k in steps], axis=0
    ).astype(jnp.float32)
    sums = jnp.zeros((len(steps) * owned, width), jnp.float32)
    for b in range(count):
        one_hot = jnp.where(wanted == id_rows[b, :1, :], 1.0, 0.0).astype(jnp.bfloat16)
        sums = sums + jnp.dot(one_hot, kv[b, :, :width], preferred_element_type=jnp.float32)

    def pair(b, masked):
        score = lax.dot_general(
            query[...],
            kv[b, :, :width],
            (((1,), (1,)), ((), ())),
            preferred_element_type=jnp.float32,
        )
        weight = jnp.exp(score)
        same = jnp.concatenate([id_cols[...]] * (rows // width), axis=1) == id_rows[b, :1, :]
        if masked:
            row_at = lax.broadcasted_iota(jnp.int32, weight.shape, 0)
            col_at = lax.broadcasted_iota(jnp.int32, weight.shape, 1)
            same = jnp.logical_and(same, col_at <= row_at)
        weight = jnp.where(same, weight, 0.0)
        share = weight[:, :width]
        for part in range(1, rows // width):
            share = share + weight[:, part * width : (part + 1) * width]
        mixed = jnp.dot(
            weight.astype(jnp.bfloat16), kv[b, :, width:], preferred_element_type=jnp.float32
        )
        if masked:
            den[...] = share
            acc[...] = mixed
        else:
            den[...] += share
            acc[...] += mixed

    for at, k in enumerate(steps):
        query[...] = kv[k, :, :width] * jnp.bfloat16(SCORE_SCALE)
        for part in range(rows // width):
            here = pl.ds(part * width, width)
            id_cols[here, :] = jnp.transpose(
                jnp.broadcast_to(id_rows[k, :1, part * width : (part + 1) * width], (width, width))
            )
        pair(k, True)
        block = block_of(k, heads)

        def per_key(b, carry):
            @pl.when(block_of(b, heads) < block)
            def _():
                pair(b, False)

            return carry

        lax.fori_loop(0, count, per_key, 0)
        out = outs[at]
        whole = jnp.sum(den[...], axis=-1, keepdims=True)
        out[:rows, :] = (acc[...] / whole).astype(jnp.bfloat16)
        out[rows:, :] = sums[at * owned : (at + 1) * owned].astype(jnp.bfloat16)


def attend(inputs, heads, rows, width, owned, steps, first):
    result = shape((rows + owned, width))
    out_shape = (result,) * len(steps)
    if first:
        out_shape += (
            shape((2 * heads, rows, 2 * width)),
            shape((2 * heads, 8, rows), jnp.float32),
        )
    units = (heads * heads + heads // 2) * len(steps) // heads
    return pl.pallas_call(
        functools.partial(
            attend_body, heads=heads, width=width, owned=owned, steps=steps, first=first
        ),
        out_shape=out_shape,
        in_specs=[vmem_spec()] * len(inputs),
        out_specs=(vmem_spec(),) * len(out_shape),
        scratch_shapes=[
            pltpu.VMEM((rows, width), jnp.bfloat16),
            pltpu.VMEM((rows, width), jnp.float32),
            pltpu.VMEM((rows, width), jnp.float32),
            pltpu.VMEM((rows, width), jnp.float32),
        ],
        compiler_params=params(20),
        cost_estimate=cost(
            units * rows * rows * width * 8,
            2 * heads * rows * width * 4,
            units * rows * rows,
        ),
    )(*inputs)


def cut_body(*refs, count, share):
    back, kept, away, sums = refs[:count], refs[count], refs[count + 1 : -1], refs[-1]
    at = lax.axis_index(TENSOR)
    for k in range(count):
        for turn in range(len(away) + 1):
            here = pl.ds(pl.multiple_of((at ^ turn) * share, share), share)
            (kept if turn == 0 else away[turn - 1])[k] = back[k][here, :]
        rows = back[k].shape[0] - sums.shape[1]
        sums[k] = back[k][rows:, :].astype(jnp.float32)


def cut(back, owned, share, tensor_count):
    count, width = len(back), back[0].shape[1]
    piece = shape((count, share, width))
    return pl.pallas_call(
        functools.partial(cut_body, count=count, share=share),
        out_shape=(piece,) * tensor_count + (shape((count, owned, width), jnp.float32),),
        in_specs=[vmem_spec()] * count,
        out_specs=(vmem_spec(),) * (tensor_count + 1),
        compiler_params=params(8),
        cost_estimate=cost(0, 4 * count * tensor_count * share * width),
    )(*back)


def head_rows(weights, buf, sems, steps, width):
    z = lax.axis_index(SEQ) >> 1
    copies = []
    for g, w in enumerate(weights):
        for i, k in enumerate(steps):
            here = pl.ds(pl.multiple_of((z ^ k) * width, width), width)
            to = pl.ds((g * len(steps) + i) * width, width)
            copies.append(
                pltpu.make_async_copy(w.at[here, :], buf.at[to, :], sems.at[len(copies)])
            )
    return copies


def side_by_side(pieces, count):
    return jnp.concatenate([p[k] for p in pieces for k in range(count)], axis=1)


def products(pieces, count, near_rows, far_halves, known, put):
    y = lax.axis_index(SEQ) & 1
    half = far_halves[0].shape[1]
    near = side_by_side(pieces[:2], count)
    same, cross = side_by_side(pieces[2:3], count), side_by_side(pieces[3:4], count)
    for turn in range(2):
        cols = pl.ds(pl.multiple_of((y ^ turn) * half, half), half)
        total = known(cols)
        for left, rows in (
            (near, near_rows[:, cols]),
            (same, far_halves[turn][...]),
            (cross, far_halves[2 + turn][...]),
        ):
            total = total + jnp.dot(left, rows, preferred_element_type=jnp.float32)
        put(cols, total)


def mix_first_body(*refs, groups, width, steps, later):
    pieces, weights = refs[:groups], refs[groups : groups + 2]
    far_halves = refs[groups + 2 : groups + 6]
    tokens, mine, got, total, kept, buf, sems, later_sems = refs[groups + 6 :]
    now = head_rows(weights, buf, sems, steps, width)
    then = head_rows(weights, kept, later_sems, later, width)
    for copy in now + then:
        copy.start()
    share = total.shape[0]
    at = lax.axis_index(TENSOR)
    here = pl.ds(pl.multiple_of(at * share, share), share)
    for copy in now:
        copy.wait()

    def known(cols):
        base = tokens[here, cols].astype(jnp.float32) + mine[:, cols]
        return base + got[0, :, cols].astype(jnp.float32)

    def put(cols, value):
        total[:, cols] = value

    products(pieces, len(steps), buf, far_halves, known, put)
    for copy in then:
        copy.wait()


def mix_first(pieces, weights, far_halves, tokens, mine, got, steps, later):
    groups = len(pieces)
    count, share, width = pieces[0].shape
    depth = tokens.shape[1]
    rows = (2 * count * width, depth)
    return pl.pallas_call(
        functools.partial(
            mix_first_body, groups=groups, width=width, steps=steps, later=later
        ),
        out_shape=(shape((share, depth), jnp.float32), shape(rows)),
        in_specs=[vmem_spec()] * groups + [any_spec()] * 2 + [vmem_spec()] * 7,
        out_specs=(vmem_spec(), vmem_spec()),
        scratch_shapes=[
            pltpu.VMEM(rows, jnp.bfloat16),
            pltpu.SemaphoreType.DMA((2 * count,)),
            pltpu.SemaphoreType.DMA((2 * count,)),
        ],
        compiler_params=params(20),
        cost_estimate=cost(
            2 * groups * share * count * width * depth,
            4 * groups * count * width * depth + 8 * share * depth,
        ),
    )(*pieces, *weights, *far_halves, tokens, mine, got)


def mix_last_body(*refs, groups, steps, later):
    pieces, far_halves = refs[:groups], refs[groups : groups + 4]
    total, kept, came, first_sums, last_sums, centroids, out, updated = refs[groups + 4 :]
    z = lax.axis_index(SEQ) >> 1

    def known(cols):
        return total[:, cols] + came[:, cols].astype(jnp.float32)

    def put(cols, value):
        out[:, cols] = value.astype(jnp.bfloat16)

    products(pieces, len(later), kept, far_halves, known, put)
    for sums, turns in ((first_sums, steps), (last_sums, later)):
        for i, k in enumerate(turns):
            head = z ^ k
            updated[head] = EMA_DECAY * centroids[head] + (1.0 - EMA_DECAY) * sums[i]


def mix_last(
    pieces, far_halves, total, kept, came, first_sums, last_sums, centroids, steps, later
):
    groups = len(pieces)
    share, depth = total.shape
    return pl.pallas_call(
        functools.partial(mix_last_body, groups=groups, steps=steps, later=later),
        out_shape=(shape((share, depth)), shape(centroids.shape, jnp.float32)),
        in_specs=[vmem_spec()] * (groups + 10),
        out_specs=(vmem_spec(), vmem_spec()),
        compiler_params=params(16),
        cost_estimate=cost(4 * kept.size * share, 4 * kept.size + 8 * share * depth),
    )(*pieces, *far_halves, total, kept, came, first_sums, last_sums, centroids)


def by_heads(
    tokens, norm_gain, w_qk, w_value, w_out, w_up, w_down, centroids, clusters, slots
):
    tok_rows, _ = tokens.shape
    seq_count = lax.axis_size(SEQ)
    tensor_count = lax.axis_size(TENSOR)
    heads = clusters.shape[0]
    owned = centroids.shape[1]
    width = w_qk.shape[1] // heads
    share = tok_rows // tensor_count
    swaps = [None] + [[(t, t ^ d) for t in range(tensor_count)] for d in range(1, tensor_count)]

    w_core = lax.ppermute(w_out, TENSOR, swaps[1])
    steps = [owner_pairs(k, seq_count, tensor_count) for k in range(heads)]
    swap_y = [(s, s ^ 1) for s in range(seq_count)]
    messages, own, other = [None] * heads, [None] * heads, [None] * heads
    early, late = (heads - 1, 0), (heads - 2, 1)
    messages[2], messages[3], normed, ids, qk_next, val_next, *out_parts = project_far(
        tokens, norm_gain, w_qk, w_value, clusters, w_out, width, (early, late)
    )
    for k in (3, 2):
        own[k] = lax.ppermute(messages[k], BOTH, steps[k])
    halves = {}
    for name, part in zip("el", out_parts):
        here = lax.ppermute(part, TENSOR, swaps[2])
        there = lax.ppermute(here, SEQ, swap_y)
        halves[name] = [here, there] + [lax.ppermute(w, TENSOR, swaps[1]) for w in (here, there)]
    messages[0], messages[1] = project_near(normed, qk_next, val_next, ids, width)
    for k in (1, 0):
        own[k] = lax.ppermute(messages[k], BOTH, steps[k])
    hidden = up(normed, held(w_up))
    half_down = down(hidden, held(w_down), share, 0)
    mine, far, sent = down(hidden, held(w_down), share, 1, half_down)
    got = lax.ppermute(sent, TENSOR, swaps[1])
    for k in range(heads):
        other[k] = lax.ppermute(own[k], TENSOR, swaps[1])
    picked = pick(far, got)
    came = lax.ppermute(picked, TENSOR, swaps[2])
    back, pieces, sums = [None] * heads, {}, {}
    *results, kv, id_rows = attend(
        own + other, heads, tok_rows, width, owned, early, True
    )
    for k, result in zip(early, results):
        back[k] = lax.ppermute(result, BOTH, turned(steps[k]))
    results = attend([kv, id_rows], heads, tok_rows, width, owned, late, False)
    for k, result in zip(late, results):
        back[k] = lax.ppermute(result, BOTH, turned(steps[k]))

    for name, turns in (("e", early), ("l", late)):
        kept, *away, sums[name] = cut([back[k] for k in turns], owned, share, tensor_count)
        pieces[name] = [kept] + [
            lax.ppermute(away[d - 1], TENSOR, swaps[d])
            for d in range(1, tensor_count)
        ]
    total, late_rows = mix_first(
        pieces["e"], [held(w_out), w_core], halves["e"], tokens, mine, got, early, late
    )
    mixed_rows, new_centroids = mix_last(
        pieces["l"], halves["l"], total, late_rows, came, sums["e"], sums["l"],
        centroids, early, late,
    )
    return (mixed_rows, new_centroids)


def by_clusters(tokens, norm_gain, w_qk, w_value, w_out, w_up, w_down, centroids, clusters, slots):
    tok_rows = tokens.shape[0]
    seq_count = lax.axis_size(SEQ)
    tensor_count = lax.axis_size(TENSOR)
    heads_here = clusters.shape[0]
    owned_count = centroids.shape[1]
    head_width = w_qk.shape[1] // heads_here
    share_rows = tok_rows // tensor_count
    row_first = lax.axis_index(TENSOR) * share_rows
    tokens_wide = tokens.astype(jnp.float32)
    normed = (
        tokens_wide
        * lax.rsqrt(jnp.mean(tokens_wide * tokens_wide, axis=-1, keepdims=True) + NORM_EPS)
        * norm_gain
    ).astype(jnp.bfloat16)
    key_proj = jnp.dot(normed, w_qk, preferred_element_type=jnp.float32).reshape(
        tok_rows, heads_here, head_width
    )
    key_unit = (
        key_proj * lax.rsqrt(jnp.sum(key_proj * key_proj, axis=-1, keepdims=True) + NORM_EPS)
    ).astype(jnp.bfloat16)
    val_proj = (
        jnp.dot(normed, w_value, preferred_element_type=jnp.float32)
        .astype(jnp.bfloat16)
        .reshape(tok_rows, heads_here, head_width)
    )
    positions = lax.axis_index(SEQ) * tok_rows + jnp.arange(tok_rows, dtype=jnp.int32)
    pos_high = (positions // 256).astype(jnp.float32).astype(jnp.bfloat16)
    pos_low = (positions % 256).astype(jnp.float32).astype(jnp.bfloat16)
    flat_slot = clusters.T * CAP + slots.T
    head_grid = jnp.broadcast_to(jnp.arange(heads_here, dtype=jnp.int32)[None, :], flat_slot.shape)
    slot_total = CLUSTERS * CAP
    layout = (heads_here, seq_count, owned_count, CAP)
    key_buf = (
        jnp.zeros((heads_here, slot_total, head_width), jnp.bfloat16)
        .at[head_grid, flat_slot]
        .set(key_unit)
        .reshape(layout + (head_width,))
    )
    val_buf = (
        jnp.zeros((heads_here, slot_total, head_width), jnp.bfloat16)
        .at[head_grid, flat_slot]
        .set(val_proj)
        .reshape(layout + (head_width,))
    )
    high_buf = (
        jnp.full((heads_here, slot_total), 256.0, jnp.bfloat16)
        .at[head_grid, flat_slot]
        .set(jnp.broadcast_to(pos_high[:, None], flat_slot.shape))
        .reshape(layout)
    )
    low_buf = (
        jnp.zeros((heads_here, slot_total), jnp.bfloat16)
        .at[head_grid, flat_slot]
        .set(jnp.broadcast_to(pos_low[:, None], flat_slot.shape))
        .reshape(layout)
    )
    key_in = lax.all_to_all(key_buf, SEQ, split_axis=1, concat_axis=1, tiled=True)
    val_in = lax.all_to_all(val_buf, SEQ, split_axis=1, concat_axis=1, tiled=True)
    high_in = lax.all_to_all(high_buf, SEQ, split_axis=1, concat_axis=1, tiled=True)
    low_in = lax.all_to_all(low_buf, SEQ, split_axis=1, concat_axis=1, tiled=True)
    scores = (
        jnp.einsum("hskad,htkbd->hksatb", key_in, key_in, preferred_element_type=jnp.float32)
        * SCORE_SCALE
    )
    key_place = high_in.astype(jnp.float32) * 256.0 + low_in.astype(jnp.float32)
    ordered = jnp.transpose(key_place, (0, 2, 1, 3))
    causal = ordered[:, :, None, None, :, :] <= ordered[:, :, :, :, None, None]
    exponent = jnp.where(causal, jnp.exp(scores), 0.0)
    weights = (exponent / jnp.sum(exponent, axis=(4, 5), keepdims=True)).astype(jnp.bfloat16)
    mixed_out = jnp.einsum(
        "hksatb,htkbd->hskad", weights, val_in, preferred_element_type=jnp.float32
    ).astype(jnp.bfloat16)
    returned_back = lax.all_to_all(mixed_out, SEQ, split_axis=1, concat_axis=1, tiled=True)
    one_hot = (clusters[:, :, None] == jnp.arange(CLUSTERS, dtype=jnp.int32)[None, None, :]).astype(
        jnp.bfloat16
    )
    local_sums = jnp.einsum("htk,thd->hkd", one_hot, key_unit, preferred_element_type=jnp.float32)
    totals = lax.psum_scatter(
        local_sums.astype(jnp.bfloat16), SEQ, scatter_dimension=1, tiled=True
    ).astype(jnp.float32)
    new_centroids = EMA_DECAY * centroids + (1.0 - EMA_DECAY) * totals
    returned = returned_back.reshape(heads_here, slot_total, head_width)
    attended = returned[head_grid, flat_slot].reshape(tok_rows, heads_here * head_width)
    attn_part = jnp.dot(attended, w_out, preferred_element_type=jnp.float32)
    hidden = jax.nn.relu(jnp.dot(normed, w_up, preferred_element_type=jnp.float32)).astype(
        jnp.bfloat16
    )
    ffn_part = jnp.dot(hidden, w_down, preferred_element_type=jnp.float32)
    summed = lax.psum_scatter(
        rounded(attn_part + ffn_part).astype(jnp.bfloat16),
        TENSOR,
        scatter_dimension=0,
        tiled=True,
    ).astype(jnp.float32)
    own_rows = lax.dynamic_slice_in_dim(tokens_wide, row_first, share_rows, 0)
    mixed_rows = (own_rows + summed).astype(jnp.bfloat16)
    return (mixed_rows, new_centroids)


def solution(mesh):
    in_specs = (
        P(SEQ, None),
        P(),
        P(None, TENSOR),
        P(None, TENSOR),
        P(TENSOR, None),
        P(None, TENSOR),
        P(TENSOR, None),
        P(TENSOR, SEQ, None),
        P(TENSOR, SEQ),
        P(TENSOR, SEQ),
    )
    out_specs = (P((SEQ, TENSOR), None), P(TENSOR, SEQ, None))
    sizes = dict(mesh.shape)

    def local(*args):
        heads = args[8].shape[0]
        fits = (
            sizes[TENSOR] == 4
            and sizes[SEQ] == 2 * heads
            and heads & (heads - 1) == 0
            and heads == 4
        )
        if not fits:
            return by_clusters(*args)
        return by_heads(*args)

    return jax.shard_map(
        local, mesh=mesh, in_specs=in_specs, out_specs=out_specs, check_vma=False
    )
```

```python
import functools

import jax
import jax.numpy as jnp
from jax import lax
from jax.experimental import pallas as pl
from jax.experimental.pallas import tpu as pltpu
from jax.sharding import PartitionSpec as P


CLUSTERS = 256
CAP = 4

SCORE_SCALE = 2.0
EMA_DECAY = 0.9
NORM_EPS = 1e-06
SEQ, TENSOR = "seq", "tensor"
BOTH = (SEQ, TENSOR)
EXTRA = 16
MIB = 1024 * 1024


def rounded(term_value):
    return lax.optimization_barrier(term_value.astype(jnp.bfloat16)).astype(jnp.float32)


def owner_pairs(step, seq_count, tensor_count):
    pairs = []
    for s in range(seq_count):
        for t in range(tensor_count):
            z, y, c = s // 2, s % 2, t % 2
            dest_s = 2 * (z ^ step) + c
            dest_t = (t - c) + (y ^ (z & 1))
            pairs.append((s * tensor_count + t, dest_s * tensor_count + dest_t))
    return pairs


def turned(pairs):
    return [(b, a) for a, b in pairs]


def any_spec():
    return pl.BlockSpec(memory_space=pl.ANY)


def vmem_spec():
    return pl.BlockSpec(memory_space=pltpu.VMEM)


def held(value):
    return pltpu.with_memory_space_constraint(value, pltpu.HBM)


def params(mib):
    return pltpu.CompilerParams(vmem_limit_bytes=mib * MIB)


def cost(flops, moved, transcendentals=0):
    return pl.CostEstimate(
        flops=flops, bytes_accessed=moved, transcendentals=transcendentals
    )


def shape(dims, kind=jnp.bfloat16):
    return jax.ShapeDtypeStruct(dims, kind)


def unit_heads(normed, w_qk, w_value, outs, clusters, steps, width):
    z = lax.axis_index(SEQ) >> 1
    rows = normed.shape[0]
    span = 2 * width
    odd = (z & 1) == 1
    row_at = lax.broadcasted_iota(jnp.int32, (EXTRA, span), 0)
    key_proj = jnp.dot(normed[...], w_qk[...], preferred_element_type=jnp.float32)
    units = []
    for q in range(2):
        k = key_proj[:, q * width : (q + 1) * width]
        total = jnp.sum(k * k, axis=-1, keepdims=True)
        units.append((k * lax.rsqrt(total + NORM_EPS)).astype(jnp.bfloat16))
    val_proj = jnp.dot(normed[...], w_value[...], preferred_element_type=jnp.float32)
    values = [val_proj[:, q * width : (q + 1) * width].astype(jnp.bfloat16) for q in range(2)]
    for q, out in enumerate(outs):
        out[:rows, :width] = jnp.where(odd, units[1 - q], units[q])
        out[:rows, width:] = jnp.where(odd, values[1 - q], values[q])
        id_row = clusters[pl.ds(steps[q] ^ z, 1), :].astype(jnp.float32)
        tail = jnp.zeros((EXTRA, span), jnp.float32)
        for part in range(rows // span):
            piece = id_row[:, part * span : (part + 1) * span]
            tail = jnp.where(row_at == part, piece, tail)
        out[rows:, :] = tail.astype(jnp.bfloat16)


def project_far_body(
    tokens_at, gain_at, w_qk, w_value, clusters_at, w_out, *rest, width, stages, parts
):
    out_low, out_high, normed, clusters, qk_next, val_next, out_early, out_late, out_rest = rest[:9]
    tokens, gain, qk_buf, val_buf, sems, token_sems, out_sems = rest[9:]
    z = lax.axis_index(SEQ) >> 1
    y = lax.axis_index(SEQ) & 1
    step = tokens.shape[0] // parts
    span = 2 * width
    slabs = [pl.ds(r * step, step) for r in range(parts)]
    slab_copies = [
        pltpu.make_async_copy(tokens_at.at[here, :], tokens.at[here, :], token_sems.at[r])
        for r, here in enumerate(slabs)
    ]

    def columns(block):
        return pl.ds(pl.multiple_of(block * span, span), span)

    first, second = columns(1 ^ (z >> 1)), columns(z >> 1)
    half = out_early.shape[1]
    out_copies = []
    for part, turns, at in (
        (out_early, stages[0], y),
        (out_late, stages[1], y),
        (out_rest, stages[1], 1 - y),
    ):
        out_cols = pl.ds(pl.multiple_of(at * half, half), half)
        for i, k in enumerate(turns):
            here = pl.ds(pl.multiple_of((z ^ k) * width, width), width)
            out_copies.append(
                pltpu.make_async_copy(
                    w_out.at[here, out_cols],
                    part.at[pl.ds(i * width, width), :],
                    out_sems.at[len(out_copies)],
                )
            )
    copies = [
        pltpu.make_async_copy(gain_at, gain, sems.at[0]),
        pltpu.make_async_copy(w_qk.at[:, first], qk_buf, sems.at[1]),
        pltpu.make_async_copy(w_value.at[:, first], val_buf, sems.at[2]),
        pltpu.make_async_copy(clusters_at, clusters, sems.at[3]),
        pltpu.make_async_copy(w_qk.at[:, second], qk_next, sems.at[4]),
        pltpu.make_async_copy(w_value.at[:, second], val_next, sems.at[5]),
    ]
    for copy in (copies[0], *slab_copies, *copies[1:4], *out_copies, *copies[4:]):
        copy.start()
    copies[0].wait()
    for copy, here in zip(slab_copies, slabs):
        copy.wait()
        wide = tokens[here, :].astype(jnp.float32)
        mean = jnp.mean(wide * wide, axis=-1, keepdims=True)
        normed[here, :] = (wide * lax.rsqrt(mean + NORM_EPS) * gain[...]).astype(jnp.bfloat16)
    for copy in copies[1:4]:
        copy.wait()
    unit_heads(normed, qk_buf, val_buf, (out_low, out_high), clusters, (2, 3), width)
    for copy in copies[4:] + out_copies:
        copy.wait()


def project_far(tokens, gain, w_qk, w_value, clusters, w_out, width, stages, parts=4):
    rows, depth = tokens.shape
    message = shape((rows + EXTRA, 2 * width))
    pair = (depth, 2 * width)
    return pl.pallas_call(
        functools.partial(project_far_body, width=width, stages=stages, parts=parts),
        out_shape=(
            message,
            message,
            shape((rows, depth)),
            shape(clusters.shape, jnp.int32),
            shape(pair),
            shape(pair),
            shape((2 * width, w_out.shape[1] // 2)),
            shape((2 * width, w_out.shape[1] // 2)),
            shape((2 * width, w_out.shape[1] // 2)),
        ),
        in_specs=[any_spec()] * 6,
        out_specs=(vmem_spec(),) * 9,
        scratch_shapes=[
            pltpu.VMEM((rows, depth), jnp.bfloat16),
            pltpu.VMEM((1, depth), jnp.float32),
            pltpu.VMEM(pair, jnp.bfloat16),
            pltpu.VMEM(pair, jnp.bfloat16),
            pltpu.SemaphoreType.DMA((6,)),
            pltpu.SemaphoreType.DMA((parts,)),
            pltpu.SemaphoreType.DMA((6,)),
        ],
        compiler_params=params(20),
        cost_estimate=cost(8 * rows * depth * width, 2 * rows * depth + 12 * depth * width),
    )(*[held(a) for a in (tokens, gain.reshape(1, depth), w_qk, w_value, clusters, w_out)])


def project_near_body(
    normed, w_qk, w_value, clusters, w_up, out_low, out_high, next_half, sem, *, width
):
    copy = pltpu.make_async_copy(w_up.at[:, pl.ds(0, next_half.shape[1])], next_half, sem)
    copy.start()
    unit_heads(normed, w_qk, w_value, (out_low, out_high), clusters, (0, 1), width)
    copy.wait()


def project_near(normed, w_qk, w_value, clusters, w_up, width):
    rows, depth = normed.shape
    message = shape((rows + EXTRA, 2 * width))
    return pl.pallas_call(
        functools.partial(project_near_body, width=width),
        out_shape=(message, message, shape((depth, w_up.shape[1] // 2))),
        in_specs=[vmem_spec()] * 4 + [any_spec()],
        out_specs=(vmem_spec(),) * 3,
        scratch_shapes=[pltpu.SemaphoreType.DMA],
        compiler_params=params(16),
        cost_estimate=cost(8 * rows * depth * width, 2 * rows * depth + 8 * depth * width),
    )(normed, w_qk, w_value, clusters, held(w_up))


def up_body(normed, first, w_up, w_down, hidden, next_half, second, sems):
    half = first.shape[1]
    copies = (
        pltpu.make_async_copy(w_up.at[:, pl.ds(half, half)], second, sems.at[0]),
        pltpu.make_async_copy(
            w_down.at[:, pl.ds(0, next_half.shape[1])], next_half, sems.at[1]
        ),
    )
    for copy in copies:
        copy.start()
    for at, weights in enumerate((first, second)):
        if at == 1:
            copies[0].wait()
        grown = jnp.dot(normed[...], weights[...], preferred_element_type=jnp.float32)
        hidden[:, at * half : (at + 1) * half] = jnp.maximum(grown, 0.0).astype(jnp.bfloat16)
    copies[1].wait()


def up(normed, first, w_up, w_down):
    rows, depth = normed.shape
    units = w_up.shape[1]
    return pl.pallas_call(
        up_body,
        out_shape=(shape((rows, units)), shape((units, w_down.shape[1] // 2))),
        in_specs=[vmem_spec(), vmem_spec(), any_spec(), any_spec()],
        out_specs=(vmem_spec(), vmem_spec()),
        scratch_shapes=[
            pltpu.VMEM((depth, units // 2), jnp.bfloat16),
            pltpu.SemaphoreType.DMA((2,)),
        ],
        compiler_params=params(24),
        cost_estimate=cost(2 * rows * depth * units, 2 * depth * units + 4 * rows * depth),
    )(normed, first, held(w_up), held(w_down))


def down_body(hidden, first, w_down, mine, far, away, second, held_rows, sem, *, share):
    at = lax.axis_index(TENSOR)
    half = first.shape[1]
    copy = pltpu.make_async_copy(w_down.at[:, pl.ds(half, half)], second, sem)
    copy.start()

    def quarter(turn):
        return held_rows[pl.ds(pl.multiple_of((at ^ turn) * share, share), share), :]

    for part, weights in enumerate((first, second)):
        if part == 1:
            copy.wait()
        cols = slice(part * half, (part + 1) * half)
        held_rows[...] = jnp.dot(
            hidden[...], weights[...], preferred_element_type=jnp.float32
        )
        mine[:, cols] = quarter(0)
        far[:, cols] = quarter(2)
        away[0, :, cols] = quarter(1).astype(jnp.bfloat16)
        away[1, :, cols] = quarter(3).astype(jnp.bfloat16)


def down(hidden, first, w_down, share):
    rows, units = hidden.shape
    depth = w_down.shape[1]
    return pl.pallas_call(
        functools.partial(down_body, share=share),
        out_shape=(
            shape((share, depth), jnp.float32),
            shape((share, depth), jnp.float32),
            shape((2, share, depth)),
        ),
        in_specs=[vmem_spec(), vmem_spec(), any_spec()],
        out_specs=(vmem_spec(),) * 3,
        scratch_shapes=[
            pltpu.VMEM((units, depth // 2), jnp.bfloat16),
            pltpu.VMEM((rows, depth // 2), jnp.float32),
            pltpu.SemaphoreType.DMA,
        ],
        compiler_params=params(24),
        cost_estimate=cost(2 * rows * depth * units, 2 * depth * units + 6 * rows * depth),
    )(hidden, first, held(w_down))


def pick_body(far, got, sent):
    sent[...] = (far[...] + got[1].astype(jnp.float32)).astype(jnp.bfloat16)


def pick(far, got):
    return pl.pallas_call(
        pick_body,
        out_shape=shape(far.shape),
        in_specs=[vmem_spec(), vmem_spec()],
        out_specs=vmem_spec(),
        compiler_params=params(6),
        cost_estimate=cost(far.size, far.size * 8),
    )(far, got)


def block_of(b, heads):
    z = lax.axis_index(SEQ) >> 1
    core = lax.axis_index(TENSOR) % 2
    pair = z ^ (b % heads)
    return 2 * pair + (core ^ (pair & 1) ^ (b // heads))


def attend_body(*refs, heads, width, owned, steps, first):
    if first:
        own, other = refs[:heads], refs[heads : 2 * heads]
        refs = refs[2 * heads :]
        outs = refs[: len(steps)]
        kv, id_rows = refs[len(steps) : len(steps) + 2]
        query, id_cols, acc, den = refs[len(steps) + 2 :]
        rows = kv.shape[1]
        for b, source in enumerate(list(own) + list(other)):
            kv[b] = source[:rows, :]
            tile = source[rows:, :].astype(jnp.float32)
            id_row = jnp.concatenate(
                [tile[r : r + 1, :] for r in range(rows // (2 * width))], axis=1
            )
            id_rows[b] = jnp.broadcast_to(id_row, (8, rows))
    else:
        kv, id_rows = refs[:2]
        outs = refs[2 : 2 + len(steps)]
        query, id_cols, acc, den = refs[2 + len(steps) :]
        rows = kv.shape[1]

    count = 2 * heads
    cluster_col = lax.broadcasted_iota(jnp.int32, (owned, rows), 0)
    wanted = jnp.concatenate(
        [cluster_col + owned * block_of(k, heads) for k in steps], axis=0
    ).astype(jnp.float32)
    sums = jnp.zeros((len(steps) * owned, width), jnp.float32)
    for b in range(count):
        one_hot = jnp.where(wanted == id_rows[b, :1, :], 1.0, 0.0).astype(jnp.bfloat16)
        sums = sums + jnp.dot(one_hot, kv[b, :, :width], preferred_element_type=jnp.float32)

    def pair(b, masked):
        score = lax.dot_general(
            query[...],
            kv[b, :, :width],
            (((1,), (1,)), ((), ())),
            preferred_element_type=jnp.float32,
        )
        weight = jnp.exp(score)
        same = jnp.concatenate([id_cols[...]] * (rows // width), axis=1) == id_rows[b, :1, :]
        if masked:
            row_at = lax.broadcasted_iota(jnp.int32, weight.shape, 0)
            col_at = lax.broadcasted_iota(jnp.int32, weight.shape, 1)
            same = jnp.logical_and(same, col_at <= row_at)
        weight = jnp.where(same, weight, 0.0)
        share = weight[:, :width]
        for part in range(1, rows // width):
            share = share + weight[:, part * width : (part + 1) * width]
        mixed = jnp.dot(
            weight.astype(jnp.bfloat16), kv[b, :, width:], preferred_element_type=jnp.float32
        )
        if masked:
            den[...] = share
            acc[...] = mixed
        else:
            den[...] += share
            acc[...] += mixed

    for at, k in enumerate(steps):
        query[...] = kv[k, :, :width] * jnp.bfloat16(SCORE_SCALE)
        for part in range(rows // width):
            here = pl.ds(part * width, width)
            id_cols[here, :] = jnp.transpose(
                jnp.broadcast_to(id_rows[k, :1, part * width : (part + 1) * width], (width, width))
            )
        pair(k, True)
        block = block_of(k, heads)

        def per_key(b, carry):
            @pl.when(block_of(b, heads) < block)
            def _():
                pair(b, False)

            return carry

        lax.fori_loop(0, count, per_key, 0)
        out = outs[at]
        whole = jnp.sum(den[...], axis=-1, keepdims=True)
        out[:rows, :] = (acc[...] / whole).astype(jnp.bfloat16)
        out[rows:, :] = sums[at * owned : (at + 1) * owned].astype(jnp.bfloat16)


def attend(inputs, heads, rows, width, owned, steps, first):
    result = shape((rows + owned, width))
    out_shape = (result,) * len(steps)
    if first:
        out_shape += (
            shape((2 * heads, rows, 2 * width)),
            shape((2 * heads, 8, rows), jnp.float32),
        )
    units = (heads * heads + heads // 2) * len(steps) // heads
    return pl.pallas_call(
        functools.partial(
            attend_body, heads=heads, width=width, owned=owned, steps=steps, first=first
        ),
        out_shape=out_shape,
        in_specs=[vmem_spec()] * len(inputs),
        out_specs=(vmem_spec(),) * len(out_shape),
        scratch_shapes=[
            pltpu.VMEM((rows, width), jnp.bfloat16),
            pltpu.VMEM((rows, width), jnp.float32),
            pltpu.VMEM((rows, width), jnp.float32),
            pltpu.VMEM((rows, width), jnp.float32),
        ],
        compiler_params=params(20),
        cost_estimate=cost(
            units * rows * rows * width * 8,
            2 * heads * rows * width * 4,
            units * rows * rows,
        ),
    )(*inputs)


def cut_body(*refs, count, share):
    back, kept, away, sums = refs[:count], refs[count], refs[count + 1 : -1], refs[-1]
    at = lax.axis_index(TENSOR)
    for k in range(count):
        for turn in range(len(away) + 1):
            here = pl.ds(pl.multiple_of((at ^ turn) * share, share), share)
            (kept if turn == 0 else away[turn - 1])[k] = back[k][here, :]
        rows = back[k].shape[0] - sums.shape[1]
        sums[k] = back[k][rows:, :].astype(jnp.float32)


def cut(back, owned, share, tensor_count):
    count, width = len(back), back[0].shape[1]
    piece = shape((count, share, width))
    return pl.pallas_call(
        functools.partial(cut_body, count=count, share=share),
        out_shape=(piece,) * tensor_count + (shape((count, owned, width), jnp.float32),),
        in_specs=[vmem_spec()] * count,
        out_specs=(vmem_spec(),) * (tensor_count + 1),
        compiler_params=params(8),
        cost_estimate=cost(0, 4 * count * tensor_count * share * width),
    )(*back)


def head_rows(weights, buf, sems, steps, width):
    z = lax.axis_index(SEQ) >> 1
    copies = []
    for g, w in enumerate(weights):
        for i, k in enumerate(steps):
            here = pl.ds(pl.multiple_of((z ^ k) * width, width), width)
            to = pl.ds((g * len(steps) + i) * width, width)
            copies.append(
                pltpu.make_async_copy(w.at[here, :], buf.at[to, :], sems.at[len(copies)])
            )
    return copies


def side_by_side(pieces, count):
    return jnp.concatenate([p[k] for p in pieces for k in range(count)], axis=1)


def products(pieces, count, near_rows, far_halves, known, put):
    y = lax.axis_index(SEQ) & 1
    half = far_halves[0].shape[1]
    near = side_by_side(pieces[:2], count)
    same, cross = side_by_side(pieces[2:3], count), side_by_side(pieces[3:4], count)
    for turn in range(2):
        cols = pl.ds(pl.multiple_of((y ^ turn) * half, half), half)
        total = known(cols)
        for left, rows in (
            (near, near_rows[:, cols]),
            (same, far_halves[turn][...]),
            (cross, far_halves[2 + turn][...]),
        ):
            total = total + jnp.dot(left, rows, preferred_element_type=jnp.float32)
        put(cols, total)


def mix_first_body(*refs, groups, width, steps, later):
    pieces, weights = refs[:groups], refs[groups : groups + 2]
    far_halves = refs[groups + 2 : groups + 6]
    tokens, mine, got, total, kept, buf, sems, later_sems = refs[groups + 6 :]
    now = head_rows(weights, buf, sems, steps, width)
    then = head_rows(weights, kept, later_sems, later, width)
    for copy in now + then:
        copy.start()
    share = total.shape[0]
    at = lax.axis_index(TENSOR)
    here = pl.ds(pl.multiple_of(at * share, share), share)
    for copy in now:
        copy.wait()

    def known(cols):
        base = tokens[here, cols].astype(jnp.float32) + mine[:, cols]
        return base + got[0, :, cols].astype(jnp.float32)

    def put(cols, value):
        total[:, cols] = value

    products(pieces, len(steps), buf, far_halves, known, put)
    for copy in then:
        copy.wait()


def mix_first(pieces, weights, far_halves, tokens, mine, got, steps, later):
    groups = len(pieces)
    count, share, width = pieces[0].shape
    depth = tokens.shape[1]
    rows = (2 * count * width, depth)
    return pl.pallas_call(
        functools.partial(
            mix_first_body, groups=groups, width=width, steps=steps, later=later
        ),
        out_shape=(shape((share, depth), jnp.float32), shape(rows)),
        in_specs=[vmem_spec()] * groups + [any_spec()] * 2 + [vmem_spec()] * 7,
        out_specs=(vmem_spec(), vmem_spec()),
        scratch_shapes=[
            pltpu.VMEM(rows, jnp.bfloat16),
            pltpu.SemaphoreType.DMA((2 * count,)),
            pltpu.SemaphoreType.DMA((2 * count,)),
        ],
        compiler_params=params(20),
        cost_estimate=cost(
            2 * groups * share * count * width * depth,
            4 * groups * count * width * depth + 8 * share * depth,
        ),
    )(*pieces, *weights, *far_halves, tokens, mine, got)


def mix_last_body(*refs, groups, steps, later):
    pieces, far_halves = refs[:groups], refs[groups : groups + 4]
    total, kept, came, first_sums, last_sums, centroids, out, updated = refs[groups + 4 :]
    z = lax.axis_index(SEQ) >> 1

    def known(cols):
        return total[:, cols] + came[:, cols].astype(jnp.float32)

    def put(cols, value):
        out[:, cols] = value.astype(jnp.bfloat16)

    products(pieces, len(later), kept, far_halves, known, put)
    for sums, turns in ((first_sums, steps), (last_sums, later)):
        for i, k in enumerate(turns):
            head = z ^ k
            updated[head] = EMA_DECAY * centroids[head] + (1.0 - EMA_DECAY) * sums[i]


def mix_last(
    pieces, far_halves, total, kept, came, first_sums, last_sums, centroids, steps, later
):
    groups = len(pieces)
    share, depth = total.shape
    return pl.pallas_call(
        functools.partial(mix_last_body, groups=groups, steps=steps, later=later),
        out_shape=(shape((share, depth)), shape(centroids.shape, jnp.float32)),
        in_specs=[vmem_spec()] * (groups + 10),
        out_specs=(vmem_spec(), vmem_spec()),
        compiler_params=params(16),
        cost_estimate=cost(4 * kept.size * share, 4 * kept.size + 8 * share * depth),
    )(*pieces, *far_halves, total, kept, came, first_sums, last_sums, centroids)


def by_heads(
    tokens, norm_gain, w_qk, w_value, w_out, w_up, w_down, centroids, clusters, slots
):
    tok_rows, _ = tokens.shape
    seq_count = lax.axis_size(SEQ)
    tensor_count = lax.axis_size(TENSOR)
    heads = clusters.shape[0]
    owned = centroids.shape[1]
    width = w_qk.shape[1] // heads
    share = tok_rows // tensor_count
    swaps = [None] + [[(t, t ^ d) for t in range(tensor_count)] for d in range(1, tensor_count)]

    w_core = lax.ppermute(w_out, TENSOR, swaps[1])
    steps = [owner_pairs(k, seq_count, tensor_count) for k in range(heads)]
    swap_y = [(s, s ^ 1) for s in range(seq_count)]
    messages, own, other = [None] * heads, [None] * heads, [None] * heads
    early, late = (heads - 1, 0), (heads - 2, 1)
    messages[2], messages[3], normed, ids, qk_next, val_next, *out_parts = project_far(
        tokens, norm_gain, w_qk, w_value, clusters, w_out, width, (early, late)
    )
    for k in (3, 2):
        own[k] = lax.ppermute(messages[k], BOTH, steps[k])
    halves = {}
    for name in "el":
        here = lax.ppermute(out_parts.pop(0), TENSOR, swaps[2])
        if name == "e":
            there = lax.ppermute(here, SEQ, swap_y)
        else:
            there = lax.ppermute(out_parts.pop(0), TENSOR, swaps[2])
        halves[name] = [here, there] + [lax.ppermute(w, TENSOR, swaps[1]) for w in (here, there)]
    messages[0], messages[1], up_first = project_near(normed, qk_next, val_next, ids, w_up, width)
    for k in (1, 0):
        own[k] = lax.ppermute(messages[k], BOTH, steps[k])
    hidden, down_first = up(normed, up_first, w_up, w_down)
    mine, far, sent = down(hidden, down_first, w_down, share)
    got = lax.ppermute(sent, TENSOR, swaps[1])
    for k in range(heads):
        other[k] = lax.ppermute(own[k], TENSOR, swaps[1])
    picked = pick(far, got)
    came = lax.ppermute(picked, TENSOR, swaps[2])
    back, pieces, sums = [None] * heads, {}, {}
    *results, kv, id_rows = attend(
        own + other, heads, tok_rows, width, owned, early, True
    )
    for k, result in zip(early, results):
        back[k] = lax.ppermute(result, BOTH, turned(steps[k]))
    results = attend([kv, id_rows], heads, tok_rows, width, owned, late, False)
    for k, result in zip(late, results):
        back[k] = lax.ppermute(result, BOTH, turned(steps[k]))

    for name, turns in (("e", early), ("l", late)):
        kept, *away, sums[name] = cut([back[k] for k in turns], owned, share, tensor_count)
        pieces[name] = [kept] + [
            lax.ppermute(away[d - 1], TENSOR, swaps[d])
            for d in range(1, tensor_count)
        ]
    total, late_rows = mix_first(
        pieces["e"], [held(w_out), w_core], halves["e"], tokens, mine, got, early, late
    )
    mixed_rows, new_centroids = mix_last(
        pieces["l"], halves["l"], total, late_rows, came, sums["e"], sums["l"],
        centroids, early, late,
    )
    return (mixed_rows, new_centroids)


def by_clusters(tokens, norm_gain, w_qk, w_value, w_out, w_up, w_down, centroids, clusters, slots):
    tok_rows = tokens.shape[0]
    seq_count = lax.axis_size(SEQ)
    tensor_count = lax.axis_size(TENSOR)
    heads_here = clusters.shape[0]
    owned_count = centroids.shape[1]
    head_width = w_qk.shape[1] // heads_here
    share_rows = tok_rows // tensor_count
    row_first = lax.axis_index(TENSOR) * share_rows
    tokens_wide = tokens.astype(jnp.float32)
    normed = (
        tokens_wide
        * lax.rsqrt(jnp.mean(tokens_wide * tokens_wide, axis=-1, keepdims=True) + NORM_EPS)
        * norm_gain
    ).astype(jnp.bfloat16)
    key_proj = jnp.dot(normed, w_qk, preferred_element_type=jnp.float32).reshape(
        tok_rows, heads_here, head_width
    )
    key_unit = (
        key_proj * lax.rsqrt(jnp.sum(key_proj * key_proj, axis=-1, keepdims=True) + NORM_EPS)
    ).astype(jnp.bfloat16)
    val_proj = (
        jnp.dot(normed, w_value, preferred_element_type=jnp.float32)
        .astype(jnp.bfloat16)
        .reshape(tok_rows, heads_here, head_width)
    )
    positions = lax.axis_index(SEQ) * tok_rows + jnp.arange(tok_rows, dtype=jnp.int32)
    pos_high = (positions // 256).astype(jnp.float32).astype(jnp.bfloat16)
    pos_low = (positions % 256).astype(jnp.float32).astype(jnp.bfloat16)
    flat_slot = clusters.T * CAP + slots.T
    head_grid = jnp.broadcast_to(jnp.arange(heads_here, dtype=jnp.int32)[None, :], flat_slot.shape)
    slot_total = CLUSTERS * CAP
    layout = (heads_here, seq_count, owned_count, CAP)
    key_buf = (
        jnp.zeros((heads_here, slot_total, head_width), jnp.bfloat16)
        .at[head_grid, flat_slot]
        .set(key_unit)
        .reshape(layout + (head_width,))
    )
    val_buf = (
        jnp.zeros((heads_here, slot_total, head_width), jnp.bfloat16)
        .at[head_grid, flat_slot]
        .set(val_proj)
        .reshape(layout + (head_width,))
    )
    high_buf = (
        jnp.full((heads_here, slot_total), 256.0, jnp.bfloat16)
        .at[head_grid, flat_slot]
        .set(jnp.broadcast_to(pos_high[:, None], flat_slot.shape))
        .reshape(layout)
    )
    low_buf = (
        jnp.zeros((heads_here, slot_total), jnp.bfloat16)
        .at[head_grid, flat_slot]
        .set(jnp.broadcast_to(pos_low[:, None], flat_slot.shape))
        .reshape(layout)
    )
    key_in = lax.all_to_all(key_buf, SEQ, split_axis=1, concat_axis=1, tiled=True)
    val_in = lax.all_to_all(val_buf, SEQ, split_axis=1, concat_axis=1, tiled=True)
    high_in = lax.all_to_all(high_buf, SEQ, split_axis=1, concat_axis=1, tiled=True)
    low_in = lax.all_to_all(low_buf, SEQ, split_axis=1, concat_axis=1, tiled=True)
    scores = (
        jnp.einsum("hskad,htkbd->hksatb", key_in, key_in, preferred_element_type=jnp.float32)
        * SCORE_SCALE
    )
    key_place = high_in.astype(jnp.float32) * 256.0 + low_in.astype(jnp.float32)
    ordered = jnp.transpose(key_place, (0, 2, 1, 3))
    causal = ordered[:, :, None, None, :, :] <= ordered[:, :, :, :, None, None]
    exponent = jnp.where(causal, jnp.exp(scores), 0.0)
    weights = (exponent / jnp.sum(exponent, axis=(4, 5), keepdims=True)).astype(jnp.bfloat16)
    mixed_out = jnp.einsum(
        "hksatb,htkbd->hskad", weights, val_in, preferred_element_type=jnp.float32
    ).astype(jnp.bfloat16)
    returned_back = lax.all_to_all(mixed_out, SEQ, split_axis=1, concat_axis=1, tiled=True)
    one_hot = (clusters[:, :, None] == jnp.arange(CLUSTERS, dtype=jnp.int32)[None, None, :]).astype(
        jnp.bfloat16
    )
    local_sums = jnp.einsum("htk,thd->hkd", one_hot, key_unit, preferred_element_type=jnp.float32)
    totals = lax.psum_scatter(
        local_sums.astype(jnp.bfloat16), SEQ, scatter_dimension=1, tiled=True
    ).astype(jnp.float32)
    new_centroids = EMA_DECAY * centroids + (1.0 - EMA_DECAY) * totals
    returned = returned_back.reshape(heads_here, slot_total, head_width)
    attended = returned[head_grid, flat_slot].reshape(tok_rows, heads_here * head_width)
    attn_part = jnp.dot(attended, w_out, preferred_element_type=jnp.float32)
    hidden = jax.nn.relu(jnp.dot(normed, w_up, preferred_element_type=jnp.float32)).astype(
        jnp.bfloat16
    )
    ffn_part = jnp.dot(hidden, w_down, preferred_element_type=jnp.float32)
    summed = lax.psum_scatter(
        rounded(attn_part + ffn_part).astype(jnp.bfloat16),
        TENSOR,
        scatter_dimension=0,
        tiled=True,
    ).astype(jnp.float32)
    own_rows = lax.dynamic_slice_in_dim(tokens_wide, row_first, share_rows, 0)
    mixed_rows = (own_rows + summed).astype(jnp.bfloat16)
    return (mixed_rows, new_centroids)


def solution(mesh):
    in_specs = (
        P(SEQ, None),
        P(),
        P(None, TENSOR),
        P(None, TENSOR),
        P(TENSOR, None),
        P(None, TENSOR),
        P(TENSOR, None),
        P(TENSOR, SEQ, None),
        P(TENSOR, SEQ),
        P(TENSOR, SEQ),
    )
    out_specs = (P((SEQ, TENSOR), None), P(TENSOR, SEQ, None))
    sizes = dict(mesh.shape)

    def local(*args):
        heads = args[8].shape[0]
        fits = (
            sizes[TENSOR] == 4
            and sizes[SEQ] == 2 * heads
            and heads & (heads - 1) == 0
            and heads == 4
        )
        if not fits:
            return by_clusters(*args)
        return by_heads(*args)

    return jax.shard_map(
        local, mesh=mesh, in_specs=in_specs, out_specs=out_specs, check_vma=False
    )
```

```python
import functools

import jax
import jax.numpy as jnp
from jax import lax
from jax.experimental import pallas as pl
from jax.experimental.pallas import tpu as pltpu
from jax.sharding import PartitionSpec as P


CLUSTERS = 256
CAP = 4

SCORE_SCALE = 2.0
EMA_DECAY = 0.9
NORM_EPS = 1e-06
SEQ, TENSOR = "seq", "tensor"
BOTH = (SEQ, TENSOR)
EXTRA = 16
SLABS = 4
MIB = 1024 * 1024


def rounded(term_value):
    return lax.optimization_barrier(term_value.astype(jnp.bfloat16)).astype(jnp.float32)


def owner_pairs(step, seq_count, tensor_count):
    pairs = []
    for s in range(seq_count):
        for t in range(tensor_count):
            z, y, c = s // 2, s % 2, t % 2
            dest_s = 2 * (z ^ step) + c
            dest_t = (t - c) + (y ^ (z & 1))
            pairs.append((s * tensor_count + t, dest_s * tensor_count + dest_t))
    return pairs


def turned(pairs):
    return [(b, a) for a, b in pairs]


def any_spec():
    return pl.BlockSpec(memory_space=pl.ANY)


def vmem_spec():
    return pl.BlockSpec(memory_space=pltpu.VMEM)


def held(value):
    return pltpu.with_memory_space_constraint(value, pltpu.HBM)


def params(mib):
    return pltpu.CompilerParams(vmem_limit_bytes=mib * MIB)


def cost(flops, moved, transcendentals=0):
    return pl.CostEstimate(
        flops=flops, bytes_accessed=moved, transcendentals=transcendentals
    )


def shape(dims, kind=jnp.bfloat16):
    return jax.ShapeDtypeStruct(dims, kind)


def slab_copies(source, column, buf, sems):
    step = buf.shape[0] // SLABS
    cols = pl.ds(column, buf.shape[1])
    return [
        pltpu.make_async_copy(
            source.at[pl.ds(r * step, step), cols],
            buf.at[pl.ds(r * step, step), :],
            sems.at[r],
        )
        for r in range(SLABS)
    ]


def unit_heads(normed, w_qk, w_value, outs, clusters, steps, width):
    z = lax.axis_index(SEQ) >> 1
    rows = normed.shape[0]
    span = 2 * width
    odd = (z & 1) == 1
    row_at = lax.broadcasted_iota(jnp.int32, (EXTRA, span), 0)
    key_proj = jnp.dot(normed[...], w_qk[...], preferred_element_type=jnp.float32)
    units = []
    for q in range(2):
        k = key_proj[:, q * width : (q + 1) * width]
        total = jnp.sum(k * k, axis=-1, keepdims=True)
        units.append((k * lax.rsqrt(total + NORM_EPS)).astype(jnp.bfloat16))
    val_proj = jnp.dot(normed[...], w_value[...], preferred_element_type=jnp.float32)
    values = [val_proj[:, q * width : (q + 1) * width].astype(jnp.bfloat16) for q in range(2)]
    for q, out in enumerate(outs):
        out[:rows, :width] = jnp.where(odd, units[1 - q], units[q])
        out[:rows, width:] = jnp.where(odd, values[1 - q], values[q])
        id_row = clusters[pl.ds(steps[q] ^ z, 1), :].astype(jnp.float32)
        tail = jnp.zeros((EXTRA, span), jnp.float32)
        for part in range(rows // span):
            piece = id_row[:, part * span : (part + 1) * span]
            tail = jnp.where(row_at == part, piece, tail)
        out[rows:, :] = tail.astype(jnp.bfloat16)


def project_far_body(
    tokens_at, gain_at, w_qk, w_value, clusters_at, w_out, *rest, width, stages, parts
):
    out_low, out_high, normed, clusters, qk_next, val_next, out_early, out_late, out_rest = rest[:9]
    tokens, gain, qk_buf, val_buf, sems, token_sems, out_sems = rest[9:]
    z = lax.axis_index(SEQ) >> 1
    y = lax.axis_index(SEQ) & 1
    step = tokens.shape[0] // parts
    span = 2 * width
    slabs = [pl.ds(r * step, step) for r in range(parts)]
    slab_copies = [
        pltpu.make_async_copy(tokens_at.at[here, :], tokens.at[here, :], token_sems.at[r])
        for r, here in enumerate(slabs)
    ]

    def columns(block):
        return pl.ds(pl.multiple_of(block * span, span), span)

    first, second = columns(1 ^ (z >> 1)), columns(z >> 1)
    half = out_early.shape[1]
    out_copies = []
    for part, turns, at in (
        (out_early, stages[0], y),
        (out_late, stages[1], y),
        (out_rest, stages[1], 1 - y),
    ):
        out_cols = pl.ds(pl.multiple_of(at * half, half), half)
        for i, k in enumerate(turns):
            here = pl.ds(pl.multiple_of((z ^ k) * width, width), width)
            out_copies.append(
                pltpu.make_async_copy(
                    w_out.at[here, out_cols],
                    part.at[pl.ds(i * width, width), :],
                    out_sems.at[len(out_copies)],
                )
            )
    copies = [
        pltpu.make_async_copy(gain_at, gain, sems.at[0]),
        pltpu.make_async_copy(w_qk.at[:, first], qk_buf, sems.at[1]),
        pltpu.make_async_copy(w_value.at[:, first], val_buf, sems.at[2]),
        pltpu.make_async_copy(clusters_at, clusters, sems.at[3]),
        pltpu.make_async_copy(w_qk.at[:, second], qk_next, sems.at[4]),
        pltpu.make_async_copy(w_value.at[:, second], val_next, sems.at[5]),
    ]
    for copy in (copies[0], *slab_copies, *copies[1:4], *out_copies, *copies[4:]):
        copy.start()
    copies[0].wait()
    for copy, here in zip(slab_copies, slabs):
        copy.wait()
        wide = tokens[here, :].astype(jnp.float32)
        mean = jnp.mean(wide * wide, axis=-1, keepdims=True)
        normed[here, :] = (wide * lax.rsqrt(mean + NORM_EPS) * gain[...]).astype(jnp.bfloat16)
    for copy in copies[1:4]:
        copy.wait()
    unit_heads(normed, qk_buf, val_buf, (out_low, out_high), clusters, (2, 3), width)
    for copy in copies[4:] + out_copies:
        copy.wait()


def project_far(tokens, gain, w_qk, w_value, clusters, w_out, width, stages, parts=4):
    rows, depth = tokens.shape
    message = shape((rows + EXTRA, 2 * width))
    pair = (depth, 2 * width)
    return pl.pallas_call(
        functools.partial(project_far_body, width=width, stages=stages, parts=parts),
        out_shape=(
            message,
            message,
            shape((rows, depth)),
            shape(clusters.shape, jnp.int32),
            shape(pair),
            shape(pair),
            shape((2 * width, w_out.shape[1] // 2)),
            shape((2 * width, w_out.shape[1] // 2)),
            shape((2 * width, w_out.shape[1] // 2)),
        ),
        in_specs=[any_spec()] * 6,
        out_specs=(vmem_spec(),) * 9,
        scratch_shapes=[
            pltpu.VMEM((rows, depth), jnp.bfloat16),
            pltpu.VMEM((1, depth), jnp.float32),
            pltpu.VMEM(pair, jnp.bfloat16),
            pltpu.VMEM(pair, jnp.bfloat16),
            pltpu.SemaphoreType.DMA((6,)),
            pltpu.SemaphoreType.DMA((parts,)),
            pltpu.SemaphoreType.DMA((6,)),
        ],
        compiler_params=params(20),
        cost_estimate=cost(8 * rows * depth * width, 2 * rows * depth + 12 * depth * width),
    )(*[held(a) for a in (tokens, gain.reshape(1, depth), w_qk, w_value, clusters, w_out)])


def project_near_body(
    normed, w_qk, w_value, clusters, w_up, out_low, out_high, next_half, sems, *, width
):
    copies = slab_copies(w_up, 0, next_half, sems)
    for copy in copies:
        copy.start()
    unit_heads(normed, w_qk, w_value, (out_low, out_high), clusters, (0, 1), width)
    for copy in copies:
        copy.wait()


def project_near(normed, w_qk, w_value, clusters, w_up, width):
    rows, depth = normed.shape
    message = shape((rows + EXTRA, 2 * width))
    return pl.pallas_call(
        functools.partial(project_near_body, width=width),
        out_shape=(message, message, shape((depth, w_up.shape[1] // 2))),
        in_specs=[vmem_spec()] * 4 + [any_spec()],
        out_specs=(vmem_spec(),) * 3,
        scratch_shapes=[pltpu.SemaphoreType.DMA((SLABS,))],
        compiler_params=params(16),
        cost_estimate=cost(8 * rows * depth * width, 2 * rows * depth + 8 * depth * width),
    )(normed, w_qk, w_value, clusters, held(w_up))


def up_body(normed, first, w_up, w_down, hidden, next_half, second, sems, later_sems):
    half = first.shape[1]
    copies = slab_copies(w_up, half, second, sems)
    later = slab_copies(w_down, 0, next_half, later_sems)
    for copy in copies + later:
        copy.start()
    for at, weights in enumerate((first, second)):
        for copy in copies if at == 1 else []:
            copy.wait()
        grown = jnp.dot(normed[...], weights[...], preferred_element_type=jnp.float32)
        hidden[:, at * half : (at + 1) * half] = jnp.maximum(grown, 0.0).astype(jnp.bfloat16)
    for copy in later:
        copy.wait()


def up(normed, first, w_up, w_down):
    rows, depth = normed.shape
    units = w_up.shape[1]
    return pl.pallas_call(
        up_body,
        out_shape=(shape((rows, units)), shape((units, w_down.shape[1] // 2))),
        in_specs=[vmem_spec(), vmem_spec(), any_spec(), any_spec()],
        out_specs=(vmem_spec(), vmem_spec()),
        scratch_shapes=[
            pltpu.VMEM((depth, units // 2), jnp.bfloat16),
            pltpu.SemaphoreType.DMA((SLABS,)),
            pltpu.SemaphoreType.DMA((SLABS,)),
        ],
        compiler_params=params(24),
        cost_estimate=cost(2 * rows * depth * units, 2 * depth * units + 4 * rows * depth),
    )(normed, first, held(w_up), held(w_down))


def down_body(hidden, first, w_down, mine, far, away, second, held_rows, sems, *, share):
    at = lax.axis_index(TENSOR)
    half = first.shape[1]
    copies = slab_copies(w_down, half, second, sems)
    for copy in copies:
        copy.start()

    def quarter(turn):
        return held_rows[pl.ds(pl.multiple_of((at ^ turn) * share, share), share), :]

    for part, weights in enumerate((first, second)):
        for copy in copies if part == 1 else []:
            copy.wait()
        cols = slice(part * half, (part + 1) * half)
        held_rows[...] = jnp.dot(
            hidden[...], weights[...], preferred_element_type=jnp.float32
        )
        mine[:, cols] = quarter(0)
        far[:, cols] = quarter(2)
        away[0, :, cols] = quarter(1).astype(jnp.bfloat16)
        away[1, :, cols] = quarter(3).astype(jnp.bfloat16)


def down(hidden, first, w_down, share):
    rows, units = hidden.shape
    depth = w_down.shape[1]
    return pl.pallas_call(
        functools.partial(down_body, share=share),
        out_shape=(
            shape((share, depth), jnp.float32),
            shape((share, depth), jnp.float32),
            shape((2, share, depth)),
        ),
        in_specs=[vmem_spec(), vmem_spec(), any_spec()],
        out_specs=(vmem_spec(),) * 3,
        scratch_shapes=[
            pltpu.VMEM((units, depth // 2), jnp.bfloat16),
            pltpu.VMEM((rows, depth // 2), jnp.float32),
            pltpu.SemaphoreType.DMA((SLABS,)),
        ],
        compiler_params=params(24),
        cost_estimate=cost(2 * rows * depth * units, 2 * depth * units + 6 * rows * depth),
    )(hidden, first, held(w_down))


def pick_body(far, got, sent):
    sent[...] = (far[...] + got[1].astype(jnp.float32)).astype(jnp.bfloat16)


def pick(far, got):
    return pl.pallas_call(
        pick_body,
        out_shape=shape(far.shape),
        in_specs=[vmem_spec(), vmem_spec()],
        out_specs=vmem_spec(),
        compiler_params=params(6),
        cost_estimate=cost(far.size, far.size * 8),
    )(far, got)


def block_of(b, heads):
    z = lax.axis_index(SEQ) >> 1
    core = lax.axis_index(TENSOR) % 2
    pair = z ^ (b % heads)
    return 2 * pair + (core ^ (pair & 1) ^ (b // heads))


def attend_body(*refs, heads, width, owned, steps, first):
    if first:
        own, other = refs[:heads], refs[heads : 2 * heads]
        refs = refs[2 * heads :]
        outs = refs[: len(steps)]
        kv, id_rows = refs[len(steps) : len(steps) + 2]
        query, id_cols, acc, den = refs[len(steps) + 2 :]
        rows = kv.shape[1]
        for b, source in enumerate(list(own) + list(other)):
            kv[b] = source[:rows, :]
            tile = source[rows:, :].astype(jnp.float32)
            id_row = jnp.concatenate(
                [tile[r : r + 1, :] for r in range(rows // (2 * width))], axis=1
            )
            id_rows[b] = jnp.broadcast_to(id_row, (8, rows))
    else:
        kv, id_rows = refs[:2]
        outs = refs[2 : 2 + len(steps)]
        query, id_cols, acc, den = refs[2 + len(steps) :]
        rows = kv.shape[1]

    count = 2 * heads
    cluster_col = lax.broadcasted_iota(jnp.int32, (owned, rows), 0)
    wanted = jnp.concatenate(
        [cluster_col + owned * block_of(k, heads) for k in steps], axis=0
    ).astype(jnp.float32)
    sums = jnp.zeros((len(steps) * owned, width), jnp.float32)
    for b in range(count):
        one_hot = jnp.where(wanted == id_rows[b, :1, :], 1.0, 0.0).astype(jnp.bfloat16)
        sums = sums + jnp.dot(one_hot, kv[b, :, :width], preferred_element_type=jnp.float32)

    def pair(b, masked):
        score = lax.dot_general(
            query[...],
            kv[b, :, :width],
            (((1,), (1,)), ((), ())),
            preferred_element_type=jnp.float32,
        )
        weight = jnp.exp(score)
        same = jnp.concatenate([id_cols[...]] * (rows // width), axis=1) == id_rows[b, :1, :]
        if masked:
            row_at = lax.broadcasted_iota(jnp.int32, weight.shape, 0)
            col_at = lax.broadcasted_iota(jnp.int32, weight.shape, 1)
            same = jnp.logical_and(same, col_at <= row_at)
        weight = jnp.where(same, weight, 0.0)
        share = weight[:, :width]
        for part in range(1, rows // width):
            share = share + weight[:, part * width : (part + 1) * width]
        mixed = jnp.dot(
            weight.astype(jnp.bfloat16), kv[b, :, width:], preferred_element_type=jnp.float32
        )
        if masked:
            den[...] = share
            acc[...] = mixed
        else:
            den[...] += share
            acc[...] += mixed

    for at, k in enumerate(steps):
        query[...] = kv[k, :, :width] * jnp.bfloat16(SCORE_SCALE)
        for part in range(rows // width):
            here = pl.ds(part * width, width)
            id_cols[here, :] = jnp.transpose(
                jnp.broadcast_to(id_rows[k, :1, part * width : (part + 1) * width], (width, width))
            )
        pair(k, True)
        block = block_of(k, heads)

        def per_key(b, carry):
            @pl.when(block_of(b, heads) < block)
            def _():
                pair(b, False)

            return carry

        lax.fori_loop(0, count, per_key, 0)
        out = outs[at]
        whole = jnp.sum(den[...], axis=-1, keepdims=True)
        out[:rows, :] = (acc[...] / whole).astype(jnp.bfloat16)
        out[rows:, :] = sums[at * owned : (at + 1) * owned].astype(jnp.bfloat16)


def attend(inputs, heads, rows, width, owned, steps, first):
    result = shape((rows + owned, width))
    out_shape = (result,) * len(steps)
    if first:
        out_shape += (
            shape((2 * heads, rows, 2 * width)),
            shape((2 * heads, 8, rows), jnp.float32),
        )
    units = (heads * heads + heads // 2) * len(steps) // heads
    return pl.pallas_call(
        functools.partial(
            attend_body, heads=heads, width=width, owned=owned, steps=steps, first=first
        ),
        out_shape=out_shape,
        in_specs=[vmem_spec()] * len(inputs),
        out_specs=(vmem_spec(),) * len(out_shape),
        scratch_shapes=[
            pltpu.VMEM((rows, width), jnp.bfloat16),
            pltpu.VMEM((rows, width), jnp.float32),
            pltpu.VMEM((rows, width), jnp.float32),
            pltpu.VMEM((rows, width), jnp.float32),
        ],
        compiler_params=params(20),
        cost_estimate=cost(
            units * rows * rows * width * 8,
            2 * heads * rows * width * 4,
            units * rows * rows,
        ),
    )(*inputs)


def cut_body(*refs, count, share):
    back, kept, away, sums = refs[:count], refs[count], refs[count + 1 : -1], refs[-1]
    at = lax.axis_index(TENSOR)
    for k in range(count):
        for turn in range(len(away) + 1):
            here = pl.ds(pl.multiple_of((at ^ turn) * share, share), share)
            (kept if turn == 0 else away[turn - 1])[k] = back[k][here, :]
        rows = back[k].shape[0] - sums.shape[1]
        sums[k] = back[k][rows:, :].astype(jnp.float32)


def cut(back, owned, share, tensor_count):
    count, width = len(back), back[0].shape[1]
    piece = shape((count, share, width))
    return pl.pallas_call(
        functools.partial(cut_body, count=count, share=share),
        out_shape=(piece,) * tensor_count + (shape((count, owned, width), jnp.float32),),
        in_specs=[vmem_spec()] * count,
        out_specs=(vmem_spec(),) * (tensor_count + 1),
        compiler_params=params(8),
        cost_estimate=cost(0, 4 * count * tensor_count * share * width),
    )(*back)


def head_rows(weights, buf, sems, steps, width):
    z = lax.axis_index(SEQ) >> 1
    copies = []
    for g, w in enumerate(weights):
        for i, k in enumerate(steps):
            here = pl.ds(pl.multiple_of((z ^ k) * width, width), width)
            to = pl.ds((g * len(steps) + i) * width, width)
            copies.append(
                pltpu.make_async_copy(w.at[here, :], buf.at[to, :], sems.at[len(copies)])
            )
    return copies


def side_by_side(pieces, count):
    return jnp.concatenate([p[k] for p in pieces for k in range(count)], axis=1)


def products(pieces, count, near_rows, far_halves, known, put):
    y = lax.axis_index(SEQ) & 1
    half = far_halves[0].shape[1]
    near = side_by_side(pieces[:2], count)
    same, cross = side_by_side(pieces[2:3], count), side_by_side(pieces[3:4], count)
    for turn in range(2):
        cols = pl.ds(pl.multiple_of((y ^ turn) * half, half), half)
        total = known(cols)
        for left, rows in (
            (near, near_rows[:, cols]),
            (same, far_halves[turn][...]),
            (cross, far_halves[2 + turn][...]),
        ):
            total = total + jnp.dot(left, rows, preferred_element_type=jnp.float32)
        put(cols, total)


def mix_first_body(*refs, groups, width, steps, later):
    pieces, weights = refs[:groups], refs[groups : groups + 2]
    far_halves = refs[groups + 2 : groups + 6]
    tokens, mine, got, total, kept, buf, sems, later_sems = refs[groups + 6 :]
    now = head_rows(weights, buf, sems, steps, width)
    then = head_rows(weights, kept, later_sems, later, width)
    for copy in now + then:
        copy.start()
    share = total.shape[0]
    at = lax.axis_index(TENSOR)
    here = pl.ds(pl.multiple_of(at * share, share), share)
    for copy in now:
        copy.wait()

    def known(cols):
        base = tokens[here, cols].astype(jnp.float32) + mine[:, cols]
        return base + got[0, :, cols].astype(jnp.float32)

    def put(cols, value):
        total[:, cols] = value

    products(pieces, len(steps), buf, far_halves, known, put)
    for copy in then:
        copy.wait()


def mix_first(pieces, weights, far_halves, tokens, mine, got, steps, later):
    groups = len(pieces)
    count, share, width = pieces[0].shape
    depth = tokens.shape[1]
    rows = (2 * count * width, depth)
    return pl.pallas_call(
        functools.partial(
            mix_first_body, groups=groups, width=width, steps=steps, later=later
        ),
        out_shape=(shape((share, depth), jnp.float32), shape(rows)),
        in_specs=[vmem_spec()] * groups + [any_spec()] * 2 + [vmem_spec()] * 7,
        out_specs=(vmem_spec(), vmem_spec()),
        scratch_shapes=[
            pltpu.VMEM(rows, jnp.bfloat16),
            pltpu.SemaphoreType.DMA((2 * count,)),
            pltpu.SemaphoreType.DMA((2 * count,)),
        ],
        compiler_params=params(20),
        cost_estimate=cost(
            2 * groups * share * count * width * depth,
            4 * groups * count * width * depth + 8 * share * depth,
        ),
    )(*pieces, *weights, *far_halves, tokens, mine, got)


def mix_last_body(*refs, groups, steps, later):
    pieces, far_halves = refs[:groups], refs[groups : groups + 4]
    total, kept, came, first_sums, last_sums, centroids, out, updated = refs[groups + 4 :]
    z = lax.axis_index(SEQ) >> 1

    def known(cols):
        return total[:, cols] + came[:, cols].astype(jnp.float32)

    def put(cols, value):
        out[:, cols] = value.astype(jnp.bfloat16)

    products(pieces, len(later), kept, far_halves, known, put)
    for sums, turns in ((first_sums, steps), (last_sums, later)):
        for i, k in enumerate(turns):
            head = z ^ k
            updated[head] = EMA_DECAY * centroids[head] + (1.0 - EMA_DECAY) * sums[i]


def mix_last(
    pieces, far_halves, total, kept, came, first_sums, last_sums, centroids, steps, later
):
    groups = len(pieces)
    share, depth = total.shape
    return pl.pallas_call(
        functools.partial(mix_last_body, groups=groups, steps=steps, later=later),
        out_shape=(shape((share, depth)), shape(centroids.shape, jnp.float32)),
        in_specs=[vmem_spec()] * (groups + 10),
        out_specs=(vmem_spec(), vmem_spec()),
        compiler_params=params(16),
        cost_estimate=cost(4 * kept.size * share, 4 * kept.size + 8 * share * depth),
    )(*pieces, *far_halves, total, kept, came, first_sums, last_sums, centroids)


def by_heads(
    tokens, norm_gain, w_qk, w_value, w_out, w_up, w_down, centroids, clusters, slots
):
    tok_rows, _ = tokens.shape
    seq_count = lax.axis_size(SEQ)
    tensor_count = lax.axis_size(TENSOR)
    heads = clusters.shape[0]
    owned = centroids.shape[1]
    width = w_qk.shape[1] // heads
    share = tok_rows // tensor_count
    swaps = [None] + [[(t, t ^ d) for t in range(tensor_count)] for d in range(1, tensor_count)]

    w_core = lax.ppermute(w_out, TENSOR, swaps[1])
    steps = [owner_pairs(k, seq_count, tensor_count) for k in range(heads)]
    swap_y = [(s, s ^ 1) for s in range(seq_count)]
    messages, own, other = [None] * heads, [None] * heads, [None] * heads
    early, late = (heads - 1, 0), (heads - 2, 1)
    messages[2], messages[3], normed, ids, qk_next, val_next, *out_parts = project_far(
        tokens, norm_gain, w_qk, w_value, clusters, w_out, width, (early, late)
    )
    for k in (3, 2):
        own[k] = lax.ppermute(messages[k], BOTH, steps[k])
    halves = {}
    for name in "el":
        here = lax.ppermute(out_parts.pop(0), TENSOR, swaps[2])
        if name == "e":
            there = lax.ppermute(here, SEQ, swap_y)
        else:
            there = lax.ppermute(out_parts.pop(0), TENSOR, swaps[2])
        halves[name] = [here, there] + [lax.ppermute(w, TENSOR, swaps[1]) for w in (here, there)]
    messages[0], messages[1], up_first = project_near(normed, qk_next, val_next, ids, w_up, width)
    for k in (1, 0):
        own[k] = lax.ppermute(messages[k], BOTH, steps[k])
    hidden, down_first = up(normed, up_first, w_up, w_down)
    mine, far, sent = down(hidden, down_first, w_down, share)
    got = lax.ppermute(sent, TENSOR, swaps[1])
    for k in range(heads):
        other[k] = lax.ppermute(own[k], TENSOR, swaps[1])
    picked = pick(far, got)
    came = lax.ppermute(picked, TENSOR, swaps[2])
    back, pieces, sums = [None] * heads, {}, {}
    *results, kv, id_rows = attend(
        own + other, heads, tok_rows, width, owned, early, True
    )
    for k, result in zip(early, results):
        back[k] = lax.ppermute(result, BOTH, turned(steps[k]))
    results = attend([kv, id_rows], heads, tok_rows, width, owned, late, False)
    for k, result in zip(late, results):
        back[k] = lax.ppermute(result, BOTH, turned(steps[k]))

    for name, turns in (("e", early), ("l", late)):
        kept, *away, sums[name] = cut([back[k] for k in turns], owned, share, tensor_count)
        pieces[name] = [kept] + [
            lax.ppermute(away[d - 1], TENSOR, swaps[d])
            for d in range(1, tensor_count)
        ]
    total, late_rows = mix_first(
        pieces["e"], [held(w_out), w_core], halves["e"], tokens, mine, got, early, late
    )
    mixed_rows, new_centroids = mix_last(
        pieces["l"], halves["l"], total, late_rows, came, sums["e"], sums["l"],
        centroids, early, late,
    )
    return (mixed_rows, new_centroids)


def by_clusters(tokens, norm_gain, w_qk, w_value, w_out, w_up, w_down, centroids, clusters, slots):
    tok_rows = tokens.shape[0]
    seq_count = lax.axis_size(SEQ)
    tensor_count = lax.axis_size(TENSOR)
    heads_here = clusters.shape[0]
    owned_count = centroids.shape[1]
    head_width = w_qk.shape[1] // heads_here
    share_rows = tok_rows // tensor_count
    row_first = lax.axis_index(TENSOR) * share_rows
    tokens_wide = tokens.astype(jnp.float32)
    normed = (
        tokens_wide
        * lax.rsqrt(jnp.mean(tokens_wide * tokens_wide, axis=-1, keepdims=True) + NORM_EPS)
        * norm_gain
    ).astype(jnp.bfloat16)
    key_proj = jnp.dot(normed, w_qk, preferred_element_type=jnp.float32).reshape(
        tok_rows, heads_here, head_width
    )
    key_unit = (
        key_proj * lax.rsqrt(jnp.sum(key_proj * key_proj, axis=-1, keepdims=True) + NORM_EPS)
    ).astype(jnp.bfloat16)
    val_proj = (
        jnp.dot(normed, w_value, preferred_element_type=jnp.float32)
        .astype(jnp.bfloat16)
        .reshape(tok_rows, heads_here, head_width)
    )
    positions = lax.axis_index(SEQ) * tok_rows + jnp.arange(tok_rows, dtype=jnp.int32)
    pos_high = (positions // 256).astype(jnp.float32).astype(jnp.bfloat16)
    pos_low = (positions % 256).astype(jnp.float32).astype(jnp.bfloat16)
    flat_slot = clusters.T * CAP + slots.T
    head_grid = jnp.broadcast_to(jnp.arange(heads_here, dtype=jnp.int32)[None, :], flat_slot.shape)
    slot_total = CLUSTERS * CAP
    layout = (heads_here, seq_count, owned_count, CAP)
    key_buf = (
        jnp.zeros((heads_here, slot_total, head_width), jnp.bfloat16)
        .at[head_grid, flat_slot]
        .set(key_unit)
        .reshape(layout + (head_width,))
    )
    val_buf = (
        jnp.zeros((heads_here, slot_total, head_width), jnp.bfloat16)
        .at[head_grid, flat_slot]
        .set(val_proj)
        .reshape(layout + (head_width,))
    )
    high_buf = (
        jnp.full((heads_here, slot_total), 256.0, jnp.bfloat16)
        .at[head_grid, flat_slot]
        .set(jnp.broadcast_to(pos_high[:, None], flat_slot.shape))
        .reshape(layout)
    )
    low_buf = (
        jnp.zeros((heads_here, slot_total), jnp.bfloat16)
        .at[head_grid, flat_slot]
        .set(jnp.broadcast_to(pos_low[:, None], flat_slot.shape))
        .reshape(layout)
    )
    key_in = lax.all_to_all(key_buf, SEQ, split_axis=1, concat_axis=1, tiled=True)
    val_in = lax.all_to_all(val_buf, SEQ, split_axis=1, concat_axis=1, tiled=True)
    high_in = lax.all_to_all(high_buf, SEQ, split_axis=1, concat_axis=1, tiled=True)
    low_in = lax.all_to_all(low_buf, SEQ, split_axis=1, concat_axis=1, tiled=True)
    scores = (
        jnp.einsum("hskad,htkbd->hksatb", key_in, key_in, preferred_element_type=jnp.float32)
        * SCORE_SCALE
    )
    key_place = high_in.astype(jnp.float32) * 256.0 + low_in.astype(jnp.float32)
    ordered = jnp.transpose(key_place, (0, 2, 1, 3))
    causal = ordered[:, :, None, None, :, :] <= ordered[:, :, :, :, None, None]
    exponent = jnp.where(causal, jnp.exp(scores), 0.0)
    weights = (exponent / jnp.sum(exponent, axis=(4, 5), keepdims=True)).astype(jnp.bfloat16)
    mixed_out = jnp.einsum(
        "hksatb,htkbd->hskad", weights, val_in, preferred_element_type=jnp.float32
    ).astype(jnp.bfloat16)
    returned_back = lax.all_to_all(mixed_out, SEQ, split_axis=1, concat_axis=1, tiled=True)
    one_hot = (clusters[:, :, None] == jnp.arange(CLUSTERS, dtype=jnp.int32)[None, None, :]).astype(
        jnp.bfloat16
    )
    local_sums = jnp.einsum("htk,thd->hkd", one_hot, key_unit, preferred_element_type=jnp.float32)
    totals = lax.psum_scatter(
        local_sums.astype(jnp.bfloat16), SEQ, scatter_dimension=1, tiled=True
    ).astype(jnp.float32)
    new_centroids = EMA_DECAY * centroids + (1.0 - EMA_DECAY) * totals
    returned = returned_back.reshape(heads_here, slot_total, head_width)
    attended = returned[head_grid, flat_slot].reshape(tok_rows, heads_here * head_width)
    attn_part = jnp.dot(attended, w_out, preferred_element_type=jnp.float32)
    hidden = jax.nn.relu(jnp.dot(normed, w_up, preferred_element_type=jnp.float32)).astype(
        jnp.bfloat16
    )
    ffn_part = jnp.dot(hidden, w_down, preferred_element_type=jnp.float32)
    summed = lax.psum_scatter(
        rounded(attn_part + ffn_part).astype(jnp.bfloat16),
        TENSOR,
        scatter_dimension=0,
        tiled=True,
    ).astype(jnp.float32)
    own_rows = lax.dynamic_slice_in_dim(tokens_wide, row_first, share_rows, 0)
    mixed_rows = (own_rows + summed).astype(jnp.bfloat16)
    return (mixed_rows, new_centroids)


def solution(mesh):
    in_specs = (
        P(SEQ, None),
        P(),
        P(None, TENSOR),
        P(None, TENSOR),
        P(TENSOR, None),
        P(None, TENSOR),
        P(TENSOR, None),
        P(TENSOR, SEQ, None),
        P(TENSOR, SEQ),
        P(TENSOR, SEQ),
    )
    out_specs = (P((SEQ, TENSOR), None), P(TENSOR, SEQ, None))
    sizes = dict(mesh.shape)

    def local(*args):
        heads = args[8].shape[0]
        fits = (
            sizes[TENSOR] == 4
            and sizes[SEQ] == 2 * heads
            and heads & (heads - 1) == 0
            and heads == 4
        )
        if not fits:
            return by_clusters(*args)
        return by_heads(*args)

    return jax.shard_map(
        local, mesh=mesh, in_specs=in_specs, out_specs=out_specs, check_vma=False
    )
```

```python
import functools

import jax
import jax.numpy as jnp
from jax import lax
from jax.experimental import pallas as pl
from jax.experimental.pallas import tpu as pltpu
from jax.sharding import PartitionSpec as P


CLUSTERS = 256
CAP = 4

SCORE_SCALE = 2.0
EMA_DECAY = 0.9
NORM_EPS = 1e-06
SEQ, TENSOR = "seq", "tensor"
BOTH = (SEQ, TENSOR)
EXTRA = 16
MIB = 1024 * 1024


def rounded(term_value):
    return lax.optimization_barrier(term_value.astype(jnp.bfloat16)).astype(jnp.float32)


def owner_pairs(step, seq_count, tensor_count):
    pairs = []
    for s in range(seq_count):
        for t in range(tensor_count):
            z, y, c = s // 2, s % 2, t % 2
            dest_s = 2 * (z ^ step) + c
            dest_t = (t - c) + (y ^ (z & 1))
            pairs.append((s * tensor_count + t, dest_s * tensor_count + dest_t))
    return pairs


def turned(pairs):
    return [(b, a) for a, b in pairs]


def any_spec():
    return pl.BlockSpec(memory_space=pl.ANY)


def vmem_spec():
    return pl.BlockSpec(memory_space=pltpu.VMEM)


def held(value):
    return pltpu.with_memory_space_constraint(value, pltpu.HBM)


def params(mib):
    return pltpu.CompilerParams(vmem_limit_bytes=mib * MIB)


def cost(flops, moved, transcendentals=0):
    return pl.CostEstimate(
        flops=flops, bytes_accessed=moved, transcendentals=transcendentals
    )


def shape(dims, kind=jnp.bfloat16):
    return jax.ShapeDtypeStruct(dims, kind)


def unit_heads(normed, w_qk, w_value, outs, clusters, steps, width):
    z = lax.axis_index(SEQ) >> 1
    rows = normed.shape[0]
    span = 2 * width
    odd = (z & 1) == 1
    row_at = lax.broadcasted_iota(jnp.int32, (EXTRA, span), 0)
    key_proj = jnp.dot(normed[...], w_qk[...], preferred_element_type=jnp.float32)
    units = []
    for q in range(2):
        k = key_proj[:, q * width : (q + 1) * width]
        total = jnp.sum(k * k, axis=-1, keepdims=True)
        units.append((k * lax.rsqrt(total + NORM_EPS)).astype(jnp.bfloat16))
    val_proj = jnp.dot(normed[...], w_value[...], preferred_element_type=jnp.float32)
    values = [val_proj[:, q * width : (q + 1) * width].astype(jnp.bfloat16) for q in range(2)]
    for q, out in enumerate(outs):
        out[:rows, :width] = jnp.where(odd, units[1 - q], units[q])
        out[:rows, width:] = jnp.where(odd, values[1 - q], values[q])
        id_row = clusters[pl.ds(steps[q] ^ z, 1), :].astype(jnp.float32)
        tail = jnp.zeros((EXTRA, span), jnp.float32)
        for part in range(rows // span):
            piece = id_row[:, part * span : (part + 1) * span]
            tail = jnp.where(row_at == part, piece, tail)
        out[rows:, :] = tail.astype(jnp.bfloat16)


def project_far_body(
    tokens_at, gain_at, w_qk, w_value, clusters_at, w_out, *rest, width, stages, parts
):
    out_low, out_high, normed, clusters, qk_next, val_next, out_early, out_late, out_rest = rest[:9]
    tokens, gain, qk_buf, val_buf, sems, token_sems, out_sems = rest[9:]
    z = lax.axis_index(SEQ) >> 1
    y = lax.axis_index(SEQ) & 1
    step = tokens.shape[0] // parts
    span = 2 * width
    slabs = [pl.ds(r * step, step) for r in range(parts)]
    slab_copies = [
        pltpu.make_async_copy(tokens_at.at[here, :], tokens.at[here, :], token_sems.at[r])
        for r, here in enumerate(slabs)
    ]

    def columns(block):
        return pl.ds(pl.multiple_of(block * span, span), span)

    first, second = columns(1 ^ (z >> 1)), columns(z >> 1)
    half = out_early.shape[1]
    out_copies = []
    for part, turns, at in (
        (out_early, stages[0], y),
        (out_late, stages[1], y),
        (out_rest, stages[1], 1 - y),
    ):
        out_cols = pl.ds(pl.multiple_of(at * half, half), half)
        for i, k in enumerate(turns):
            here = pl.ds(pl.multiple_of((z ^ k) * width, width), width)
            out_copies.append(
                pltpu.make_async_copy(
                    w_out.at[here, out_cols],
                    part.at[pl.ds(i * width, width), :],
                    out_sems.at[len(out_copies)],
                )
            )
    copies = [
        pltpu.make_async_copy(gain_at, gain, sems.at[0]),
        pltpu.make_async_copy(w_qk.at[:, first], qk_buf, sems.at[1]),
        pltpu.make_async_copy(w_value.at[:, first], val_buf, sems.at[2]),
        pltpu.make_async_copy(clusters_at, clusters, sems.at[3]),
        pltpu.make_async_copy(w_qk.at[:, second], qk_next, sems.at[4]),
        pltpu.make_async_copy(w_value.at[:, second], val_next, sems.at[5]),
    ]
    for copy in (copies[0], *slab_copies, *copies[1:4], *out_copies, *copies[4:]):
        copy.start()
    copies[0].wait()
    for copy, here in zip(slab_copies, slabs):
        copy.wait()
        wide = tokens[here, :].astype(jnp.float32)
        mean = jnp.mean(wide * wide, axis=-1, keepdims=True)
        normed[here, :] = (wide * lax.rsqrt(mean + NORM_EPS) * gain[...]).astype(jnp.bfloat16)
    for copy in copies[1:4]:
        copy.wait()
    unit_heads(normed, qk_buf, val_buf, (out_low, out_high), clusters, (2, 3), width)
    for copy in copies[4:] + out_copies:
        copy.wait()


def project_far(tokens, gain, w_qk, w_value, clusters, w_out, width, stages, parts=4):
    rows, depth = tokens.shape
    message = shape((rows + EXTRA, 2 * width))
    pair = (depth, 2 * width)
    return pl.pallas_call(
        functools.partial(project_far_body, width=width, stages=stages, parts=parts),
        out_shape=(
            message,
            message,
            shape((rows, depth)),
            shape(clusters.shape, jnp.int32),
            shape(pair),
            shape(pair),
            shape((2 * width, w_out.shape[1] // 2)),
            shape((2 * width, w_out.shape[1] // 2)),
            shape((2 * width, w_out.shape[1] // 2)),
        ),
        in_specs=[any_spec()] * 6,
        out_specs=(vmem_spec(),) * 9,
        scratch_shapes=[
            pltpu.VMEM((rows, depth), jnp.bfloat16),
            pltpu.VMEM((1, depth), jnp.float32),
            pltpu.VMEM(pair, jnp.bfloat16),
            pltpu.VMEM(pair, jnp.bfloat16),
            pltpu.SemaphoreType.DMA((6,)),
            pltpu.SemaphoreType.DMA((parts,)),
            pltpu.SemaphoreType.DMA((6,)),
        ],
        compiler_params=params(20),
        cost_estimate=cost(8 * rows * depth * width, 2 * rows * depth + 12 * depth * width),
    )(*[held(a) for a in (tokens, gain.reshape(1, depth), w_qk, w_value, clusters, w_out)])


def project_near_body(
    normed, w_qk, w_value, clusters, w_up, out_low, out_high, next_half, sem, *, width
):
    copy = pltpu.make_async_copy(w_up.at[:, pl.ds(0, next_half.shape[1])], next_half, sem)
    copy.start()
    unit_heads(normed, w_qk, w_value, (out_low, out_high), clusters, (0, 1), width)
    copy.wait()


def project_near(normed, w_qk, w_value, clusters, w_up, width):
    rows, depth = normed.shape
    message = shape((rows + EXTRA, 2 * width))
    return pl.pallas_call(
        functools.partial(project_near_body, width=width),
        out_shape=(message, message, shape((depth, w_up.shape[1] // 2))),
        in_specs=[vmem_spec()] * 4 + [any_spec()],
        out_specs=(vmem_spec(),) * 3,
        scratch_shapes=[pltpu.SemaphoreType.DMA],
        compiler_params=params(16),
        cost_estimate=cost(8 * rows * depth * width, 2 * rows * depth + 8 * depth * width),
    )(normed, w_qk, w_value, clusters, held(w_up))


def up_body(normed, first, w_up, w_down, hidden, next_half, second, sems):
    half = first.shape[1]
    copies = (
        pltpu.make_async_copy(w_up.at[:, pl.ds(half, half)], second, sems.at[0]),
        pltpu.make_async_copy(
            w_down.at[:, pl.ds(0, next_half.shape[1])], next_half, sems.at[1]
        ),
    )
    for copy in copies:
        copy.start()
    for at, weights in enumerate((first, second)):
        if at == 1:
            copies[0].wait()
        grown = jnp.dot(normed[...], weights[...], preferred_element_type=jnp.float32)
        hidden[:, at * half : (at + 1) * half] = jnp.maximum(grown, 0.0).astype(jnp.bfloat16)
    copies[1].wait()


def up(normed, first, w_up, w_down):
    rows, depth = normed.shape
    units = w_up.shape[1]
    return pl.pallas_call(
        up_body,
        out_shape=(shape((rows, units)), shape((units, w_down.shape[1] // 2))),
        in_specs=[vmem_spec(), vmem_spec(), any_spec(), any_spec()],
        out_specs=(vmem_spec(), vmem_spec()),
        scratch_shapes=[
            pltpu.VMEM((depth, units // 2), jnp.bfloat16),
            pltpu.SemaphoreType.DMA((2,)),
        ],
        compiler_params=params(24),
        cost_estimate=cost(2 * rows * depth * units, 2 * depth * units + 4 * rows * depth),
    )(normed, first, held(w_up), held(w_down))


def down_body(hidden, first, w_down, mine, far, away, second, held_rows, sem, *, share):
    at = lax.axis_index(TENSOR)
    half = first.shape[1]
    copy = pltpu.make_async_copy(w_down.at[:, pl.ds(half, half)], second, sem)
    copy.start()

    def quarter(turn):
        return held_rows[pl.ds(pl.multiple_of((at ^ turn) * share, share), share), :]

    for part, weights in enumerate((first, second)):
        if part == 1:
            copy.wait()
        cols = slice(part * half, (part + 1) * half)
        held_rows[...] = jnp.dot(
            hidden[...], weights[...], preferred_element_type=jnp.float32
        )
        mine[:, cols] = quarter(0)
        far[:, cols] = quarter(2)
        away[0, :, cols] = quarter(1).astype(jnp.bfloat16)
        away[1, :, cols] = quarter(3).astype(jnp.bfloat16)


def down(hidden, first, w_down, share):
    rows, units = hidden.shape
    depth = w_down.shape[1]
    return pl.pallas_call(
        functools.partial(down_body, share=share),
        out_shape=(
            shape((share, depth), jnp.float32),
            shape((share, depth), jnp.float32),
            shape((2, share, depth)),
        ),
        in_specs=[vmem_spec(), vmem_spec(), any_spec()],
        out_specs=(vmem_spec(),) * 3,
        scratch_shapes=[
            pltpu.VMEM((units, depth // 2), jnp.bfloat16),
            pltpu.VMEM((rows, depth // 2), jnp.float32),
            pltpu.SemaphoreType.DMA,
        ],
        compiler_params=params(24),
        cost_estimate=cost(2 * rows * depth * units, 2 * depth * units + 6 * rows * depth),
    )(hidden, first, held(w_down))


def pick_body(far, got, sent):
    sent[...] = (far[...] + got[1].astype(jnp.float32)).astype(jnp.bfloat16)


def pick(far, got):
    return pl.pallas_call(
        pick_body,
        out_shape=shape(far.shape),
        in_specs=[vmem_spec(), vmem_spec()],
        out_specs=vmem_spec(),
        compiler_params=params(6),
        cost_estimate=cost(far.size, far.size * 8),
    )(far, got)


def block_of(b, heads):
    z = lax.axis_index(SEQ) >> 1
    core = lax.axis_index(TENSOR) % 2
    pair = z ^ (b % heads)
    return 2 * pair + (core ^ (pair & 1) ^ (b // heads))


def attend_body(*refs, heads, width, owned, steps, first):
    if first:
        own, other = refs[:heads], refs[heads : 2 * heads]
        refs = refs[2 * heads :]
        outs = refs[: len(steps)]
        kv, id_rows = refs[len(steps) : len(steps) + 2]
        query, id_cols, acc, den = refs[len(steps) + 2 :]
        rows = kv.shape[1]
        for b, source in enumerate(list(own) + list(other)):
            kv[b] = source[:rows, :]
            tile = source[rows:, :].astype(jnp.float32)
            id_row = jnp.concatenate(
                [tile[r : r + 1, :] for r in range(rows // (2 * width))], axis=1
            )
            id_rows[b] = jnp.broadcast_to(id_row, (8, rows))
    else:
        kv, id_rows = refs[:2]
        outs = refs[2 : 2 + len(steps)]
        query, id_cols, acc, den = refs[2 + len(steps) :]
        rows = kv.shape[1]

    count = 2 * heads
    cluster_col = lax.broadcasted_iota(jnp.int32, (owned, rows), 0)
    wanted = jnp.concatenate(
        [cluster_col + owned * block_of(k, heads) for k in steps], axis=0
    ).astype(jnp.float32)
    sums = jnp.zeros((len(steps) * owned, width), jnp.float32)
    for b in range(count):
        one_hot = jnp.where(wanted == id_rows[b, :1, :], 1.0, 0.0).astype(jnp.bfloat16)
        sums = sums + jnp.dot(one_hot, kv[b, :, :width], preferred_element_type=jnp.float32)

    def pair(blocks, masked):
        spread = jnp.concatenate([id_cols[...]] * (rows // width), axis=1)
        shares, mixes = [], []
        for b in blocks:
            score = lax.dot_general(
                query[...],
                kv[b, :, :width],
                (((1,), (1,)), ((), ())),
                preferred_element_type=jnp.float32,
            )
            weight = jnp.exp(score)
            same = spread == id_rows[b, :1, :]
            if masked:
                row_at = lax.broadcasted_iota(jnp.int32, weight.shape, 0)
                col_at = lax.broadcasted_iota(jnp.int32, weight.shape, 1)
                same = jnp.logical_and(same, col_at <= row_at)
            weight = jnp.where(same, weight, 0.0)
            shares += [
                weight[:, part * width : (part + 1) * width] for part in range(rows // width)
            ]
            mixes.append(
                jnp.dot(
                    weight.astype(jnp.bfloat16),
                    kv[b, :, width:],
                    preferred_element_type=jnp.float32,
                )
            )
        if masked:
            den[...], acc[...] = sum(shares[1:], shares[0]), sum(mixes[1:], mixes[0])
        else:
            den[...] += sum(shares[1:], shares[0])
            acc[...] += sum(mixes[1:], mixes[0])

    z = lax.axis_index(SEQ) >> 1
    for at, k in enumerate(steps):
        query[...] = kv[k, :, :width] * jnp.bfloat16(SCORE_SCALE)
        for part in range(rows // width):
            here = pl.ds(part * width, width)
            id_cols[here, :] = jnp.transpose(
                jnp.broadcast_to(id_rows[k, :1, part * width : (part + 1) * width], (width, width))
            )
        pair((k,), True)

        @pl.when(block_of(k + heads, heads) < block_of(k, heads))
        def _():
            pair((k + heads,), False)

        def per_pair(turn, carry):
            b = k ^ turn

            @pl.when((z ^ b) < (z ^ k))
            def _():
                pair((b, b + heads), False)

            return carry

        lax.fori_loop(1, heads, per_pair, 0)
        out = outs[at]
        whole = jnp.sum(den[...], axis=-1, keepdims=True)
        out[:rows, :] = (acc[...] / whole).astype(jnp.bfloat16)
        out[rows:, :] = sums[at * owned : (at + 1) * owned].astype(jnp.bfloat16)


def attend(inputs, heads, rows, width, owned, steps, first):
    result = shape((rows + owned, width))
    out_shape = (result,) * len(steps)
    if first:
        out_shape += (
            shape((2 * heads, rows, 2 * width)),
            shape((2 * heads, 8, rows), jnp.float32),
        )
    units = (heads * heads + heads // 2) * len(steps) // heads
    return pl.pallas_call(
        functools.partial(
            attend_body, heads=heads, width=width, owned=owned, steps=steps, first=first
        ),
        out_shape=out_shape,
        in_specs=[vmem_spec()] * len(inputs),
        out_specs=(vmem_spec(),) * len(out_shape),
        scratch_shapes=[
            pltpu.VMEM((rows, width), jnp.bfloat16),
            pltpu.VMEM((rows, width), jnp.float32),
            pltpu.VMEM((rows, width), jnp.float32),
            pltpu.VMEM((rows, width), jnp.float32),
        ],
        compiler_params=params(20),
        cost_estimate=cost(
            units * rows * rows * width * 8,
            2 * heads * rows * width * 4,
            units * rows * rows,
        ),
    )(*inputs)


def cut_body(*refs, count, share):
    back, kept, away, sums = refs[:count], refs[count], refs[count + 1 : -1], refs[-1]
    at = lax.axis_index(TENSOR)
    for k in range(count):
        for turn in range(len(away) + 1):
            here = pl.ds(pl.multiple_of((at ^ turn) * share, share), share)
            (kept if turn == 0 else away[turn - 1])[k] = back[k][here, :]
        rows = back[k].shape[0] - sums.shape[1]
        sums[k] = back[k][rows:, :].astype(jnp.float32)


def cut(back, owned, share, tensor_count):
    count, width = len(back), back[0].shape[1]
    piece = shape((count, share, width))
    return pl.pallas_call(
        functools.partial(cut_body, count=count, share=share),
        out_shape=(piece,) * tensor_count + (shape((count, owned, width), jnp.float32),),
        in_specs=[vmem_spec()] * count,
        out_specs=(vmem_spec(),) * (tensor_count + 1),
        compiler_params=params(8),
        cost_estimate=cost(0, 4 * count * tensor_count * share * width),
    )(*back)


def head_rows(weights, buf, sems, steps, width):
    z = lax.axis_index(SEQ) >> 1
    copies = []
    for g, w in enumerate(weights):
        for i, k in enumerate(steps):
            here = pl.ds(pl.multiple_of((z ^ k) * width, width), width)
            to = pl.ds((g * len(steps) + i) * width, width)
            copies.append(
                pltpu.make_async_copy(w.at[here, :], buf.at[to, :], sems.at[len(copies)])
            )
    return copies


def side_by_side(pieces, count):
    return jnp.concatenate([p[k] for p in pieces for k in range(count)], axis=1)


def products(pieces, count, near_rows, far_halves, known, put):
    y = lax.axis_index(SEQ) & 1
    half = far_halves[0].shape[1]
    near = side_by_side(pieces[:2], count)
    same, cross = side_by_side(pieces[2:3], count), side_by_side(pieces[3:4], count)
    for turn in range(2):
        cols = pl.ds(pl.multiple_of((y ^ turn) * half, half), half)
        total = known(cols)
        for left, rows in (
            (near, near_rows[:, cols]),
            (same, far_halves[turn][...]),
            (cross, far_halves[2 + turn][...]),
        ):
            total = total + jnp.dot(left, rows, preferred_element_type=jnp.float32)
        put(cols, total)


def mix_first_body(*refs, groups, width, steps, later):
    pieces, weights = refs[:groups], refs[groups : groups + 2]
    far_halves = refs[groups + 2 : groups + 6]
    tokens, mine, got, total, kept, buf, sems, later_sems = refs[groups + 6 :]
    now = head_rows(weights, buf, sems, steps, width)
    then = head_rows(weights, kept, later_sems, later, width)
    for copy in now + then:
        copy.start()
    share = total.shape[0]
    at = lax.axis_index(TENSOR)
    here = pl.ds(pl.multiple_of(at * share, share), share)
    for copy in now:
        copy.wait()

    def known(cols):
        base = tokens[here, cols].astype(jnp.float32) + mine[:, cols]
        return base + got[0, :, cols].astype(jnp.float32)

    def put(cols, value):
        total[:, cols] = value

    products(pieces, len(steps), buf, far_halves, known, put)
    for copy in then:
        copy.wait()


def mix_first(pieces, weights, far_halves, tokens, mine, got, steps, later):
    groups = len(pieces)
    count, share, width = pieces[0].shape
    depth = tokens.shape[1]
    rows = (2 * count * width, depth)
    return pl.pallas_call(
        functools.partial(
            mix_first_body, groups=groups, width=width, steps=steps, later=later
        ),
        out_shape=(shape((share, depth), jnp.float32), shape(rows)),
        in_specs=[vmem_spec()] * groups + [any_spec()] * 2 + [vmem_spec()] * 7,
        out_specs=(vmem_spec(), vmem_spec()),
        scratch_shapes=[
            pltpu.VMEM(rows, jnp.bfloat16),
            pltpu.SemaphoreType.DMA((2 * count,)),
            pltpu.SemaphoreType.DMA((2 * count,)),
        ],
        compiler_params=params(20),
        cost_estimate=cost(
            2 * groups * share * count * width * depth,
            4 * groups * count * width * depth + 8 * share * depth,
        ),
    )(*pieces, *weights, *far_halves, tokens, mine, got)


def mix_last_body(*refs, groups, steps, later):
    pieces, far_halves = refs[:groups], refs[groups : groups + 4]
    total, kept, came, first_sums, last_sums, centroids, out, updated = refs[groups + 4 :]
    z = lax.axis_index(SEQ) >> 1

    def known(cols):
        return total[:, cols] + came[:, cols].astype(jnp.float32)

    def put(cols, value):
        out[:, cols] = value.astype(jnp.bfloat16)

    products(pieces, len(later), kept, far_halves, known, put)
    for sums, turns in ((first_sums, steps), (last_sums, later)):
        for i, k in enumerate(turns):
            head = z ^ k
            updated[head] = EMA_DECAY * centroids[head] + (1.0 - EMA_DECAY) * sums[i]


def mix_last(
    pieces, far_halves, total, kept, came, first_sums, last_sums, centroids, steps, later
):
    groups = len(pieces)
    share, depth = total.shape
    return pl.pallas_call(
        functools.partial(mix_last_body, groups=groups, steps=steps, later=later),
        out_shape=(shape((share, depth)), shape(centroids.shape, jnp.float32)),
        in_specs=[vmem_spec()] * (groups + 10),
        out_specs=(vmem_spec(), vmem_spec()),
        compiler_params=params(16),
        cost_estimate=cost(4 * kept.size * share, 4 * kept.size + 8 * share * depth),
    )(*pieces, *far_halves, total, kept, came, first_sums, last_sums, centroids)


def by_heads(
    tokens, norm_gain, w_qk, w_value, w_out, w_up, w_down, centroids, clusters, slots
):
    tok_rows, _ = tokens.shape
    seq_count = lax.axis_size(SEQ)
    tensor_count = lax.axis_size(TENSOR)
    heads = clusters.shape[0]
    owned = centroids.shape[1]
    width = w_qk.shape[1] // heads
    share = tok_rows // tensor_count
    swaps = [None] + [[(t, t ^ d) for t in range(tensor_count)] for d in range(1, tensor_count)]

    w_core = lax.ppermute(w_out, TENSOR, swaps[1])
    steps = [owner_pairs(k, seq_count, tensor_count) for k in range(heads)]
    swap_y = [(s, s ^ 1) for s in range(seq_count)]
    messages, own, other = [None] * heads, [None] * heads, [None] * heads
    early, late = (heads - 1, 0), (heads - 2, 1)
    messages[2], messages[3], normed, ids, qk_next, val_next, *out_parts = project_far(
        tokens, norm_gain, w_qk, w_value, clusters, w_out, width, (early, late)
    )
    for k in (3, 2):
        own[k] = lax.ppermute(messages[k], BOTH, steps[k])
    halves = {}
    for name in "el":
        here = lax.ppermute(out_parts.pop(0), TENSOR, swaps[2])
        if name == "e":
            there = lax.ppermute(here, SEQ, swap_y)
        else:
            there = lax.ppermute(out_parts.pop(0), TENSOR, swaps[2])
        halves[name] = [here, there] + [lax.ppermute(w, TENSOR, swaps[1]) for w in (here, there)]
    messages[0], messages[1], up_first = project_near(normed, qk_next, val_next, ids, w_up, width)
    for k in (1, 0):
        own[k] = lax.ppermute(messages[k], BOTH, steps[k])
    hidden, down_first = up(normed, up_first, w_up, w_down)
    mine, far, sent = down(hidden, down_first, w_down, share)
    got = lax.ppermute(sent, TENSOR, swaps[1])
    for k in range(heads):
        other[k] = lax.ppermute(own[k], TENSOR, swaps[1])
    picked = pick(far, got)
    came = lax.ppermute(picked, TENSOR, swaps[2])
    back, pieces, sums = [None] * heads, {}, {}
    *results, kv, id_rows = attend(
        own + other, heads, tok_rows, width, owned, early, True
    )
    for k, result in zip(early, results):
        back[k] = lax.ppermute(result, BOTH, turned(steps[k]))
    results = attend([kv, id_rows], heads, tok_rows, width, owned, late, False)
    for k, result in zip(late, results):
        back[k] = lax.ppermute(result, BOTH, turned(steps[k]))

    for name, turns in (("e", early), ("l", late)):
        kept, *away, sums[name] = cut([back[k] for k in turns], owned, share, tensor_count)
        pieces[name] = [kept] + [
            lax.ppermute(away[d - 1], TENSOR, swaps[d])
            for d in range(1, tensor_count)
        ]
    total, late_rows = mix_first(
        pieces["e"], [held(w_out), w_core], halves["e"], tokens, mine, got, early, late
    )
    mixed_rows, new_centroids = mix_last(
        pieces["l"], halves["l"], total, late_rows, came, sums["e"], sums["l"],
        centroids, early, late,
    )
    return (mixed_rows, new_centroids)


def by_clusters(tokens, norm_gain, w_qk, w_value, w_out, w_up, w_down, centroids, clusters, slots):
    tok_rows = tokens.shape[0]
    seq_count = lax.axis_size(SEQ)
    tensor_count = lax.axis_size(TENSOR)
    heads_here = clusters.shape[0]
    owned_count = centroids.shape[1]
    head_width = w_qk.shape[1] // heads_here
    share_rows = tok_rows // tensor_count
    row_first = lax.axis_index(TENSOR) * share_rows
    tokens_wide = tokens.astype(jnp.float32)
    normed = (
        tokens_wide
        * lax.rsqrt(jnp.mean(tokens_wide * tokens_wide, axis=-1, keepdims=True) + NORM_EPS)
        * norm_gain
    ).astype(jnp.bfloat16)
    key_proj = jnp.dot(normed, w_qk, preferred_element_type=jnp.float32).reshape(
        tok_rows, heads_here, head_width
    )
    key_unit = (
        key_proj * lax.rsqrt(jnp.sum(key_proj * key_proj, axis=-1, keepdims=True) + NORM_EPS)
    ).astype(jnp.bfloat16)
    val_proj = (
        jnp.dot(normed, w_value, preferred_element_type=jnp.float32)
        .astype(jnp.bfloat16)
        .reshape(tok_rows, heads_here, head_width)
    )
    positions = lax.axis_index(SEQ) * tok_rows + jnp.arange(tok_rows, dtype=jnp.int32)
    pos_high = (positions // 256).astype(jnp.float32).astype(jnp.bfloat16)
    pos_low = (positions % 256).astype(jnp.float32).astype(jnp.bfloat16)
    flat_slot = clusters.T * CAP + slots.T
    head_grid = jnp.broadcast_to(jnp.arange(heads_here, dtype=jnp.int32)[None, :], flat_slot.shape)
    slot_total = CLUSTERS * CAP
    layout = (heads_here, seq_count, owned_count, CAP)
    key_buf = (
        jnp.zeros((heads_here, slot_total, head_width), jnp.bfloat16)
        .at[head_grid, flat_slot]
        .set(key_unit)
        .reshape(layout + (head_width,))
    )
    val_buf = (
        jnp.zeros((heads_here, slot_total, head_width), jnp.bfloat16)
        .at[head_grid, flat_slot]
        .set(val_proj)
        .reshape(layout + (head_width,))
    )
    high_buf = (
        jnp.full((heads_here, slot_total), 256.0, jnp.bfloat16)
        .at[head_grid, flat_slot]
        .set(jnp.broadcast_to(pos_high[:, None], flat_slot.shape))
        .reshape(layout)
    )
    low_buf = (
        jnp.zeros((heads_here, slot_total), jnp.bfloat16)
        .at[head_grid, flat_slot]
        .set(jnp.broadcast_to(pos_low[:, None], flat_slot.shape))
        .reshape(layout)
    )
    key_in = lax.all_to_all(key_buf, SEQ, split_axis=1, concat_axis=1, tiled=True)
    val_in = lax.all_to_all(val_buf, SEQ, split_axis=1, concat_axis=1, tiled=True)
    high_in = lax.all_to_all(high_buf, SEQ, split_axis=1, concat_axis=1, tiled=True)
    low_in = lax.all_to_all(low_buf, SEQ, split_axis=1, concat_axis=1, tiled=True)
    scores = (
        jnp.einsum("hskad,htkbd->hksatb", key_in, key_in, preferred_element_type=jnp.float32)
        * SCORE_SCALE
    )
    key_place = high_in.astype(jnp.float32) * 256.0 + low_in.astype(jnp.float32)
    ordered = jnp.transpose(key_place, (0, 2, 1, 3))
    causal = ordered[:, :, None, None, :, :] <= ordered[:, :, :, :, None, None]
    exponent = jnp.where(causal, jnp.exp(scores), 0.0)
    weights = (exponent / jnp.sum(exponent, axis=(4, 5), keepdims=True)).astype(jnp.bfloat16)
    mixed_out = jnp.einsum(
        "hksatb,htkbd->hskad", weights, val_in, preferred_element_type=jnp.float32
    ).astype(jnp.bfloat16)
    returned_back = lax.all_to_all(mixed_out, SEQ, split_axis=1, concat_axis=1, tiled=True)
    one_hot = (clusters[:, :, None] == jnp.arange(CLUSTERS, dtype=jnp.int32)[None, None, :]).astype(
        jnp.bfloat16
    )
    local_sums = jnp.einsum("htk,thd->hkd", one_hot, key_unit, preferred_element_type=jnp.float32)
    totals = lax.psum_scatter(
        local_sums.astype(jnp.bfloat16), SEQ, scatter_dimension=1, tiled=True
    ).astype(jnp.float32)
    new_centroids = EMA_DECAY * centroids + (1.0 - EMA_DECAY) * totals
    returned = returned_back.reshape(heads_here, slot_total, head_width)
    attended = returned[head_grid, flat_slot].reshape(tok_rows, heads_here * head_width)
    attn_part = jnp.dot(attended, w_out, preferred_element_type=jnp.float32)
    hidden = jax.nn.relu(jnp.dot(normed, w_up, preferred_element_type=jnp.float32)).astype(
        jnp.bfloat16
    )
    ffn_part = jnp.dot(hidden, w_down, preferred_element_type=jnp.float32)
    summed = lax.psum_scatter(
        rounded(attn_part + ffn_part).astype(jnp.bfloat16),
        TENSOR,
        scatter_dimension=0,
        tiled=True,
    ).astype(jnp.float32)
    own_rows = lax.dynamic_slice_in_dim(tokens_wide, row_first, share_rows, 0)
    mixed_rows = (own_rows + summed).astype(jnp.bfloat16)
    return (mixed_rows, new_centroids)


def solution(mesh):
    in_specs = (
        P(SEQ, None),
        P(),
        P(None, TENSOR),
        P(None, TENSOR),
        P(TENSOR, None),
        P(None, TENSOR),
        P(TENSOR, None),
        P(TENSOR, SEQ, None),
        P(TENSOR, SEQ),
        P(TENSOR, SEQ),
    )
    out_specs = (P((SEQ, TENSOR), None), P(TENSOR, SEQ, None))
    sizes = dict(mesh.shape)

    def local(*args):
        heads = args[8].shape[0]
        fits = (
            sizes[TENSOR] == 4
            and sizes[SEQ] == 2 * heads
            and heads & (heads - 1) == 0
            and heads == 4
        )
        if not fits:
            return by_clusters(*args)
        return by_heads(*args)

    return jax.shard_map(
        local, mesh=mesh, in_specs=in_specs, out_specs=out_specs, check_vma=False
    )
```

```python
import functools

import jax
import jax.numpy as jnp
from jax import lax
from jax.experimental import pallas as pl
from jax.experimental.pallas import tpu as pltpu
from jax.sharding import PartitionSpec as P


CLUSTERS = 256
CAP = 4

SCORE_SCALE = 2.0
EMA_DECAY = 0.9
NORM_EPS = 1e-06
SEQ, TENSOR = "seq", "tensor"
BOTH = (SEQ, TENSOR)
EXTRA = 8
CHUNKS = 4
MIB = 1024 * 1024


def rounded(term_value):
    return lax.optimization_barrier(term_value.astype(jnp.bfloat16)).astype(jnp.float32)


def owner_pairs(step, seq_count, tensor_count):
    pairs = []
    for s in range(seq_count):
        for t in range(tensor_count):
            z, y, c = s // 2, s % 2, t % 2
            dest_s = 2 * (z ^ step) + c
            dest_t = (t - c) + (y ^ (z & 1))
            pairs.append((s * tensor_count + t, dest_s * tensor_count + dest_t))
    return pairs


def turned(pairs):
    return [(b, a) for a, b in pairs]


def any_spec():
    return pl.BlockSpec(memory_space=pl.ANY)


def vmem_spec():
    return pl.BlockSpec(memory_space=pltpu.VMEM)


def held(value):
    return pltpu.with_memory_space_constraint(value, pltpu.HBM)


def params(mib):
    return pltpu.CompilerParams(vmem_limit_bytes=mib * MIB)


def cost(flops, moved, transcendentals=0):
    return pl.CostEstimate(
        flops=flops, bytes_accessed=moved, transcendentals=transcendentals
    )


def shape(dims, kind=jnp.bfloat16):
    return jax.ShapeDtypeStruct(dims, kind)


def out_rows(w_out, wanted, sems, width):
    z = lax.axis_index(SEQ) >> 1
    copies = []
    for part, turns, at in wanted:
        half = part.shape[1]
        cols = pl.ds(pl.multiple_of(at * half, half), half)
        for i, k in enumerate(turns):
            here = pl.ds(pl.multiple_of((z ^ k) * width, width), width)
            to = part.at[pl.ds(i * width, width), :]
            copies.append(
                pltpu.make_async_copy(w_out.at[here, cols], to, sems.at[len(copies)])
            )
    return copies


def unit_heads(normed, w_qk, w_value, outs, clusters, steps, width):
    z = lax.axis_index(SEQ) >> 1
    rows = normed.shape[0]
    span = 2 * width
    odd = (z & 1) == 1
    row_at = lax.broadcasted_iota(jnp.int32, (EXTRA, span), 0)
    key_proj = jnp.dot(normed[...], w_qk[...], preferred_element_type=jnp.float32)
    units = []
    for q in range(2):
        k = key_proj[:, q * width : (q + 1) * width]
        total = jnp.sum(k * k, axis=-1, keepdims=True)
        units.append((k * lax.rsqrt(total + NORM_EPS)).astype(jnp.bfloat16))
    val_proj = jnp.dot(normed[...], w_value[...], preferred_element_type=jnp.float32)
    values = [val_proj[:, q * width : (q + 1) * width].astype(jnp.bfloat16) for q in range(2)]
    for q, out in enumerate(outs):
        out[:rows, :width] = jnp.where(odd, units[1 - q], units[q])
        out[:rows, width:] = jnp.where(odd, values[1 - q], values[q])
        id_row = clusters[pl.ds(steps[q] ^ z, 1), :].astype(jnp.float32)
        tail = jnp.zeros((EXTRA, span), jnp.float32)
        for part in range(rows // span):
            piece = id_row[:, part * span : (part + 1) * span]
            tail = jnp.where(row_at == part, piece, tail)
        out[rows:, :] = tail.astype(jnp.bfloat16)


def project_far_body(
    tokens_at, gain_at, w_qk, w_value, clusters_at, w_out, *rest, width, stages, parts
):
    out_low, out_high, normed, clusters, qk_next, val_next, out_early = rest[:7]
    tokens, gain, qk_buf, val_buf, sems, token_sems, out_sems = rest[7:]
    z = lax.axis_index(SEQ) >> 1
    y = lax.axis_index(SEQ) & 1
    step = tokens.shape[0] // parts
    span = 2 * width
    slabs = [pl.ds(r * step, step) for r in range(parts)]
    slab_copies = [
        pltpu.make_async_copy(tokens_at.at[here, :], tokens.at[here, :], token_sems.at[r])
        for r, here in enumerate(slabs)
    ]

    def columns(block):
        return pl.ds(pl.multiple_of(block * span, span), span)

    first, second = columns(1 ^ (z >> 1)), columns(z >> 1)
    out_copies = out_rows(w_out, ((out_early, stages[0], y),), out_sems, width)
    copies = [
        pltpu.make_async_copy(gain_at, gain, sems.at[0]),
        pltpu.make_async_copy(w_qk.at[:, first], qk_buf, sems.at[1]),
        pltpu.make_async_copy(w_value.at[:, first], val_buf, sems.at[2]),
        pltpu.make_async_copy(clusters_at, clusters, sems.at[3]),
        pltpu.make_async_copy(w_qk.at[:, second], qk_next, sems.at[4]),
        pltpu.make_async_copy(w_value.at[:, second], val_next, sems.at[5]),
    ]
    for copy in (copies[0], *slab_copies, *copies[1:4], *out_copies, *copies[4:]):
        copy.start()
    copies[0].wait()
    for copy, here in zip(slab_copies, slabs):
        copy.wait()
        wide = tokens[here, :].astype(jnp.float32)
        mean = jnp.mean(wide * wide, axis=-1, keepdims=True)
        normed[here, :] = (wide * lax.rsqrt(mean + NORM_EPS) * gain[...]).astype(jnp.bfloat16)
    for copy in copies[1:4]:
        copy.wait()
    unit_heads(normed, qk_buf, val_buf, (out_low, out_high), clusters, (2, 3), width)
    for copy in copies[4:] + out_copies:
        copy.wait()


def project_far(tokens, gain, w_qk, w_value, clusters, w_out, width, stages, parts=4):
    rows, depth = tokens.shape
    message = shape((rows + EXTRA, 2 * width))
    pair = (depth, 2 * width)
    return pl.pallas_call(
        functools.partial(project_far_body, width=width, stages=stages, parts=parts),
        out_shape=(
            message,
            message,
            shape((rows, depth)),
            shape(clusters.shape, jnp.int32),
            shape(pair),
            shape(pair),
            shape((2 * width, w_out.shape[1] // 2)),
        ),
        in_specs=[any_spec()] * 6,
        out_specs=(vmem_spec(),) * 7,
        scratch_shapes=[
            pltpu.VMEM((rows, depth), jnp.bfloat16),
            pltpu.VMEM((1, depth), jnp.float32),
            pltpu.VMEM(pair, jnp.bfloat16),
            pltpu.VMEM(pair, jnp.bfloat16),
            pltpu.SemaphoreType.DMA((6,)),
            pltpu.SemaphoreType.DMA((parts,)),
            pltpu.SemaphoreType.DMA((2,)),
        ],
        compiler_params=params(20),
        cost_estimate=cost(8 * rows * depth * width, 2 * rows * depth + 12 * depth * width),
    )(*[held(a) for a in (tokens, gain.reshape(1, depth), w_qk, w_value, clusters, w_out)])


def project_near_body(
    normed, w_qk, w_value, clusters, w_up, w_out, *rest, width, late
):
    out_low, out_high, first, out_late, out_rest, sem, out_sems = rest
    y = lax.axis_index(SEQ) & 1
    wanted = ((out_late, late, y), (out_rest, late, 1 - y))
    copies = [
        pltpu.make_async_copy(w_up.at[:, pl.ds(0, first.shape[1])], first, sem),
        *out_rows(w_out, wanted, out_sems, width),
    ]
    for copy in copies:
        copy.start()
    unit_heads(normed, w_qk, w_value, (out_low, out_high), clusters, (0, 1), width)
    for copy in copies:
        copy.wait()


def project_near(normed, w_qk, w_value, clusters, w_up, w_out, width, late):
    rows, depth = normed.shape
    message = shape((rows + EXTRA, 2 * width))
    part = shape((2 * width, w_out.shape[1] // 2))
    return pl.pallas_call(
        functools.partial(project_near_body, width=width, late=late),
        out_shape=(message, message, shape((depth, w_up.shape[1] // CHUNKS)), part, part),
        in_specs=[vmem_spec()] * 4 + [any_spec()] * 2,
        out_specs=(vmem_spec(),) * 5,
        scratch_shapes=[pltpu.SemaphoreType.DMA, pltpu.SemaphoreType.DMA((4,))],
        compiler_params=params(16),
        cost_estimate=cost(8 * rows * depth * width, 2 * rows * depth + 8 * depth * width),
    )(normed, w_qk, w_value, clusters, held(w_up), held(w_out))


def chunk_copies(source, buf, sems):
    step = buf.shape[2]
    return [
        pltpu.make_async_copy(source.at[:, pl.ds((c + 1) * step, step)], buf.at[c], sems.at[c])
        for c in range(CHUNKS - 1)
    ]


def up_body(normed, first, w_up, w_down, hidden, next_first, others, sems, next_sem):
    step = first.shape[1]
    copies = chunk_copies(w_up, others, sems)
    later = pltpu.make_async_copy(
        w_down.at[:, pl.ds(0, next_first.shape[1])], next_first, next_sem
    )
    for copy in (*copies, later):
        copy.start()
    for c in range(CHUNKS):
        if c:
            copies[c - 1].wait()
        weights = others[c - 1] if c else first[...]
        grown = jnp.dot(normed[...], weights, preferred_element_type=jnp.float32)
        hidden[:, c * step : (c + 1) * step] = jnp.maximum(grown, 0.0).astype(jnp.bfloat16)
    later.wait()


def up(normed, first, w_up, w_down):
    rows, depth = normed.shape
    units = w_up.shape[1]
    return pl.pallas_call(
        up_body,
        out_shape=(shape((rows, units)), shape((units, w_down.shape[1] // CHUNKS))),
        in_specs=[vmem_spec(), vmem_spec(), any_spec(), any_spec()],
        out_specs=(vmem_spec(), vmem_spec()),
        scratch_shapes=[
            pltpu.VMEM((CHUNKS - 1, depth, units // CHUNKS), jnp.bfloat16),
            pltpu.SemaphoreType.DMA((CHUNKS - 1,)),
            pltpu.SemaphoreType.DMA,
        ],
        compiler_params=params(24),
        cost_estimate=cost(2 * rows * depth * units, 2 * depth * units + 4 * rows * depth),
    )(normed, first, held(w_up), held(w_down))


def down_body(hidden, first, w_down, mine, far, away, others, held_rows, sems, *, share):
    at = lax.axis_index(TENSOR)
    step = first.shape[1]
    copies = chunk_copies(w_down, others, sems)
    for copy in copies:
        copy.start()

    def quarter(turn):
        return held_rows[pl.ds(pl.multiple_of((at ^ turn) * share, share), share), :]

    for c in range(CHUNKS):
        if c:
            copies[c - 1].wait()
        weights = others[c - 1] if c else first[...]
        cols = slice(c * step, (c + 1) * step)
        held_rows[...] = jnp.dot(hidden[...], weights, preferred_element_type=jnp.float32)
        mine[:, cols] = quarter(0)
        far[:, cols] = quarter(2)
        away[0, :, cols] = quarter(1).astype(jnp.bfloat16)
        away[1, :, cols] = quarter(3).astype(jnp.bfloat16)


def down(hidden, first, w_down, share):
    rows, units = hidden.shape
    depth = w_down.shape[1]
    return pl.pallas_call(
        functools.partial(down_body, share=share),
        out_shape=(
            shape((share, depth), jnp.float32),
            shape((share, depth), jnp.float32),
            shape((2, share, depth)),
        ),
        in_specs=[vmem_spec(), vmem_spec(), any_spec()],
        out_specs=(vmem_spec(),) * 3,
        scratch_shapes=[
            pltpu.VMEM((CHUNKS - 1, units, depth // CHUNKS), jnp.bfloat16),
            pltpu.VMEM((rows, depth // CHUNKS), jnp.float32),
            pltpu.SemaphoreType.DMA((CHUNKS - 1,)),
        ],
        compiler_params=params(24),
        cost_estimate=cost(2 * rows * depth * units, 2 * depth * units + 6 * rows * depth),
    )(hidden, first, held(w_down))


def pick_body(far, got, sent):
    sent[...] = (far[...] + got[1].astype(jnp.float32)).astype(jnp.bfloat16)


def pick(far, got):
    return pl.pallas_call(
        pick_body,
        out_shape=shape(far.shape),
        in_specs=[vmem_spec(), vmem_spec()],
        out_specs=vmem_spec(),
        compiler_params=params(6),
        cost_estimate=cost(far.size, far.size * 8),
    )(far, got)


def block_of(b, heads):
    z = lax.axis_index(SEQ) >> 1
    core = lax.axis_index(TENSOR) % 2
    pair = z ^ (b % heads)
    return 2 * pair + (core ^ (pair & 1) ^ (b // heads))


def attend_body(*refs, heads, width, owned, steps, first):
    if first:
        own, other = refs[:heads], refs[heads : 2 * heads]
        refs = refs[2 * heads :]
        outs = refs[: len(steps)]
        kv, id_rows = refs[len(steps) : len(steps) + 2]
        query, id_cols, acc, den = refs[len(steps) + 2 :]
        rows = kv.shape[1]
        for b, source in enumerate(list(own) + list(other)):
            kv[b] = source[:rows, :]
            tile = source[rows:, :].astype(jnp.float32)
            id_row = jnp.concatenate(
                [tile[r : r + 1, :] for r in range(rows // (2 * width))], axis=1
            )
            id_rows[b] = jnp.broadcast_to(id_row, (8, rows))
    else:
        kv, id_rows = refs[:2]
        outs = refs[2 : 2 + len(steps)]
        query, id_cols, acc, den = refs[2 + len(steps) :]
        rows = kv.shape[1]

    count = 2 * heads
    cluster_col = lax.broadcasted_iota(jnp.int32, (owned, rows), 0)
    wanted = jnp.concatenate(
        [cluster_col + owned * block_of(k, heads) for k in steps], axis=0
    ).astype(jnp.float32)
    sums = jnp.zeros((len(steps) * owned, width), jnp.float32)
    for b in range(count):
        one_hot = jnp.where(wanted == id_rows[b, :1, :], 1.0, 0.0).astype(jnp.bfloat16)
        sums = sums + jnp.dot(one_hot, kv[b, :, :width], preferred_element_type=jnp.float32)

    def pair(blocks, masked):
        spread = jnp.concatenate([id_cols[...]] * (rows // width), axis=1)
        shares, mixes = [], []
        for b in blocks:
            score = lax.dot_general(
                query[...],
                kv[b, :, :width],
                (((1,), (1,)), ((), ())),
                preferred_element_type=jnp.float32,
            )
            weight = jnp.exp(score)
            same = spread == id_rows[b, :1, :]
            if masked:
                row_at = lax.broadcasted_iota(jnp.int32, weight.shape, 0)
                col_at = lax.broadcasted_iota(jnp.int32, weight.shape, 1)
                same = jnp.logical_and(same, col_at <= row_at)
            weight = jnp.where(same, weight, 0.0)
            shares += [
                weight[:, part * width : (part + 1) * width] for part in range(rows // width)
            ]
            mixes.append(
                jnp.dot(
                    weight.astype(jnp.bfloat16),
                    kv[b, :, width:],
                    preferred_element_type=jnp.float32,
                )
            )
        if masked:
            den[...], acc[...] = sum(shares[1:], shares[0]), sum(mixes[1:], mixes[0])
        else:
            den[...] += sum(shares[1:], shares[0])
            acc[...] += sum(mixes[1:], mixes[0])

    z = lax.axis_index(SEQ) >> 1
    for at, k in enumerate(steps):
        query[...] = kv[k, :, :width] * jnp.bfloat16(SCORE_SCALE)
        for part in range(rows // width):
            here = pl.ds(part * width, width)
            id_cols[here, :] = jnp.transpose(
                jnp.broadcast_to(id_rows[k, :1, part * width : (part + 1) * width], (width, width))
            )
        pair((k,), True)

        @pl.when(block_of(k + heads, heads) < block_of(k, heads))
        def _():
            pair((k + heads,), False)

        def per_pair(turn, carry):
            b = k ^ turn

            @pl.when((z ^ b) < (z ^ k))
            def _():
                pair((b, b + heads), False)

            return carry

        lax.fori_loop(1, heads, per_pair, 0)
        out = outs[at]
        whole = jnp.sum(den[...], axis=-1, keepdims=True)
        out[:rows, :] = (acc[...] / whole).astype(jnp.bfloat16)
        out[rows:, :] = sums[at * owned : (at + 1) * owned].astype(jnp.bfloat16)


def attend(inputs, heads, rows, width, owned, steps, first):
    result = shape((rows + owned, width))
    out_shape = (result,) * len(steps)
    if first:
        out_shape += (
            shape((2 * heads, rows, 2 * width)),
            shape((2 * heads, 8, rows), jnp.float32),
        )
    units = (heads * heads + heads // 2) * len(steps) // heads
    return pl.pallas_call(
        functools.partial(
            attend_body, heads=heads, width=width, owned=owned, steps=steps, first=first
        ),
        out_shape=out_shape,
        in_specs=[vmem_spec()] * len(inputs),
        out_specs=(vmem_spec(),) * len(out_shape),
        scratch_shapes=[
            pltpu.VMEM((rows, width), jnp.bfloat16),
            pltpu.VMEM((rows, width), jnp.float32),
            pltpu.VMEM((rows, width), jnp.float32),
            pltpu.VMEM((rows, width), jnp.float32),
        ],
        compiler_params=params(20),
        cost_estimate=cost(
            units * rows * rows * width * 8,
            2 * heads * rows * width * 4,
            units * rows * rows,
        ),
    )(*inputs)


def cut_body(*refs, count, share):
    back, kept, away, sums = refs[:count], refs[count], refs[count + 1 : -1], refs[-1]
    at = lax.axis_index(TENSOR)
    for k in range(count):
        for turn in range(len(away) + 1):
            here = pl.ds(pl.multiple_of((at ^ turn) * share, share), share)
            (kept if turn == 0 else away[turn - 1])[k] = back[k][here, :]
        rows = back[k].shape[0] - sums.shape[1]
        sums[k] = back[k][rows:, :].astype(jnp.float32)


def cut(back, owned, share, tensor_count):
    count, width = len(back), back[0].shape[1]
    piece = shape((count, share, width))
    return pl.pallas_call(
        functools.partial(cut_body, count=count, share=share),
        out_shape=(piece,) * tensor_count + (shape((count, owned, width), jnp.float32),),
        in_specs=[vmem_spec()] * count,
        out_specs=(vmem_spec(),) * (tensor_count + 1),
        compiler_params=params(8),
        cost_estimate=cost(0, 4 * count * tensor_count * share * width),
    )(*back)


def head_rows(weights, buf, sems, steps, width):
    z = lax.axis_index(SEQ) >> 1
    copies = []
    for g, w in enumerate(weights):
        for i, k in enumerate(steps):
            here = pl.ds(pl.multiple_of((z ^ k) * width, width), width)
            to = pl.ds((g * len(steps) + i) * width, width)
            copies.append(
                pltpu.make_async_copy(w.at[here, :], buf.at[to, :], sems.at[len(copies)])
            )
    return copies


def side_by_side(pieces, count):
    return jnp.concatenate([p[k] for p in pieces for k in range(count)], axis=1)


def products(pieces, count, near_rows, far_halves, known, put):
    y = lax.axis_index(SEQ) & 1
    half = far_halves[0].shape[1]
    near = side_by_side(pieces[:2], count)
    same, cross = side_by_side(pieces[2:3], count), side_by_side(pieces[3:4], count)
    for turn in range(2):
        cols = pl.ds(pl.multiple_of((y ^ turn) * half, half), half)
        total = known(cols)
        for left, rows in (
            (near, near_rows[:, cols]),
            (same, far_halves[turn][...]),
            (cross, far_halves[2 + turn][...]),
        ):
            total = total + jnp.dot(left, rows, preferred_element_type=jnp.float32)
        put(cols, total)


def mix_first_body(*refs, groups, width, steps, later):
    pieces, weights = refs[:groups], refs[groups : groups + 2]
    far_halves = refs[groups + 2 : groups + 6]
    tokens, mine, got, total, kept, buf, sems, later_sems = refs[groups + 6 :]
    now = head_rows(weights, buf, sems, steps, width)
    then = head_rows(weights, kept, later_sems, later, width)
    for copy in now + then:
        copy.start()
    share = total.shape[0]
    at = lax.axis_index(TENSOR)
    here = pl.ds(pl.multiple_of(at * share, share), share)
    for copy in now:
        copy.wait()

    def known(cols):
        base = tokens[here, cols].astype(jnp.float32) + mine[:, cols]
        return base + got[0, :, cols].astype(jnp.float32)

    def put(cols, value):
        total[:, cols] = value

    products(pieces, len(steps), buf, far_halves, known, put)
    for copy in then:
        copy.wait()


def mix_first(pieces, weights, far_halves, tokens, mine, got, steps, later):
    groups = len(pieces)
    count, share, width = pieces[0].shape
    depth = tokens.shape[1]
    rows = (2 * count * width, depth)
    return pl.pallas_call(
        functools.partial(
            mix_first_body, groups=groups, width=width, steps=steps, later=later
        ),
        out_shape=(shape((share, depth), jnp.float32), shape(rows)),
        in_specs=[vmem_spec()] * groups + [any_spec()] * 2 + [vmem_spec()] * 7,
        out_specs=(vmem_spec(), vmem_spec()),
        scratch_shapes=[
            pltpu.VMEM(rows, jnp.bfloat16),
            pltpu.SemaphoreType.DMA((2 * count,)),
            pltpu.SemaphoreType.DMA((2 * count,)),
        ],
        compiler_params=params(20),
        cost_estimate=cost(
            2 * groups * share * count * width * depth,
            4 * groups * count * width * depth + 8 * share * depth,
        ),
    )(*pieces, *weights, *far_halves, tokens, mine, got)


def mix_last_body(*refs, groups, steps, later):
    pieces, far_halves = refs[:groups], refs[groups : groups + 4]
    total, kept, came, first_sums, last_sums, centroids, out, updated = refs[groups + 4 :]
    z = lax.axis_index(SEQ) >> 1

    def known(cols):
        return total[:, cols] + came[:, cols].astype(jnp.float32)

    def put(cols, value):
        out[:, cols] = value.astype(jnp.bfloat16)

    products(pieces, len(later), kept, far_halves, known, put)
    for sums, turns in ((first_sums, steps), (last_sums, later)):
        for i, k in enumerate(turns):
            head = z ^ k
            updated[head] = EMA_DECAY * centroids[head] + (1.0 - EMA_DECAY) * sums[i]


def mix_last(
    pieces, far_halves, total, kept, came, first_sums, last_sums, centroids, steps, later
):
    groups = len(pieces)
    share, depth = total.shape
    return pl.pallas_call(
        functools.partial(mix_last_body, groups=groups, steps=steps, later=later),
        out_shape=(shape((share, depth)), shape(centroids.shape, jnp.float32)),
        in_specs=[vmem_spec()] * (groups + 10),
        out_specs=(vmem_spec(), vmem_spec()),
        compiler_params=params(16),
        cost_estimate=cost(4 * kept.size * share, 4 * kept.size + 8 * share * depth),
    )(*pieces, *far_halves, total, kept, came, first_sums, last_sums, centroids)


def by_heads(
    tokens, norm_gain, w_qk, w_value, w_out, w_up, w_down, centroids, clusters, slots
):
    tok_rows, _ = tokens.shape
    seq_count = lax.axis_size(SEQ)
    tensor_count = lax.axis_size(TENSOR)
    heads = clusters.shape[0]
    owned = centroids.shape[1]
    width = w_qk.shape[1] // heads
    share = tok_rows // tensor_count
    swaps = [None] + [[(t, t ^ d) for t in range(tensor_count)] for d in range(1, tensor_count)]

    w_core = lax.ppermute(w_out, TENSOR, swaps[1])
    steps = [owner_pairs(k, seq_count, tensor_count) for k in range(heads)]
    swap_y = [(s, s ^ 1) for s in range(seq_count)]
    messages, own, other = [None] * heads, [None] * heads, [None] * heads
    early, late = (heads - 1, 0), (heads - 2, 1)
    messages[2], messages[3], normed, ids, qk_next, val_next, out_early = project_far(
        tokens, norm_gain, w_qk, w_value, clusters, w_out, width, (early, late)
    )
    for k in (3, 2):
        own[k] = lax.ppermute(messages[k], BOTH, steps[k])
    fx_early = lax.ppermute(out_early, TENSOR, swaps[2])
    messages[0], messages[1], up_first, out_late, out_rest = project_near(
        normed, qk_next, val_next, ids, w_up, w_out, width, late
    )
    halves = {
        "e": [fx_early, lax.ppermute(fx_early, SEQ, swap_y)],
        "l": [lax.ppermute(out_late, TENSOR, swaps[2]), lax.ppermute(out_rest, TENSOR, swaps[2])],
    }
    for pair in halves.values():
        pair += [lax.ppermute(w, TENSOR, swaps[1]) for w in (pair[0], pair[1])]
    for k in (1, 0):
        own[k] = lax.ppermute(messages[k], BOTH, steps[k])
    hidden, down_first = up(normed, up_first, w_up, w_down)
    mine, far, sent = down(hidden, down_first, w_down, share)
    got = lax.ppermute(sent, TENSOR, swaps[1])
    for k in range(heads):
        other[k] = lax.ppermute(own[k], TENSOR, swaps[1])
    picked = pick(far, got)
    came = lax.ppermute(picked, TENSOR, swaps[2])
    back, pieces, sums = [None] * heads, {}, {}
    *results, kv, id_rows = attend(
        own + other, heads, tok_rows, width, owned, early, True
    )
    for k, result in zip(early, results):
        back[k] = lax.ppermute(result, BOTH, turned(steps[k]))
    results = attend([kv, id_rows], heads, tok_rows, width, owned, late, False)
    for k, result in zip(late, results):
        back[k] = lax.ppermute(result, BOTH, turned(steps[k]))

    for name, turns in (("e", early), ("l", late)):
        kept, *away, sums[name] = cut([back[k] for k in turns], owned, share, tensor_count)
        pieces[name] = [kept] + [
            lax.ppermute(away[d - 1], TENSOR, swaps[d])
            for d in range(1, tensor_count)
        ]
    total, late_rows = mix_first(
        pieces["e"], [held(w_out), w_core], halves["e"], tokens, mine, got, early, late
    )
    mixed_rows, new_centroids = mix_last(
        pieces["l"], halves["l"], total, late_rows, came, sums["e"], sums["l"],
        centroids, early, late,
    )
    return (mixed_rows, new_centroids)


def by_clusters(tokens, norm_gain, w_qk, w_value, w_out, w_up, w_down, centroids, clusters, slots):
    tok_rows = tokens.shape[0]
    seq_count = lax.axis_size(SEQ)
    tensor_count = lax.axis_size(TENSOR)
    heads_here = clusters.shape[0]
    owned_count = centroids.shape[1]
    head_width = w_qk.shape[1] // heads_here
    share_rows = tok_rows // tensor_count
    row_first = lax.axis_index(TENSOR) * share_rows
    tokens_wide = tokens.astype(jnp.float32)
    normed = (
        tokens_wide
        * lax.rsqrt(jnp.mean(tokens_wide * tokens_wide, axis=-1, keepdims=True) + NORM_EPS)
        * norm_gain
    ).astype(jnp.bfloat16)
    key_proj = jnp.dot(normed, w_qk, preferred_element_type=jnp.float32).reshape(
        tok_rows, heads_here, head_width
    )
    key_unit = (
        key_proj * lax.rsqrt(jnp.sum(key_proj * key_proj, axis=-1, keepdims=True) + NORM_EPS)
    ).astype(jnp.bfloat16)
    val_proj = (
        jnp.dot(normed, w_value, preferred_element_type=jnp.float32)
        .astype(jnp.bfloat16)
        .reshape(tok_rows, heads_here, head_width)
    )
    positions = lax.axis_index(SEQ) * tok_rows + jnp.arange(tok_rows, dtype=jnp.int32)
    pos_high = (positions // 256).astype(jnp.float32).astype(jnp.bfloat16)
    pos_low = (positions % 256).astype(jnp.float32).astype(jnp.bfloat16)
    flat_slot = clusters.T * CAP + slots.T
    head_grid = jnp.broadcast_to(jnp.arange(heads_here, dtype=jnp.int32)[None, :], flat_slot.shape)
    slot_total = CLUSTERS * CAP
    layout = (heads_here, seq_count, owned_count, CAP)
    key_buf = (
        jnp.zeros((heads_here, slot_total, head_width), jnp.bfloat16)
        .at[head_grid, flat_slot]
        .set(key_unit)
        .reshape(layout + (head_width,))
    )
    val_buf = (
        jnp.zeros((heads_here, slot_total, head_width), jnp.bfloat16)
        .at[head_grid, flat_slot]
        .set(val_proj)
        .reshape(layout + (head_width,))
    )
    high_buf = (
        jnp.full((heads_here, slot_total), 256.0, jnp.bfloat16)
        .at[head_grid, flat_slot]
        .set(jnp.broadcast_to(pos_high[:, None], flat_slot.shape))
        .reshape(layout)
    )
    low_buf = (
        jnp.zeros((heads_here, slot_total), jnp.bfloat16)
        .at[head_grid, flat_slot]
        .set(jnp.broadcast_to(pos_low[:, None], flat_slot.shape))
        .reshape(layout)
    )
    key_in = lax.all_to_all(key_buf, SEQ, split_axis=1, concat_axis=1, tiled=True)
    val_in = lax.all_to_all(val_buf, SEQ, split_axis=1, concat_axis=1, tiled=True)
    high_in = lax.all_to_all(high_buf, SEQ, split_axis=1, concat_axis=1, tiled=True)
    low_in = lax.all_to_all(low_buf, SEQ, split_axis=1, concat_axis=1, tiled=True)
    scores = (
        jnp.einsum("hskad,htkbd->hksatb", key_in, key_in, preferred_element_type=jnp.float32)
        * SCORE_SCALE
    )
    key_place = high_in.astype(jnp.float32) * 256.0 + low_in.astype(jnp.float32)
    ordered = jnp.transpose(key_place, (0, 2, 1, 3))
    causal = ordered[:, :, None, None, :, :] <= ordered[:, :, :, :, None, None]
    exponent = jnp.where(causal, jnp.exp(scores), 0.0)
    weights = (exponent / jnp.sum(exponent, axis=(4, 5), keepdims=True)).astype(jnp.bfloat16)
    mixed_out = jnp.einsum(
        "hksatb,htkbd->hskad", weights, val_in, preferred_element_type=jnp.float32
    ).astype(jnp.bfloat16)
    returned_back = lax.all_to_all(mixed_out, SEQ, split_axis=1, concat_axis=1, tiled=True)
    one_hot = (clusters[:, :, None] == jnp.arange(CLUSTERS, dtype=jnp.int32)[None, None, :]).astype(
        jnp.bfloat16
    )
    local_sums = jnp.einsum("htk,thd->hkd", one_hot, key_unit, preferred_element_type=jnp.float32)
    totals = lax.psum_scatter(
        local_sums.astype(jnp.bfloat16), SEQ, scatter_dimension=1, tiled=True
    ).astype(jnp.float32)
    new_centroids = EMA_DECAY * centroids + (1.0 - EMA_DECAY) * totals
    returned = returned_back.reshape(heads_here, slot_total, head_width)
    attended = returned[head_grid, flat_slot].reshape(tok_rows, heads_here * head_width)
    attn_part = jnp.dot(attended, w_out, preferred_element_type=jnp.float32)
    hidden = jax.nn.relu(jnp.dot(normed, w_up, preferred_element_type=jnp.float32)).astype(
        jnp.bfloat16
    )
    ffn_part = jnp.dot(hidden, w_down, preferred_element_type=jnp.float32)
    summed = lax.psum_scatter(
        rounded(attn_part + ffn_part).astype(jnp.bfloat16),
        TENSOR,
        scatter_dimension=0,
        tiled=True,
    ).astype(jnp.float32)
    own_rows = lax.dynamic_slice_in_dim(tokens_wide, row_first, share_rows, 0)
    mixed_rows = (own_rows + summed).astype(jnp.bfloat16)
    return (mixed_rows, new_centroids)


def solution(mesh):
    in_specs = (
        P(SEQ, None),
        P(),
        P(None, TENSOR),
        P(None, TENSOR),
        P(TENSOR, None),
        P(None, TENSOR),
        P(TENSOR, None),
        P(TENSOR, SEQ, None),
        P(TENSOR, SEQ),
        P(TENSOR, SEQ),
    )
    out_specs = (P((SEQ, TENSOR), None), P(TENSOR, SEQ, None))
    sizes = dict(mesh.shape)

    def local(*args):
        heads = args[8].shape[0]
        fits = (
            sizes[TENSOR] == 4
            and sizes[SEQ] == 2 * heads
            and heads & (heads - 1) == 0
            and heads == 4
        )
        if not fits:
            return by_clusters(*args)
        return by_heads(*args)

    return jax.shard_map(
        local, mesh=mesh, in_specs=in_specs, out_specs=out_specs, check_vma=False
    )
```

```python
import functools

import jax
import jax.numpy as jnp
from jax import lax
from jax.experimental import pallas as pl
from jax.experimental.pallas import tpu as pltpu
from jax.sharding import PartitionSpec as P


CLUSTERS = 256
CAP = 4

SCORE_SCALE = 2.0
EMA_DECAY = 0.9
NORM_EPS = 1e-06
SEQ, TENSOR = "seq", "tensor"
BOTH = (SEQ, TENSOR)
EXTRA = 16
MIB = 1024 * 1024


def rounded(term_value):
    return lax.optimization_barrier(term_value.astype(jnp.bfloat16)).astype(jnp.float32)


def owner_pairs(step, seq_count, tensor_count):
    pairs = []
    for s in range(seq_count):
        for t in range(tensor_count):
            z, y, c = s // 2, s % 2, t % 2
            dest_s = 2 * (z ^ step) + c
            dest_t = (t - c) + (y ^ (z & 1))
            pairs.append((s * tensor_count + t, dest_s * tensor_count + dest_t))
    return pairs


def turned(pairs):
    return [(b, a) for a, b in pairs]


def any_spec():
    return pl.BlockSpec(memory_space=pl.ANY)


def vmem_spec():
    return pl.BlockSpec(memory_space=pltpu.VMEM)


def held(value):
    return pltpu.with_memory_space_constraint(value, pltpu.HBM)


def params(mib):
    return pltpu.CompilerParams(vmem_limit_bytes=mib * MIB)


def cost(flops, moved, transcendentals=0):
    return pl.CostEstimate(
        flops=flops, bytes_accessed=moved, transcendentals=transcendentals
    )


def shape(dims, kind=jnp.bfloat16):
    return jax.ShapeDtypeStruct(dims, kind)


def unit_rows(normed, w_qk, w_value, outs, width, here):
    odd = ((lax.axis_index(SEQ) >> 1) & 1) == 1
    key_proj = jnp.dot(normed[here, :], w_qk[...], preferred_element_type=jnp.float32)
    units = []
    for q in range(2):
        k = key_proj[:, q * width : (q + 1) * width]
        total = jnp.sum(k * k, axis=-1, keepdims=True)
        units.append((k * lax.rsqrt(total + NORM_EPS)).astype(jnp.bfloat16))
    val_proj = jnp.dot(normed[here, :], w_value[...], preferred_element_type=jnp.float32)
    values = [val_proj[:, q * width : (q + 1) * width].astype(jnp.bfloat16) for q in range(2)]
    for q, out in enumerate(outs):
        out[here, :width] = jnp.where(odd, units[1 - q], units[q])
        out[here, width:] = jnp.where(odd, values[1 - q], values[q])


def id_tails(outs, clusters, steps, rows, width):
    z = lax.axis_index(SEQ) >> 1
    span = 2 * width
    row_at = lax.broadcasted_iota(jnp.int32, (EXTRA, span), 0)
    for q, out in enumerate(outs):
        id_row = clusters[pl.ds(steps[q] ^ z, 1), :].astype(jnp.float32)
        tail = jnp.zeros((EXTRA, span), jnp.float32)
        for part in range(rows // span):
            piece = id_row[:, part * span : (part + 1) * span]
            tail = jnp.where(row_at == part, piece, tail)
        out[rows:, :] = tail.astype(jnp.bfloat16)


def project_far_body(
    tokens_at, gain_at, w_qk, w_value, clusters_at, w_out, w_up, *rest, width, stages, parts
):
    out_low, out_high, normed, clusters, qk_next, val_next, out_early, out_late, out_rest, up_part = rest[:10]
    tokens, gain, qk_buf, val_buf, sems, token_sems, out_sems = rest[10:]
    z = lax.axis_index(SEQ) >> 1
    y = lax.axis_index(SEQ) & 1
    step = tokens.shape[0] // parts
    span = 2 * width
    slabs = [pl.ds(r * step, step) for r in range(parts)]
    slab_copies = [
        pltpu.make_async_copy(tokens_at.at[here, :], tokens.at[here, :], token_sems.at[r])
        for r, here in enumerate(slabs)
    ]

    def columns(block):
        return pl.ds(pl.multiple_of(block * span, span), span)

    first, second = columns(1 ^ (z >> 1)), columns(z >> 1)
    half = out_early.shape[1]
    out_copies = []
    for part, turns, at in (
        (out_early, stages[0], y),
        (out_late, stages[1], y),
        (out_rest, stages[1], 1 - y),
    ):
        out_cols = pl.ds(pl.multiple_of(at * half, half), half)
        for i, k in enumerate(turns):
            here = pl.ds(pl.multiple_of((z ^ k) * width, width), width)
            out_copies.append(
                pltpu.make_async_copy(
                    w_out.at[here, out_cols],
                    part.at[pl.ds(i * width, width), :],
                    out_sems.at[len(out_copies)],
                )
            )
    copies = [
        pltpu.make_async_copy(gain_at, gain, sems.at[0]),
        pltpu.make_async_copy(w_qk.at[:, first], qk_buf, sems.at[1]),
        pltpu.make_async_copy(w_value.at[:, first], val_buf, sems.at[2]),
        pltpu.make_async_copy(clusters_at, clusters, sems.at[3]),
        pltpu.make_async_copy(w_qk.at[:, second], qk_next, sems.at[4]),
        pltpu.make_async_copy(w_value.at[:, second], val_next, sems.at[5]),
        pltpu.make_async_copy(w_up.at[:, pl.ds(0, up_part.shape[1])], up_part, sems.at[6]),
    ]
    for copy in (copies[0], *slab_copies, *copies[1:4], *out_copies, *copies[4:]):
        copy.start()
    copies[0].wait()
    half_rows = tokens.shape[0] // 2
    row_halves = [pl.ds(h * half_rows, half_rows) for h in range(2)]

    def normalize(h):
        here = row_halves[h]
        wide = tokens[here, :].astype(jnp.float32)
        mean = jnp.mean(wide * wide, axis=-1, keepdims=True)
        normed[here, :] = (wide * lax.rsqrt(mean + NORM_EPS) * gain[...]).astype(jnp.bfloat16)

    for copy in slab_copies[: parts // 2]:
        copy.wait()
    normalize(0)
    for copy in slab_copies[parts // 2 :] + copies[1:4]:
        copy.wait()
    outs = (out_low, out_high)
    unit_rows(normed, qk_buf, val_buf, outs, width, row_halves[0])
    normalize(1)
    unit_rows(normed, qk_buf, val_buf, outs, width, row_halves[1])
    id_tails(outs, clusters, (2, 3), tokens.shape[0], width)
    for copy in copies[4:] + out_copies:
        copy.wait()


def project_far(tokens, gain, w_qk, w_value, clusters, w_out, w_up, width, stages, parts=4):
    rows, depth = tokens.shape
    message = shape((rows + EXTRA, 2 * width))
    pair = (depth, 2 * width)
    return pl.pallas_call(
        functools.partial(project_far_body, width=width, stages=stages, parts=parts),
        out_shape=(
            message,
            message,
            shape((rows, depth)),
            shape(clusters.shape, jnp.int32),
            shape(pair),
            shape(pair),
            shape((2 * width, w_out.shape[1] // 2)),
            shape((2 * width, w_out.shape[1] // 2)),
            shape((2 * width, w_out.shape[1] // 2)),
            shape((depth, w_up.shape[1] // 4)),
        ),
        in_specs=[any_spec()] * 7,
        out_specs=(vmem_spec(),) * 10,
        scratch_shapes=[
            pltpu.VMEM((rows, depth), jnp.bfloat16),
            pltpu.VMEM((1, depth), jnp.float32),
            pltpu.VMEM(pair, jnp.bfloat16),
            pltpu.VMEM(pair, jnp.bfloat16),
            pltpu.SemaphoreType.DMA((7,)),
            pltpu.SemaphoreType.DMA((parts,)),
            pltpu.SemaphoreType.DMA((6,)),
        ],
        compiler_params=params(20),
        cost_estimate=cost(8 * rows * depth * width, 2 * rows * depth + 12 * depth * width),
    )(*[held(a) for a in (tokens, gain.reshape(1, depth), w_qk, w_value, clusters, w_out, w_up)])


def project_near_body(
    normed, w_qk, w_value, clusters, w_up, out_low, out_high, next_part, sem, *, width
):
    step = next_part.shape[1]
    copy = pltpu.make_async_copy(w_up.at[:, pl.ds(step, step)], next_part, sem)
    copy.start()
    rows = normed.shape[0]
    outs = (out_low, out_high)
    unit_rows(normed, w_qk, w_value, outs, width, pl.ds(0, rows))
    id_tails(outs, clusters, (0, 1), rows, width)
    copy.wait()


def project_near(normed, w_qk, w_value, clusters, w_up, width):
    rows, depth = normed.shape
    message = shape((rows + EXTRA, 2 * width))
    return pl.pallas_call(
        functools.partial(project_near_body, width=width),
        out_shape=(message, message, shape((depth, w_up.shape[1] // 4))),
        in_specs=[vmem_spec()] * 4 + [any_spec()],
        out_specs=(vmem_spec(),) * 3,
        scratch_shapes=[pltpu.SemaphoreType.DMA],
        compiler_params=params(16),
        cost_estimate=cost(8 * rows * depth * width, 2 * rows * depth + 8 * depth * width),
    )(normed, w_qk, w_value, clusters, held(w_up))


def up_body(normed, first, next_to, w_up, w_down, hidden, next_half, second, sems):
    step, half = first.shape[1], 2 * first.shape[1]
    copies = (
        pltpu.make_async_copy(w_up.at[:, pl.ds(half, half)], second, sems.at[0]),
        pltpu.make_async_copy(
            w_down.at[:, pl.ds(0, next_half.shape[1])], next_half, sems.at[1]
        ),
    )
    for copy in copies:
        copy.start()
    for at, weights in ((0, first), (step, next_to), (half, second)):
        if at == half:
            copies[0].wait()
        grown = jnp.dot(normed[...], weights[...], preferred_element_type=jnp.float32)
        cols = slice(at, at + weights.shape[1])
        hidden[:, cols] = jnp.maximum(grown, 0.0).astype(jnp.bfloat16)
    copies[1].wait()


def up(normed, first, next_to, w_up, w_down):
    rows, depth = normed.shape
    units = w_up.shape[1]
    return pl.pallas_call(
        up_body,
        out_shape=(shape((rows, units)), shape((units, w_down.shape[1] // 2))),
        in_specs=[vmem_spec()] * 3 + [any_spec()] * 2,
        out_specs=(vmem_spec(), vmem_spec()),
        scratch_shapes=[
            pltpu.VMEM((depth, units // 2), jnp.bfloat16),
            pltpu.SemaphoreType.DMA((2,)),
        ],
        compiler_params=params(24),
        cost_estimate=cost(2 * rows * depth * units, 2 * depth * units + 4 * rows * depth),
    )(normed, first, next_to, held(w_up), held(w_down))


def down_body(hidden, first, w_down, mine, far, away, second, held_rows, sem, *, share):
    at = lax.axis_index(TENSOR)
    half = first.shape[1]
    copy = pltpu.make_async_copy(w_down.at[:, pl.ds(half, half)], second, sem)
    copy.start()

    def quarter(turn):
        return held_rows[pl.ds(pl.multiple_of((at ^ turn) * share, share), share), :]

    for part, weights in enumerate((first, second)):
        if part == 1:
            copy.wait()
        cols = slice(part * half, (part + 1) * half)
        held_rows[...] = jnp.dot(
            hidden[...], weights[...], preferred_element_type=jnp.float32
        )
        mine[:, cols] = quarter(0)
        far[:, cols] = quarter(2)
        away[0, :, cols] = quarter(1).astype(jnp.bfloat16)
        away[1, :, cols] = quarter(3).astype(jnp.bfloat16)


def down(hidden, first, w_down, share):
    rows, units = hidden.shape
    depth = w_down.shape[1]
    return pl.pallas_call(
        functools.partial(down_body, share=share),
        out_shape=(
            shape((share, depth), jnp.float32),
            shape((share, depth), jnp.float32),
            shape((2, share, depth)),
        ),
        in_specs=[vmem_spec(), vmem_spec(), any_spec()],
        out_specs=(vmem_spec(),) * 3,
        scratch_shapes=[
            pltpu.VMEM((units, depth // 2), jnp.bfloat16),
            pltpu.VMEM((rows, depth // 2), jnp.float32),
            pltpu.SemaphoreType.DMA,
        ],
        compiler_params=params(24),
        cost_estimate=cost(2 * rows * depth * units, 2 * depth * units + 6 * rows * depth),
    )(hidden, first, held(w_down))


def pick_body(far, got, sent):
    sent[...] = (far[...] + got[1].astype(jnp.float32)).astype(jnp.bfloat16)


def pick(far, got):
    return pl.pallas_call(
        pick_body,
        out_shape=shape(far.shape),
        in_specs=[vmem_spec(), vmem_spec()],
        out_specs=vmem_spec(),
        compiler_params=params(6),
        cost_estimate=cost(far.size, far.size * 8),
    )(far, got)


def block_of(b, heads):
    z = lax.axis_index(SEQ) >> 1
    core = lax.axis_index(TENSOR) % 2
    pair = z ^ (b % heads)
    return 2 * pair + (core ^ (pair & 1) ^ (b // heads))


def attend_body(*refs, heads, width, owned, steps, first):
    if first:
        own, other = refs[:heads], refs[heads : 2 * heads]
        refs = refs[2 * heads :]
        outs = refs[: len(steps)]
        kv, id_rows = refs[len(steps) : len(steps) + 2]
        query, id_cols, acc, den = refs[len(steps) + 2 :]
        rows = kv.shape[1]
        for b, source in enumerate(list(own) + list(other)):
            kv[b] = source[:rows, :]
            tile = source[rows:, :].astype(jnp.float32)
            id_row = jnp.concatenate(
                [tile[r : r + 1, :] for r in range(rows // (2 * width))], axis=1
            )
            id_rows[b] = jnp.broadcast_to(id_row, (8, rows))
    else:
        kv, id_rows = refs[:2]
        outs = refs[2 : 2 + len(steps)]
        query, id_cols, acc, den = refs[2 + len(steps) :]
        rows = kv.shape[1]

    count = 2 * heads
    cluster_col = lax.broadcasted_iota(jnp.int32, (owned, rows), 0)
    wanted = jnp.concatenate(
        [cluster_col + owned * block_of(k, heads) for k in steps], axis=0
    ).astype(jnp.float32)
    sums = jnp.zeros((len(steps) * owned, width), jnp.float32)
    for b in range(count):
        one_hot = jnp.where(wanted == id_rows[b, :1, :], 1.0, 0.0).astype(jnp.bfloat16)
        sums = sums + jnp.dot(one_hot, kv[b, :, :width], preferred_element_type=jnp.float32)

    def pair(blocks, masked):
        spread = jnp.concatenate([id_cols[...]] * (rows // width), axis=1)
        shares, mixes = [], []
        for b in blocks:
            score = lax.dot_general(
                query[...],
                kv[b, :, :width],
                (((1,), (1,)), ((), ())),
                preferred_element_type=jnp.float32,
            )
            weight = jnp.exp(score)
            same = spread == id_rows[b, :1, :]
            if masked:
                row_at = lax.broadcasted_iota(jnp.int32, weight.shape, 0)
                col_at = lax.broadcasted_iota(jnp.int32, weight.shape, 1)
                same = jnp.logical_and(same, col_at <= row_at)
            weight = jnp.where(same, weight, 0.0)
            shares += [
                weight[:, part * width : (part + 1) * width] for part in range(rows // width)
            ]
            mixes.append(
                jnp.dot(
                    weight.astype(jnp.bfloat16),
                    kv[b, :, width:],
                    preferred_element_type=jnp.float32,
                )
            )
        if masked:
            den[...], acc[...] = sum(shares[1:], shares[0]), sum(mixes[1:], mixes[0])
        else:
            den[...] += sum(shares[1:], shares[0])
            acc[...] += sum(mixes[1:], mixes[0])

    z = lax.axis_index(SEQ) >> 1
    for at, k in enumerate(steps):
        query[...] = kv[k, :, :width] * jnp.bfloat16(SCORE_SCALE)
        for part in range(rows // width):
            here = pl.ds(part * width, width)
            id_cols[here, :] = jnp.transpose(
                jnp.broadcast_to(id_rows[k, :1, part * width : (part + 1) * width], (width, width))
            )
        pair((k,), True)

        @pl.when(block_of(k + heads, heads) < block_of(k, heads))
        def _():
            pair((k + heads,), False)

        def per_pair(turn, carry):
            b = k ^ turn

            @pl.when((z ^ b) < (z ^ k))
            def _():
                pair((b, b + heads), False)

            return carry

        lax.fori_loop(1, heads, per_pair, 0)
        out = outs[at]
        whole = jnp.sum(den[...], axis=-1, keepdims=True)
        out[:rows, :] = (acc[...] / whole).astype(jnp.bfloat16)
        out[rows:, :] = sums[at * owned : (at + 1) * owned].astype(jnp.bfloat16)


def attend(inputs, heads, rows, width, owned, steps, first):
    result = shape((rows + owned, width))
    out_shape = (result,) * len(steps)
    if first:
        out_shape += (
            shape((2 * heads, rows, 2 * width)),
            shape((2 * heads, 8, rows), jnp.float32),
        )
    units = (heads * heads + heads // 2) * len(steps) // heads
    return pl.pallas_call(
        functools.partial(
            attend_body, heads=heads, width=width, owned=owned, steps=steps, first=first
        ),
        out_shape=out_shape,
        in_specs=[vmem_spec()] * len(inputs),
        out_specs=(vmem_spec(),) * len(out_shape),
        scratch_shapes=[
            pltpu.VMEM((rows, width), jnp.bfloat16),
            pltpu.VMEM((rows, width), jnp.float32),
            pltpu.VMEM((rows, width), jnp.float32),
            pltpu.VMEM((rows, width), jnp.float32),
        ],
        compiler_params=params(20),
        cost_estimate=cost(
            units * rows * rows * width * 8,
            2 * heads * rows * width * 4,
            units * rows * rows,
        ),
    )(*inputs)


def cut_body(*refs, count, share):
    back, kept, away, sums = refs[:count], refs[count], refs[count + 1 : -1], refs[-1]
    at = lax.axis_index(TENSOR)
    for k in range(count):
        for turn in range(len(away) + 1):
            here = pl.ds(pl.multiple_of((at ^ turn) * share, share), share)
            (kept if turn == 0 else away[turn - 1])[k] = back[k][here, :]
        rows = back[k].shape[0] - sums.shape[1]
        sums[k] = back[k][rows:, :].astype(jnp.float32)


def cut(back, owned, share, tensor_count):
    count, width = len(back), back[0].shape[1]
    piece = shape((count, share, width))
    return pl.pallas_call(
        functools.partial(cut_body, count=count, share=share),
        out_shape=(piece,) * tensor_count + (shape((count, owned, width), jnp.float32),),
        in_specs=[vmem_spec()] * count,
        out_specs=(vmem_spec(),) * (tensor_count + 1),
        compiler_params=params(8),
        cost_estimate=cost(0, 4 * count * tensor_count * share * width),
    )(*back)


def head_rows(weights, buf, sems, steps, width):
    z = lax.axis_index(SEQ) >> 1
    copies = []
    for g, w in enumerate(weights):
        for i, k in enumerate(steps):
            here = pl.ds(pl.multiple_of((z ^ k) * width, width), width)
            to = pl.ds((g * len(steps) + i) * width, width)
            copies.append(
                pltpu.make_async_copy(w.at[here, :], buf.at[to, :], sems.at[len(copies)])
            )
    return copies


def side_by_side(pieces, count):
    return jnp.concatenate([p[k] for p in pieces for k in range(count)], axis=1)


def products(pieces, count, near_rows, far_halves, known, put):
    y = lax.axis_index(SEQ) & 1
    half = far_halves[0].shape[1]
    near = side_by_side(pieces[:2], count)
    same, cross = side_by_side(pieces[2:3], count), side_by_side(pieces[3:4], count)
    for turn in range(2):
        cols = pl.ds(pl.multiple_of((y ^ turn) * half, half), half)
        total = known(cols)
        for left, rows in (
            (near, near_rows[:, cols]),
            (same, far_halves[turn][...]),
            (cross, far_halves[2 + turn][...]),
        ):
            total = total + jnp.dot(left, rows, preferred_element_type=jnp.float32)
        put(cols, total)


def mix_first_body(*refs, groups, width, steps, later):
    pieces, weights = refs[:groups], refs[groups : groups + 2]
    far_halves = refs[groups + 2 : groups + 6]
    tokens, mine, got, total, kept, buf, sems, later_sems = refs[groups + 6 :]
    now = head_rows(weights, buf, sems, steps, width)
    then = head_rows(weights, kept, later_sems, later, width)
    for copy in now + then:
        copy.start()
    share = total.shape[0]
    at = lax.axis_index(TENSOR)
    here = pl.ds(pl.multiple_of(at * share, share), share)
    for copy in now:
        copy.wait()

    def known(cols):
        base = tokens[here, cols].astype(jnp.float32) + mine[:, cols]
        return base + got[0, :, cols].astype(jnp.float32)

    def put(cols, value):
        total[:, cols] = value

    products(pieces, len(steps), buf, far_halves, known, put)
    for copy in then:
        copy.wait()


def mix_first(pieces, weights, far_halves, tokens, mine, got, steps, later):
    groups = len(pieces)
    count, share, width = pieces[0].shape
    depth = tokens.shape[1]
    rows = (2 * count * width, depth)
    return pl.pallas_call(
        functools.partial(
            mix_first_body, groups=groups, width=width, steps=steps, later=later
        ),
        out_shape=(shape((share, depth), jnp.float32), shape(rows)),
        in_specs=[vmem_spec()] * groups + [any_spec()] * 2 + [vmem_spec()] * 7,
        out_specs=(vmem_spec(), vmem_spec()),
        scratch_shapes=[
            pltpu.VMEM(rows, jnp.bfloat16),
            pltpu.SemaphoreType.DMA((2 * count,)),
            pltpu.SemaphoreType.DMA((2 * count,)),
        ],
        compiler_params=params(20),
        cost_estimate=cost(
            2 * groups * share * count * width * depth,
            4 * groups * count * width * depth + 8 * share * depth,
        ),
    )(*pieces, *weights, *far_halves, tokens, mine, got)


def mix_last_body(*refs, groups, steps, later):
    pieces, far_halves = refs[:groups], refs[groups : groups + 4]
    total, kept, came, first_sums, last_sums, centroids, out, updated = refs[groups + 4 :]
    z = lax.axis_index(SEQ) >> 1

    def known(cols):
        return total[:, cols] + came[:, cols].astype(jnp.float32)

    def put(cols, value):
        out[:, cols] = value.astype(jnp.bfloat16)

    products(pieces, len(later), kept, far_halves, known, put)
    for sums, turns in ((first_sums, steps), (last_sums, later)):
        for i, k in enumerate(turns):
            head = z ^ k
            updated[head] = EMA_DECAY * centroids[head] + (1.0 - EMA_DECAY) * sums[i]


def mix_last(
    pieces, far_halves, total, kept, came, first_sums, last_sums, centroids, steps, later
):
    groups = len(pieces)
    share, depth = total.shape
    return pl.pallas_call(
        functools.partial(mix_last_body, groups=groups, steps=steps, later=later),
        out_shape=(shape((share, depth)), shape(centroids.shape, jnp.float32)),
        in_specs=[vmem_spec()] * (groups + 10),
        out_specs=(vmem_spec(), vmem_spec()),
        compiler_params=params(16),
        cost_estimate=cost(4 * kept.size * share, 4 * kept.size + 8 * share * depth),
    )(*pieces, *far_halves, total, kept, came, first_sums, last_sums, centroids)


def by_heads(
    tokens, norm_gain, w_qk, w_value, w_out, w_up, w_down, centroids, clusters, slots
):
    tok_rows, _ = tokens.shape
    seq_count = lax.axis_size(SEQ)
    tensor_count = lax.axis_size(TENSOR)
    heads = clusters.shape[0]
    owned = centroids.shape[1]
    width = w_qk.shape[1] // heads
    share = tok_rows // tensor_count
    swaps = [None] + [[(t, t ^ d) for t in range(tensor_count)] for d in range(1, tensor_count)]

    w_core = lax.ppermute(w_out, TENSOR, swaps[1])
    steps = [owner_pairs(k, seq_count, tensor_count) for k in range(heads)]
    swap_y = [(s, s ^ 1) for s in range(seq_count)]
    messages, own, other = [None] * heads, [None] * heads, [None] * heads
    early, late = (heads - 1, 0), (heads - 2, 1)
    messages[2], messages[3], normed, ids, qk_next, val_next, *out_parts, up_part = project_far(
        tokens, norm_gain, w_qk, w_value, clusters, w_out, w_up, width, (early, late)
    )
    for k in (3, 2):
        own[k] = lax.ppermute(messages[k], BOTH, steps[k])
    halves = {}
    for name in "el":
        here = lax.ppermute(out_parts.pop(0), TENSOR, swaps[2])
        if name == "e":
            there = lax.ppermute(here, SEQ, swap_y)
        else:
            there = lax.ppermute(out_parts.pop(0), TENSOR, swaps[2])
        halves[name] = [here, there] + [lax.ppermute(w, TENSOR, swaps[1]) for w in (here, there)]
    messages[0], messages[1], up_first = project_near(normed, qk_next, val_next, ids, w_up, width)
    for k in (1, 0):
        own[k] = lax.ppermute(messages[k], BOTH, steps[k])
    hidden, down_first = up(normed, up_part, up_first, w_up, w_down)
    mine, far, sent = down(hidden, down_first, w_down, share)
    got = lax.ppermute(sent, TENSOR, swaps[1])
    for k in range(heads):
        other[k] = lax.ppermute(own[k], TENSOR, swaps[1])
    picked = pick(far, got)
    came = lax.ppermute(picked, TENSOR, swaps[2])
    back, pieces, sums = [None] * heads, {}, {}
    *results, kv, id_rows = attend(
        own + other, heads, tok_rows, width, owned, early, True
    )
    for k, result in zip(early, results):
        back[k] = lax.ppermute(result, BOTH, turned(steps[k]))
    results = attend([kv, id_rows], heads, tok_rows, width, owned, late, False)
    for k, result in zip(late, results):
        back[k] = lax.ppermute(result, BOTH, turned(steps[k]))

    for name, turns in (("e", early), ("l", late)):
        kept, *away, sums[name] = cut([back[k] for k in turns], owned, share, tensor_count)
        pieces[name] = [kept] + [
            lax.ppermute(away[d - 1], TENSOR, swaps[d])
            for d in range(1, tensor_count)
        ]
    total, late_rows = mix_first(
        pieces["e"], [held(w_out), w_core], halves["e"], tokens, mine, got, early, late
    )
    mixed_rows, new_centroids = mix_last(
        pieces["l"], halves["l"], total, late_rows, came, sums["e"], sums["l"],
        centroids, early, late,
    )
    return (mixed_rows, new_centroids)


def by_clusters(tokens, norm_gain, w_qk, w_value, w_out, w_up, w_down, centroids, clusters, slots):
    tok_rows = tokens.shape[0]
    seq_count = lax.axis_size(SEQ)
    tensor_count = lax.axis_size(TENSOR)
    heads_here = clusters.shape[0]
    owned_count = centroids.shape[1]
    head_width = w_qk.shape[1] // heads_here
    share_rows = tok_rows // tensor_count
    row_first = lax.axis_index(TENSOR) * share_rows
    tokens_wide = tokens.astype(jnp.float32)
    normed = (
        tokens_wide
        * lax.rsqrt(jnp.mean(tokens_wide * tokens_wide, axis=-1, keepdims=True) + NORM_EPS)
        * norm_gain
    ).astype(jnp.bfloat16)
    key_proj = jnp.dot(normed, w_qk, preferred_element_type=jnp.float32).reshape(
        tok_rows, heads_here, head_width
    )
    key_unit = (
        key_proj * lax.rsqrt(jnp.sum(key_proj * key_proj, axis=-1, keepdims=True) + NORM_EPS)
    ).astype(jnp.bfloat16)
    val_proj = (
        jnp.dot(normed, w_value, preferred_element_type=jnp.float32)
        .astype(jnp.bfloat16)
        .reshape(tok_rows, heads_here, head_width)
    )
    positions = lax.axis_index(SEQ) * tok_rows + jnp.arange(tok_rows, dtype=jnp.int32)
    pos_high = (positions // 256).astype(jnp.float32).astype(jnp.bfloat16)
    pos_low = (positions % 256).astype(jnp.float32).astype(jnp.bfloat16)
    flat_slot = clusters.T * CAP + slots.T
    head_grid = jnp.broadcast_to(jnp.arange(heads_here, dtype=jnp.int32)[None, :], flat_slot.shape)
    slot_total = CLUSTERS * CAP
    layout = (heads_here, seq_count, owned_count, CAP)
    key_buf = (
        jnp.zeros((heads_here, slot_total, head_width), jnp.bfloat16)
        .at[head_grid, flat_slot]
        .set(key_unit)
        .reshape(layout + (head_width,))
    )
    val_buf = (
        jnp.zeros((heads_here, slot_total, head_width), jnp.bfloat16)
        .at[head_grid, flat_slot]
        .set(val_proj)
        .reshape(layout + (head_width,))
    )
    high_buf = (
        jnp.full((heads_here, slot_total), 256.0, jnp.bfloat16)
        .at[head_grid, flat_slot]
        .set(jnp.broadcast_to(pos_high[:, None], flat_slot.shape))
        .reshape(layout)
    )
    low_buf = (
        jnp.zeros((heads_here, slot_total), jnp.bfloat16)
        .at[head_grid, flat_slot]
        .set(jnp.broadcast_to(pos_low[:, None], flat_slot.shape))
        .reshape(layout)
    )
    key_in = lax.all_to_all(key_buf, SEQ, split_axis=1, concat_axis=1, tiled=True)
    val_in = lax.all_to_all(val_buf, SEQ, split_axis=1, concat_axis=1, tiled=True)
    high_in = lax.all_to_all(high_buf, SEQ, split_axis=1, concat_axis=1, tiled=True)
    low_in = lax.all_to_all(low_buf, SEQ, split_axis=1, concat_axis=1, tiled=True)
    scores = (
        jnp.einsum("hskad,htkbd->hksatb", key_in, key_in, preferred_element_type=jnp.float32)
        * SCORE_SCALE
    )
    key_place = high_in.astype(jnp.float32) * 256.0 + low_in.astype(jnp.float32)
    ordered = jnp.transpose(key_place, (0, 2, 1, 3))
    causal = ordered[:, :, None, None, :, :] <= ordered[:, :, :, :, None, None]
    exponent = jnp.where(causal, jnp.exp(scores), 0.0)
    weights = (exponent / jnp.sum(exponent, axis=(4, 5), keepdims=True)).astype(jnp.bfloat16)
    mixed_out = jnp.einsum(
        "hksatb,htkbd->hskad", weights, val_in, preferred_element_type=jnp.float32
    ).astype(jnp.bfloat16)
    returned_back = lax.all_to_all(mixed_out, SEQ, split_axis=1, concat_axis=1, tiled=True)
    one_hot = (clusters[:, :, None] == jnp.arange(CLUSTERS, dtype=jnp.int32)[None, None, :]).astype(
        jnp.bfloat16
    )
    local_sums = jnp.einsum("htk,thd->hkd", one_hot, key_unit, preferred_element_type=jnp.float32)
    totals = lax.psum_scatter(
        local_sums.astype(jnp.bfloat16), SEQ, scatter_dimension=1, tiled=True
    ).astype(jnp.float32)
    new_centroids = EMA_DECAY * centroids + (1.0 - EMA_DECAY) * totals
    returned = returned_back.reshape(heads_here, slot_total, head_width)
    attended = returned[head_grid, flat_slot].reshape(tok_rows, heads_here * head_width)
    attn_part = jnp.dot(attended, w_out, preferred_element_type=jnp.float32)
    hidden = jax.nn.relu(jnp.dot(normed, w_up, preferred_element_type=jnp.float32)).astype(
        jnp.bfloat16
    )
    ffn_part = jnp.dot(hidden, w_down, preferred_element_type=jnp.float32)
    summed = lax.psum_scatter(
        rounded(attn_part + ffn_part).astype(jnp.bfloat16),
        TENSOR,
        scatter_dimension=0,
        tiled=True,
    ).astype(jnp.float32)
    own_rows = lax.dynamic_slice_in_dim(tokens_wide, row_first, share_rows, 0)
    mixed_rows = (own_rows + summed).astype(jnp.bfloat16)
    return (mixed_rows, new_centroids)


def solution(mesh):
    in_specs = (
        P(SEQ, None),
        P(),
        P(None, TENSOR),
        P(None, TENSOR),
        P(TENSOR, None),
        P(None, TENSOR),
        P(TENSOR, None),
        P(TENSOR, SEQ, None),
        P(TENSOR, SEQ),
        P(TENSOR, SEQ),
    )
    out_specs = (P((SEQ, TENSOR), None), P(TENSOR, SEQ, None))
    sizes = dict(mesh.shape)

    def local(*args):
        heads = args[8].shape[0]
        fits = (
            sizes[TENSOR] == 4
            and sizes[SEQ] == 2 * heads
            and heads & (heads - 1) == 0
            and heads == 4
        )
        if not fits:
            return by_clusters(*args)
        return by_heads(*args)

    return jax.shard_map(
        local, mesh=mesh, in_specs=in_specs, out_specs=out_specs, check_vma=False
    )
```

```python
import functools

import jax
import jax.numpy as jnp
from jax import lax
from jax.experimental import pallas as pl
from jax.experimental.pallas import tpu as pltpu
from jax.sharding import PartitionSpec as P


CLUSTERS = 256
CAP = 4

SCORE_SCALE = 2.0
EMA_DECAY = 0.9
NORM_EPS = 1e-06
SEQ, TENSOR = "seq", "tensor"
BOTH = (SEQ, TENSOR)
EXTRA = 16
MIB = 1024 * 1024


def rounded(term_value):
    return lax.optimization_barrier(term_value.astype(jnp.bfloat16)).astype(jnp.float32)


def owner_pairs(step, seq_count, tensor_count):
    pairs = []
    for s in range(seq_count):
        for t in range(tensor_count):
            z, y, c = s // 2, s % 2, t % 2
            dest_s = 2 * (z ^ step) + c
            dest_t = (t - c) + (y ^ (z & 1))
            pairs.append((s * tensor_count + t, dest_s * tensor_count + dest_t))
    return pairs


def turned(pairs):
    return [(b, a) for a, b in pairs]


def any_spec():
    return pl.BlockSpec(memory_space=pl.ANY)


def vmem_spec():
    return pl.BlockSpec(memory_space=pltpu.VMEM)


def held(value):
    return pltpu.with_memory_space_constraint(value, pltpu.HBM)


def params(mib):
    return pltpu.CompilerParams(vmem_limit_bytes=mib * MIB)


def cost(flops, moved, transcendentals=0):
    return pl.CostEstimate(
        flops=flops, bytes_accessed=moved, transcendentals=transcendentals
    )


def shape(dims, kind=jnp.bfloat16):
    return jax.ShapeDtypeStruct(dims, kind)


def unit_heads(normed, w_qk, w_value, outs, clusters, steps, width):
    z = lax.axis_index(SEQ) >> 1
    rows = normed.shape[0]
    span = 2 * width
    odd = (z & 1) == 1
    row_at = lax.broadcasted_iota(jnp.int32, (EXTRA, span), 0)
    key_proj = jnp.dot(normed[...], w_qk[...], preferred_element_type=jnp.float32)
    units = []
    for q in range(2):
        k = key_proj[:, q * width : (q + 1) * width]
        total = jnp.sum(k * k, axis=-1, keepdims=True)
        units.append((k * lax.rsqrt(total + NORM_EPS)).astype(jnp.bfloat16))
    val_proj = jnp.dot(normed[...], w_value[...], preferred_element_type=jnp.float32)
    values = [val_proj[:, q * width : (q + 1) * width].astype(jnp.bfloat16) for q in range(2)]
    for q, out in enumerate(outs):
        out[:rows, :width] = jnp.where(odd, units[1 - q], units[q])
        out[:rows, width:] = jnp.where(odd, values[1 - q], values[q])
        id_row = clusters[pl.ds(steps[q] ^ z, 1), :].astype(jnp.float32)
        tail = jnp.zeros((EXTRA, span), jnp.float32)
        for part in range(rows // span):
            piece = id_row[:, part * span : (part + 1) * span]
            tail = jnp.where(row_at == part, piece, tail)
        out[rows:, :] = tail.astype(jnp.bfloat16)


def project_far_body(
    tokens_at, gain_at, w_qk, w_value, clusters_at, w_out, *rest, width, stages, parts
):
    out_low, out_high, normed, clusters, qk_next, val_next, out_early, out_late, out_rest = rest[:9]
    tokens, gain, qk_buf, val_buf, sems, token_sems, out_sems = rest[9:]
    z = lax.axis_index(SEQ) >> 1
    y = lax.axis_index(SEQ) & 1
    step = tokens.shape[0] // parts
    span = 2 * width
    slabs = [pl.ds(r * step, step) for r in range(parts)]
    slab_copies = [
        pltpu.make_async_copy(tokens_at.at[here, :], tokens.at[here, :], token_sems.at[r])
        for r, here in enumerate(slabs)
    ]

    def columns(block):
        return pl.ds(pl.multiple_of(block * span, span), span)

    first, second = columns(1 ^ (z >> 1)), columns(z >> 1)
    half = out_early.shape[1]
    out_copies = []
    for part, turns, at in (
        (out_early, stages[0], y),
        (out_late, stages[1], y),
        (out_rest, stages[1], 1 - y),
    ):
        out_cols = pl.ds(pl.multiple_of(at * half, half), half)
        for i, k in enumerate(turns):
            here = pl.ds(pl.multiple_of((z ^ k) * width, width), width)
            out_copies.append(
                pltpu.make_async_copy(
                    w_out.at[here, out_cols],
                    part.at[pl.ds(i * width, width), :],
                    out_sems.at[len(out_copies)],
                )
            )
    copies = [
        pltpu.make_async_copy(gain_at, gain, sems.at[0]),
        pltpu.make_async_copy(w_qk.at[:, first], qk_buf, sems.at[1]),
        pltpu.make_async_copy(w_value.at[:, first], val_buf, sems.at[2]),
        pltpu.make_async_copy(clusters_at, clusters, sems.at[3]),
        pltpu.make_async_copy(w_qk.at[:, second], qk_next, sems.at[4]),
        pltpu.make_async_copy(w_value.at[:, second], val_next, sems.at[5]),
    ]
    for copy in (copies[0], *slab_copies, *copies[1:4], *out_copies, *copies[4:]):
        copy.start()
    copies[0].wait()
    for copy, here in zip(slab_copies, slabs):
        copy.wait()
        wide = tokens[here, :].astype(jnp.float32)
        mean = jnp.mean(wide * wide, axis=-1, keepdims=True)
        normed[here, :] = (wide * lax.rsqrt(mean + NORM_EPS) * gain[...]).astype(jnp.bfloat16)
    for copy in copies[1:4]:
        copy.wait()
    unit_heads(normed, qk_buf, val_buf, (out_low, out_high), clusters, (2, 3), width)
    for copy in copies[4:] + out_copies:
        copy.wait()


def project_far(tokens, gain, w_qk, w_value, clusters, w_out, width, stages, parts=4):
    rows, depth = tokens.shape
    message = shape((rows + EXTRA, 2 * width))
    pair = (depth, 2 * width)
    return pl.pallas_call(
        functools.partial(project_far_body, width=width, stages=stages, parts=parts),
        out_shape=(
            message,
            message,
            shape((rows, depth)),
            shape(clusters.shape, jnp.int32),
            shape(pair),
            shape(pair),
            shape((2 * width, w_out.shape[1] // 2)),
            shape((2 * width, w_out.shape[1] // 2)),
            shape((2 * width, w_out.shape[1] // 2)),
        ),
        in_specs=[any_spec()] * 6,
        out_specs=(vmem_spec(),) * 9,
        scratch_shapes=[
            pltpu.VMEM((rows, depth), jnp.bfloat16),
            pltpu.VMEM((1, depth), jnp.float32),
            pltpu.VMEM(pair, jnp.bfloat16),
            pltpu.VMEM(pair, jnp.bfloat16),
            pltpu.SemaphoreType.DMA((6,)),
            pltpu.SemaphoreType.DMA((parts,)),
            pltpu.SemaphoreType.DMA((6,)),
        ],
        compiler_params=params(20),
        cost_estimate=cost(8 * rows * depth * width, 2 * rows * depth + 12 * depth * width),
    )(*[held(a) for a in (tokens, gain.reshape(1, depth), w_qk, w_value, clusters, w_out)])


def project_near_body(
    normed, w_qk, w_value, clusters, w_up, out_low, out_high, next_half, sem, *, width
):
    copy = pltpu.make_async_copy(w_up.at[:, pl.ds(0, next_half.shape[1])], next_half, sem)
    copy.start()
    unit_heads(normed, w_qk, w_value, (out_low, out_high), clusters, (0, 1), width)
    copy.wait()


def project_near(normed, w_qk, w_value, clusters, w_up, width):
    rows, depth = normed.shape
    message = shape((rows + EXTRA, 2 * width))
    return pl.pallas_call(
        functools.partial(project_near_body, width=width),
        out_shape=(message, message, shape((depth, w_up.shape[1] // 2))),
        in_specs=[vmem_spec()] * 4 + [any_spec()],
        out_specs=(vmem_spec(),) * 3,
        scratch_shapes=[pltpu.SemaphoreType.DMA],
        compiler_params=params(16),
        cost_estimate=cost(8 * rows * depth * width, 2 * rows * depth + 8 * depth * width),
    )(normed, w_qk, w_value, clusters, held(w_up))


def up_body(normed, first, w_up, w_down, hidden, next_half, second, sems):
    half = first.shape[1]
    copies = (
        pltpu.make_async_copy(w_up.at[:, pl.ds(half, half)], second, sems.at[0]),
        pltpu.make_async_copy(
            w_down.at[:, pl.ds(0, next_half.shape[1])], next_half, sems.at[1]
        ),
    )
    for copy in copies:
        copy.start()
    for at, weights in enumerate((first, second)):
        if at == 1:
            copies[0].wait()
        grown = jnp.dot(normed[...], weights[...], preferred_element_type=jnp.float32)
        hidden[:, at * half : (at + 1) * half] = jnp.maximum(grown, 0.0).astype(jnp.bfloat16)
    copies[1].wait()


def up(normed, first, w_up, w_down):
    rows, depth = normed.shape
    units = w_up.shape[1]
    return pl.pallas_call(
        up_body,
        out_shape=(shape((rows, units)), shape((units, w_down.shape[1] // 2))),
        in_specs=[vmem_spec(), vmem_spec(), any_spec(), any_spec()],
        out_specs=(vmem_spec(), vmem_spec()),
        scratch_shapes=[
            pltpu.VMEM((depth, units // 2), jnp.bfloat16),
            pltpu.SemaphoreType.DMA((2,)),
        ],
        compiler_params=params(24),
        cost_estimate=cost(2 * rows * depth * units, 2 * depth * units + 4 * rows * depth),
    )(normed, first, held(w_up), held(w_down))


def down_body(hidden, first, w_down, mine, far, away, second, held_rows, sem, *, share):
    at = lax.axis_index(TENSOR)
    half = first.shape[1]
    copy = pltpu.make_async_copy(w_down.at[:, pl.ds(half, half)], second, sem)
    copy.start()

    def quarter(turn):
        return held_rows[pl.ds(pl.multiple_of((at ^ turn) * share, share), share), :]

    for part, weights in enumerate((first, second)):
        if part == 1:
            copy.wait()
        cols = slice(part * half, (part + 1) * half)
        held_rows[...] = jnp.dot(
            hidden[...], weights[...], preferred_element_type=jnp.float32
        )
        mine[:, cols] = quarter(0)
        far[:, cols] = quarter(2)
        away[0, :, cols] = quarter(1).astype(jnp.bfloat16)
        away[1, :, cols] = quarter(3).astype(jnp.bfloat16)


def down(hidden, first, w_down, share):
    rows, units = hidden.shape
    depth = w_down.shape[1]
    return pl.pallas_call(
        functools.partial(down_body, share=share),
        out_shape=(
            shape((share, depth), jnp.float32),
            shape((share, depth), jnp.float32),
            shape((2, share, depth)),
        ),
        in_specs=[vmem_spec(), vmem_spec(), any_spec()],
        out_specs=(vmem_spec(),) * 3,
        scratch_shapes=[
            pltpu.VMEM((units, depth // 2), jnp.bfloat16),
            pltpu.VMEM((rows, depth // 2), jnp.float32),
            pltpu.SemaphoreType.DMA,
        ],
        compiler_params=params(24),
        cost_estimate=cost(2 * rows * depth * units, 2 * depth * units + 6 * rows * depth),
    )(hidden, first, held(w_down))


def pick_body(far, got, sent):
    sent[...] = (far[...] + got[1].astype(jnp.float32)).astype(jnp.bfloat16)


def pick(far, got):
    return pl.pallas_call(
        pick_body,
        out_shape=shape(far.shape),
        in_specs=[vmem_spec(), vmem_spec()],
        out_specs=vmem_spec(),
        compiler_params=params(6),
        cost_estimate=cost(far.size, far.size * 8),
    )(far, got)


def block_of(b, heads):
    z = lax.axis_index(SEQ) >> 1
    core = lax.axis_index(TENSOR) % 2
    pair = z ^ (b % heads)
    return 2 * pair + (core ^ (pair & 1) ^ (b // heads))


def attend_body(*refs, heads, width, owned, steps, first):
    if first:
        own, other = refs[:heads], refs[heads : 2 * heads]
        refs = refs[2 * heads :]
        outs = refs[: len(steps)]
        kv, id_rows, later_sums = refs[len(steps) : len(steps) + 3]
        query, id_cols, acc, den = refs[len(steps) + 3 :]
        rows = kv.shape[1]
        for b, source in enumerate(list(own) + list(other)):
            kv[b] = source[:rows, :]
            tile = source[rows:, :].astype(jnp.float32)
            id_row = jnp.concatenate(
                [tile[r : r + 1, :] for r in range(rows // (2 * width))], axis=1
            )
            id_rows[b] = jnp.broadcast_to(id_row, (8, rows))
    else:
        kv, id_rows, sums = refs[:3]
        outs = refs[3 : 3 + len(steps)]
        query, id_cols, acc, den = refs[3 + len(steps) :]
        rows = kv.shape[1]

    if first:
        cluster_col = lax.broadcasted_iota(jnp.int32, (owned, rows), 0)
        order = [*steps, *(k for k in range(heads - 1, -1, -1) if k not in steps)]
        wanted = jnp.concatenate(
            [cluster_col + owned * block_of(k, heads) for k in order], axis=0
        ).astype(jnp.float32)
        sums = jnp.zeros((heads * owned, width), jnp.float32)
        for b in range(2 * heads):
            one_hot = jnp.where(wanted == id_rows[b, :1, :], 1.0, 0.0).astype(jnp.bfloat16)
            sums = sums + jnp.dot(
                one_hot, kv[b, :, :width], preferred_element_type=jnp.float32
            )
        later_sums[...] = sums[len(steps) * owned :]

    def pair(blocks, masked):
        spread = jnp.concatenate([id_cols[...]] * (rows // width), axis=1)
        shares, mixes = [], []
        for b in blocks:
            score = lax.dot_general(
                query[...],
                kv[b, :, :width],
                (((1,), (1,)), ((), ())),
                preferred_element_type=jnp.float32,
            )
            weight = jnp.exp(score)
            same = spread == id_rows[b, :1, :]
            if masked:
                row_at = lax.broadcasted_iota(jnp.int32, weight.shape, 0)
                col_at = lax.broadcasted_iota(jnp.int32, weight.shape, 1)
                same = jnp.logical_and(same, col_at <= row_at)
            weight = jnp.where(same, weight, 0.0)
            shares += [
                weight[:, part * width : (part + 1) * width] for part in range(rows // width)
            ]
            mixes.append(
                jnp.dot(
                    weight.astype(jnp.bfloat16),
                    kv[b, :, width:],
                    preferred_element_type=jnp.float32,
                )
            )
        if masked:
            den[...], acc[...] = sum(shares[1:], shares[0]), sum(mixes[1:], mixes[0])
        else:
            den[...] += sum(shares[1:], shares[0])
            acc[...] += sum(mixes[1:], mixes[0])

    z = lax.axis_index(SEQ) >> 1
    for at, k in enumerate(steps):
        query[...] = kv[k, :, :width] * jnp.bfloat16(SCORE_SCALE)
        for part in range(rows // width):
            here = pl.ds(part * width, width)
            id_cols[here, :] = jnp.transpose(
                jnp.broadcast_to(id_rows[k, :1, part * width : (part + 1) * width], (width, width))
            )
        pair((k,), True)

        @pl.when(block_of(k + heads, heads) < block_of(k, heads))
        def _():
            pair((k + heads,), False)

        def per_pair(turn, carry):
            b = k ^ turn

            @pl.when((z ^ b) < (z ^ k))
            def _():
                pair((b, b + heads), False)

            return carry

        lax.fori_loop(1, heads, per_pair, 0)
        out = outs[at]
        whole = jnp.sum(den[...], axis=-1, keepdims=True)
        out[:rows, :] = (acc[...] / whole).astype(jnp.bfloat16)
        out[rows:, :] = sums[at * owned : (at + 1) * owned].astype(jnp.bfloat16)


def attend(inputs, heads, rows, width, owned, steps, first):
    result = shape((rows + owned, width))
    out_shape = (result,) * len(steps)
    if first:
        out_shape += (
            shape((2 * heads, rows, 2 * width)),
            shape((2 * heads, 8, rows), jnp.float32),
            shape(((heads - len(steps)) * owned, width), jnp.float32),
        )
    units = (heads * heads + heads // 2) * len(steps) // heads
    return pl.pallas_call(
        functools.partial(
            attend_body, heads=heads, width=width, owned=owned, steps=steps, first=first
        ),
        out_shape=out_shape,
        in_specs=[vmem_spec()] * len(inputs),
        out_specs=(vmem_spec(),) * len(out_shape),
        scratch_shapes=[
            pltpu.VMEM((rows, width), jnp.bfloat16),
            pltpu.VMEM((rows, width), jnp.float32),
            pltpu.VMEM((rows, width), jnp.float32),
            pltpu.VMEM((rows, width), jnp.float32),
        ],
        compiler_params=params(20),
        cost_estimate=cost(
            units * rows * rows * width * 8,
            2 * heads * rows * width * 4,
            units * rows * rows,
        ),
    )(*inputs)


def cut_body(*refs, count, share):
    back, kept, away, sums = refs[:count], refs[count], refs[count + 1 : -1], refs[-1]
    at = lax.axis_index(TENSOR)
    for k in range(count):
        for turn in range(len(away) + 1):
            here = pl.ds(pl.multiple_of((at ^ turn) * share, share), share)
            (kept if turn == 0 else away[turn - 1])[k] = back[k][here, :]
        rows = back[k].shape[0] - sums.shape[1]
        sums[k] = back[k][rows:, :].astype(jnp.float32)


def cut(back, owned, share, tensor_count):
    count, width = len(back), back[0].shape[1]
    piece = shape((count, share, width))
    return pl.pallas_call(
        functools.partial(cut_body, count=count, share=share),
        out_shape=(piece,) * tensor_count + (shape((count, owned, width), jnp.float32),),
        in_specs=[vmem_spec()] * count,
        out_specs=(vmem_spec(),) * (tensor_count + 1),
        compiler_params=params(8),
        cost_estimate=cost(0, 4 * count * tensor_count * share * width),
    )(*back)


def head_rows(weights, buf, sems, steps, width):
    z = lax.axis_index(SEQ) >> 1
    copies = []
    for g, w in enumerate(weights):
        for i, k in enumerate(steps):
            here = pl.ds(pl.multiple_of((z ^ k) * width, width), width)
            to = pl.ds((g * len(steps) + i) * width, width)
            copies.append(
                pltpu.make_async_copy(w.at[here, :], buf.at[to, :], sems.at[len(copies)])
            )
    return copies


def side_by_side(pieces, count):
    return jnp.concatenate([p[k] for p in pieces for k in range(count)], axis=1)


def products(pieces, count, near_rows, far_halves, known, put):
    y = lax.axis_index(SEQ) & 1
    half = far_halves[0].shape[1]
    near = side_by_side(pieces[:2], count)
    same, cross = side_by_side(pieces[2:3], count), side_by_side(pieces[3:4], count)
    for turn in range(2):
        cols = pl.ds(pl.multiple_of((y ^ turn) * half, half), half)
        total = known(cols)
        for left, rows in (
            (near, near_rows[:, cols]),
            (same, far_halves[turn][...]),
            (cross, far_halves[2 + turn][...]),
        ):
            total = total + jnp.dot(left, rows, preferred_element_type=jnp.float32)
        put(cols, total)


def mix_first_body(*refs, groups, width, steps, later):
    pieces, weights = refs[:groups], refs[groups : groups + 2]
    far_halves = refs[groups + 2 : groups + 6]
    tokens, mine, got, total, kept, buf, sems, later_sems = refs[groups + 6 :]
    now = head_rows(weights, buf, sems, steps, width)
    then = head_rows(weights, kept, later_sems, later, width)
    for copy in now + then:
        copy.start()
    share = total.shape[0]
    at = lax.axis_index(TENSOR)
    here = pl.ds(pl.multiple_of(at * share, share), share)
    for copy in now:
        copy.wait()

    def known(cols):
        base = tokens[here, cols].astype(jnp.float32) + mine[:, cols]
        return base + got[0, :, cols].astype(jnp.float32)

    def put(cols, value):
        total[:, cols] = value

    products(pieces, len(steps), buf, far_halves, known, put)
    for copy in then:
        copy.wait()


def mix_first(pieces, weights, far_halves, tokens, mine, got, steps, later):
    groups = len(pieces)
    count, share, width = pieces[0].shape
    depth = tokens.shape[1]
    rows = (2 * count * width, depth)
    return pl.pallas_call(
        functools.partial(
            mix_first_body, groups=groups, width=width, steps=steps, later=later
        ),
        out_shape=(shape((share, depth), jnp.float32), shape(rows)),
        in_specs=[vmem_spec()] * groups + [any_spec()] * 2 + [vmem_spec()] * 7,
        out_specs=(vmem_spec(), vmem_spec()),
        scratch_shapes=[
            pltpu.VMEM(rows, jnp.bfloat16),
            pltpu.SemaphoreType.DMA((2 * count,)),
            pltpu.SemaphoreType.DMA((2 * count,)),
        ],
        compiler_params=params(20),
        cost_estimate=cost(
            2 * groups * share * count * width * depth,
            4 * groups * count * width * depth + 8 * share * depth,
        ),
    )(*pieces, *weights, *far_halves, tokens, mine, got)


def mix_last_body(*refs, groups, steps, later):
    pieces, far_halves = refs[:groups], refs[groups : groups + 4]
    total, kept, came, first_sums, last_sums, centroids, out, updated = refs[groups + 4 :]
    z = lax.axis_index(SEQ) >> 1

    def known(cols):
        return total[:, cols] + came[:, cols].astype(jnp.float32)

    def put(cols, value):
        out[:, cols] = value.astype(jnp.bfloat16)

    products(pieces, len(later), kept, far_halves, known, put)
    for sums, turns in ((first_sums, steps), (last_sums, later)):
        for i, k in enumerate(turns):
            head = z ^ k
            updated[head] = EMA_DECAY * centroids[head] + (1.0 - EMA_DECAY) * sums[i]


def mix_last(
    pieces, far_halves, total, kept, came, first_sums, last_sums, centroids, steps, later
):
    groups = len(pieces)
    share, depth = total.shape
    return pl.pallas_call(
        functools.partial(mix_last_body, groups=groups, steps=steps, later=later),
        out_shape=(shape((share, depth)), shape(centroids.shape, jnp.float32)),
        in_specs=[vmem_spec()] * (groups + 10),
        out_specs=(vmem_spec(), vmem_spec()),
        compiler_params=params(16),
        cost_estimate=cost(4 * kept.size * share, 4 * kept.size + 8 * share * depth),
    )(*pieces, *far_halves, total, kept, came, first_sums, last_sums, centroids)


def by_heads(
    tokens, norm_gain, w_qk, w_value, w_out, w_up, w_down, centroids, clusters, slots
):
    tok_rows, _ = tokens.shape
    seq_count = lax.axis_size(SEQ)
    tensor_count = lax.axis_size(TENSOR)
    heads = clusters.shape[0]
    owned = centroids.shape[1]
    width = w_qk.shape[1] // heads
    share = tok_rows // tensor_count
    swaps = [None] + [[(t, t ^ d) for t in range(tensor_count)] for d in range(1, tensor_count)]

    w_core = lax.ppermute(w_out, TENSOR, swaps[1])
    steps = [owner_pairs(k, seq_count, tensor_count) for k in range(heads)]
    swap_y = [(s, s ^ 1) for s in range(seq_count)]
    messages, own, other = [None] * heads, [None] * heads, [None] * heads
    early, late = (heads - 1, 0), (heads - 2, 1)
    messages[2], messages[3], normed, ids, qk_next, val_next, *out_parts = project_far(
        tokens, norm_gain, w_qk, w_value, clusters, w_out, width, (early, late)
    )
    for k in (3, 2):
        own[k] = lax.ppermute(messages[k], BOTH, steps[k])
    halves = {}
    for name in "el":
        here = lax.ppermute(out_parts.pop(0), TENSOR, swaps[2])
        if name == "e":
            there = lax.ppermute(here, SEQ, swap_y)
        else:
            there = lax.ppermute(out_parts.pop(0), TENSOR, swaps[2])
        halves[name] = [here, there] + [lax.ppermute(w, TENSOR, swaps[1]) for w in (here, there)]
    messages[0], messages[1], up_first = project_near(normed, qk_next, val_next, ids, w_up, width)
    for k in (1, 0):
        own[k] = lax.ppermute(messages[k], BOTH, steps[k])
    hidden, down_first = up(normed, up_first, w_up, w_down)
    mine, far, sent = down(hidden, down_first, w_down, share)
    got = lax.ppermute(sent, TENSOR, swaps[1])
    for k in range(heads):
        other[k] = lax.ppermute(own[k], TENSOR, swaps[1])
    picked = pick(far, got)
    came = lax.ppermute(picked, TENSOR, swaps[2])
    back, pieces, sums = [None] * heads, {}, {}
    *results, kv, id_rows, late_sums = attend(
        own + other, heads, tok_rows, width, owned, early, True
    )
    for k, result in zip(early, results):
        back[k] = lax.ppermute(result, BOTH, turned(steps[k]))
    results = attend([kv, id_rows, late_sums], heads, tok_rows, width, owned, late, False)
    for k, result in zip(late, results):
        back[k] = lax.ppermute(result, BOTH, turned(steps[k]))

    for name, turns in (("e", early), ("l", late)):
        kept, *away, sums[name] = cut([back[k] for k in turns], owned, share, tensor_count)
        pieces[name] = [kept] + [
            lax.ppermute(away[d - 1], TENSOR, swaps[d])
            for d in range(1, tensor_count)
        ]
    total, late_rows = mix_first(
        pieces["e"], [held(w_out), w_core], halves["e"], tokens, mine, got, early, late
    )
    mixed_rows, new_centroids = mix_last(
        pieces["l"], halves["l"], total, late_rows, came, sums["e"], sums["l"],
        centroids, early, late,
    )
    return (mixed_rows, new_centroids)


def by_clusters(tokens, norm_gain, w_qk, w_value, w_out, w_up, w_down, centroids, clusters, slots):
    tok_rows = tokens.shape[0]
    seq_count = lax.axis_size(SEQ)
    tensor_count = lax.axis_size(TENSOR)
    heads_here = clusters.shape[0]
    owned_count = centroids.shape[1]
    head_width = w_qk.shape[1] // heads_here
    share_rows = tok_rows // tensor_count
    row_first = lax.axis_index(TENSOR) * share_rows
    tokens_wide = tokens.astype(jnp.float32)
    normed = (
        tokens_wide
        * lax.rsqrt(jnp.mean(tokens_wide * tokens_wide, axis=-1, keepdims=True) + NORM_EPS)
        * norm_gain
    ).astype(jnp.bfloat16)
    key_proj = jnp.dot(normed, w_qk, preferred_element_type=jnp.float32).reshape(
        tok_rows, heads_here, head_width
    )
    key_unit = (
        key_proj * lax.rsqrt(jnp.sum(key_proj * key_proj, axis=-1, keepdims=True) + NORM_EPS)
    ).astype(jnp.bfloat16)
    val_proj = (
        jnp.dot(normed, w_value, preferred_element_type=jnp.float32)
        .astype(jnp.bfloat16)
        .reshape(tok_rows, heads_here, head_width)
    )
    positions = lax.axis_index(SEQ) * tok_rows + jnp.arange(tok_rows, dtype=jnp.int32)
    pos_high = (positions // 256).astype(jnp.float32).astype(jnp.bfloat16)
    pos_low = (positions % 256).astype(jnp.float32).astype(jnp.bfloat16)
    flat_slot = clusters.T * CAP + slots.T
    head_grid = jnp.broadcast_to(jnp.arange(heads_here, dtype=jnp.int32)[None, :], flat_slot.shape)
    slot_total = CLUSTERS * CAP
    layout = (heads_here, seq_count, owned_count, CAP)
    key_buf = (
        jnp.zeros((heads_here, slot_total, head_width), jnp.bfloat16)
        .at[head_grid, flat_slot]
        .set(key_unit)
        .reshape(layout + (head_width,))
    )
    val_buf = (
        jnp.zeros((heads_here, slot_total, head_width), jnp.bfloat16)
        .at[head_grid, flat_slot]
        .set(val_proj)
        .reshape(layout + (head_width,))
    )
    high_buf = (
        jnp.full((heads_here, slot_total), 256.0, jnp.bfloat16)
        .at[head_grid, flat_slot]
        .set(jnp.broadcast_to(pos_high[:, None], flat_slot.shape))
        .reshape(layout)
    )
    low_buf = (
        jnp.zeros((heads_here, slot_total), jnp.bfloat16)
        .at[head_grid, flat_slot]
        .set(jnp.broadcast_to(pos_low[:, None], flat_slot.shape))
        .reshape(layout)
    )
    key_in = lax.all_to_all(key_buf, SEQ, split_axis=1, concat_axis=1, tiled=True)
    val_in = lax.all_to_all(val_buf, SEQ, split_axis=1, concat_axis=1, tiled=True)
    high_in = lax.all_to_all(high_buf, SEQ, split_axis=1, concat_axis=1, tiled=True)
    low_in = lax.all_to_all(low_buf, SEQ, split_axis=1, concat_axis=1, tiled=True)
    scores = (
        jnp.einsum("hskad,htkbd->hksatb", key_in, key_in, preferred_element_type=jnp.float32)
        * SCORE_SCALE
    )
    key_place = high_in.astype(jnp.float32) * 256.0 + low_in.astype(jnp.float32)
    ordered = jnp.transpose(key_place, (0, 2, 1, 3))
    causal = ordered[:, :, None, None, :, :] <= ordered[:, :, :, :, None, None]
    exponent = jnp.where(causal, jnp.exp(scores), 0.0)
    weights = (exponent / jnp.sum(exponent, axis=(4, 5), keepdims=True)).astype(jnp.bfloat16)
    mixed_out = jnp.einsum(
        "hksatb,htkbd->hskad", weights, val_in, preferred_element_type=jnp.float32
    ).astype(jnp.bfloat16)
    returned_back = lax.all_to_all(mixed_out, SEQ, split_axis=1, concat_axis=1, tiled=True)
    one_hot = (clusters[:, :, None] == jnp.arange(CLUSTERS, dtype=jnp.int32)[None, None, :]).astype(
        jnp.bfloat16
    )
    local_sums = jnp.einsum("htk,thd->hkd", one_hot, key_unit, preferred_element_type=jnp.float32)
    totals = lax.psum_scatter(
        local_sums.astype(jnp.bfloat16), SEQ, scatter_dimension=1, tiled=True
    ).astype(jnp.float32)
    new_centroids = EMA_DECAY * centroids + (1.0 - EMA_DECAY) * totals
    returned = returned_back.reshape(heads_here, slot_total, head_width)
    attended = returned[head_grid, flat_slot].reshape(tok_rows, heads_here * head_width)
    attn_part = jnp.dot(attended, w_out, preferred_element_type=jnp.float32)
    hidden = jax.nn.relu(jnp.dot(normed, w_up, preferred_element_type=jnp.float32)).astype(
        jnp.bfloat16
    )
    ffn_part = jnp.dot(hidden, w_down, preferred_element_type=jnp.float32)
    summed = lax.psum_scatter(
        rounded(attn_part + ffn_part).astype(jnp.bfloat16),
        TENSOR,
        scatter_dimension=0,
        tiled=True,
    ).astype(jnp.float32)
    own_rows = lax.dynamic_slice_in_dim(tokens_wide, row_first, share_rows, 0)
    mixed_rows = (own_rows + summed).astype(jnp.bfloat16)
    return (mixed_rows, new_centroids)


def solution(mesh):
    in_specs = (
        P(SEQ, None),
        P(),
        P(None, TENSOR),
        P(None, TENSOR),
        P(TENSOR, None),
        P(None, TENSOR),
        P(TENSOR, None),
        P(TENSOR, SEQ, None),
        P(TENSOR, SEQ),
        P(TENSOR, SEQ),
    )
    out_specs = (P((SEQ, TENSOR), None), P(TENSOR, SEQ, None))
    sizes = dict(mesh.shape)

    def local(*args):
        heads = args[8].shape[0]
        fits = (
            sizes[TENSOR] == 4
            and sizes[SEQ] == 2 * heads
            and heads & (heads - 1) == 0
            and heads == 4
        )
        if not fits:
            return by_clusters(*args)
        return by_heads(*args)

    return jax.shard_map(
        local, mesh=mesh, in_specs=in_specs, out_specs=out_specs, check_vma=False
    )
```
